256 devices in a mesh: dp: 16 (over y_lo, z), fsdp: 16 (over x, y_hi, core).
Axes of the slice: x: 4, y: 4 (y_hi: 2, y_lo: 2; y = y_hi * 2 + y_lo), z: 8, core: 2. Of those that a mesh axis runs over, the one named last changes fastest.
Arguments:
- frames: bfloat16 [256, 256, 1536], P(('dp', 'fsdp')), may hold values from -6 to 6
- cotangent: bfloat16 [256, 256, 1536], P(('dp', 'fsdp')), may hold values from -6 to 6
- lengths: int32 [256], P(('dp', 'fsdp')), may hold values from 64 to 256, as said below
- weight_slots: bfloat16 [2304, 3072], P('fsdp'), may hold values from -0.15625 to 0.15625
- owner_rows: int32 [2304], replicated, may hold values from -1 to 1535, as said below
- gain_in: float32 [1536], replicated, may hold values from 0.5 to 1.5
- gain_mid: float32 [1536], replicated, may hold values from 0.5 to 1.5
- kernel: float32 [32, 1536], replicated, may hold values from -1 to 1
Outputs:
- frame_grads: bfloat16 [256, 256, 1536], P(('dp', 'fsdp'))
- weight_grads: bfloat16 [2304, 3072], P('fsdp')
- gain_in_grad: float32 [1536], replicated
- gain_mid_grad: float32 [1536], replicated
- kernel_grad: float32 [32, 1536], replicated
The draws below stay inside these ranges and needn't reach their ends.
Inputs may be any that keep to these rules, and one draw needn't show every extreme that they name: `owner_rows`: slots o * 144 to o * 144 + 143 belong to owner o (index o of fsdp): first the rows it holds, then -1. Each of the 1536 rows is named by exactly one slot. An owner holds between 48 and 144 rows, and some owner holds exactly 144. Rows of weight_slots in slots marked -1 are not used. `lengths`: some utterance has all 256 frames in use.
All inputs are finite; a program needn't handle non-finite values.
Results may differ from the reference program's by a relative error of at most 0.02.
Values may be sent and summed in bfloat16 or wider, within the bound.
A program may use at most 192 MiB of HBM per device.

```python
import jax
import jax.numpy as jnp
from jax import lax

D = 1536
K = 32
LEN = 256
UTT_DEV = 1
SHARE = 96
CAP = 144
BATCH = 256
N_FSDP = 16


def draw_lengths(key, part):
    drawn = jax.random.randint(key, (BATCH,), LEN // 4, LEN + 1)
    longest = jax.random.randint(jax.random.fold_in(key, 1), (), 0, BATCH)
    shortest = (longest + 1 + jax.random.randint(jax.random.fold_in(key, 2), (), 0, BATCH - 1)) % BATCH
    position = jnp.arange(BATCH)
    drawn = jnp.where(position == longest, LEN, drawn)
    drawn = jnp.where(position == shortest, LEN // 4, drawn)
    return drawn.astype(jnp.int32)


def draw_owner_rows(key, part):
    owners = N_FSDP
    pair_count = owners // 2
    owner_order = jax.random.permutation(jax.random.fold_in(key, 11), owners)
    swing_rows = jax.random.randint(jax.random.fold_in(key, 12), (pair_count,), 0, SHARE // 2 + 1)
    widest_pair = jax.random.randint(jax.random.fold_in(key, 13), (), 0, pair_count)
    swing_rows = jnp.where(jnp.arange(pair_count) == widest_pair, SHARE // 2, swing_rows)
    flip_sign = jax.random.randint(jax.random.fold_in(key, 14), (pair_count,), 0, 2)
    first_size = SHARE + swing_rows * (2 * flip_sign - 1)
    second_size = 2 * SHARE - first_size
    paired = jnp.stack([first_size, second_size], axis=1).reshape(owners).astype(jnp.int32)
    owner_sizes = jnp.zeros((owners,), jnp.int32).at[owner_order].set(paired)
    owner_start = jnp.cumsum(owner_sizes) - owner_sizes
    shuffled = jax.random.permutation(jax.random.fold_in(key, 15), D).astype(jnp.int32)
    slot_index = jnp.arange(owners * CAP)
    owner_of_slot = slot_index // CAP
    slot_within = slot_index % CAP
    position = jnp.clip(owner_start[owner_of_slot] + slot_within, 0, D - 1)
    return jnp.where(slot_within < owner_sizes[owner_of_slot], shuffled[position], -1).astype(jnp.int32)


def shard_levels(stream_key, shape, shards, low, high):
    loudness, own = 1.0, jax.random.fold_in(stream_key, 6)
    for dim, shards_of in shards:
        steps = jnp.exp(jax.random.uniform(jax.random.fold_in(own, dim), (shards_of,), jnp.float32, low / len(shards), high / len(shards)))
        loudness = loudness * jnp.repeat(steps, shape[dim] // shards_of).reshape([-1 if axis == dim else 1 for axis in range(len(shape))])
    return loudness


def scatter_about(key, extent, width, bound, pieces=(), held_as=jnp.bfloat16):
    entries = width * jax.random.normal(key, extent, jnp.float32)
    if pieces:
        entries = entries * shard_levels(key, extent, pieces, -0.22, 0.18)
    return jnp.clip(entries, -bound, bound).astype(held_as)


def setup_inputs(seed: int = 0) -> dict:
    seeds = jax.random.split(jax.random.key(seed), 9)
    return {
        "frames": scatter_about(seeds[0], (BATCH, LEN, D), 1.0, 6.0, ((0, 256),)),
        "cotangent": scatter_about(seeds[1], (BATCH, LEN, D), 1.0, 6.0, ((0, 256),)),
        "lengths": draw_lengths(jax.random.fold_in(seeds[8], 71), 0),
        "weight_slots": scatter_about(seeds[3], (N_FSDP * CAP, 2 * D), D ** -0.5, 0.15625, ((0, 16),)),
        "owner_rows": draw_owner_rows(jax.random.fold_in(seeds[8], 71), 0),
        "gain_in": jnp.clip(1.0 + 0.1 * jax.random.normal(seeds[5], (D,), jnp.float32), 0.5, 1.5),
        "gain_mid": jnp.clip(1.0 + 0.1 * jax.random.normal(seeds[6], (D,), jnp.float32), 0.5, 1.5),
        "kernel": scatter_about(seeds[7], (K, D), K ** -0.5, 1.0, (), jnp.float32),
    }


EPSILON = 1e-05

def norm_rows(values, scales):
    row_mean = lax.optimization_barrier(jnp.mean(values, axis=-1, keepdims=True))
    centred = values - row_mean
    spread = lax.optimization_barrier(jnp.mean(centred * centred, axis=-1, keepdims=True))
    return centred * lax.rsqrt(spread + EPSILON) * scales

def branch_tail(projected, gain_mid, kernel, frame_keep):
    features = gain_mid.shape[0]
    kernel_taps = kernel.shape[0]
    gated = projected[..., :features] * jax.nn.sigmoid(projected[..., features:]) * frame_keep[..., None]
    length = gated.shape[1]
    left_pad = kernel_taps // 2
    padded = jnp.pad(gated, ((0, 0), (left_pad, kernel_taps - 1 - left_pad), (0, 0)))
    convolved = jnp.zeros_like(gated)
    for offset in range(kernel_taps):
        convolved = convolved + kernel[offset] * padded[:, offset:offset + length, :]
    mixed = norm_rows(convolved, gain_mid)
    return mixed * jax.nn.sigmoid(mixed) * frame_keep[..., None]

def device_pass(frames, cotangent, lengths, weight, gain_in, gain_mid, kernel):
    utterances, length, features = frames.shape
    frame_keep = (jnp.arange(length)[None, :] < lengths[:, None]).astype(jnp.float32)
    frames_wide = frames.astype(jnp.float32)
    normed, head_back = jax.vjp(norm_rows, frames_wide, gain_in)
    normed_flat = normed.astype(jnp.bfloat16).reshape(utterances * length, features)
    projected = jnp.dot(normed_flat, weight, preferred_element_type=jnp.float32)
    projected = projected.reshape(utterances, length, 2 * features)
    cotangent_wide = cotangent.astype(jnp.float32)

    def run_tail(projected_in, mid_scales, taps_in):
        return branch_tail(projected_in, mid_scales, taps_in, frame_keep)
    branch, tail_back = jax.vjp(run_tail, projected, gain_mid, kernel)
    projected_grad, gain_mid_grad, kernel_grad = tail_back(cotangent_wide)
    grad_flat = projected_grad.astype(jnp.bfloat16).reshape(utterances * length, 2 * features)
    normed_grad = lax.dot_general(grad_flat, weight, (((1,), (1,)), ((), ())), preferred_element_type=jnp.float32)
    frames_back, gain_in_grad = head_back(normed_grad.reshape(utterances, length, features))
    frame_grads = (cotangent_wide + frames_back).astype(jnp.bfloat16)
    weight_term = lax.dot_general(normed_flat, grad_flat, (((0,), (0,)), ((), ())), preferred_element_type=jnp.float32)
    return (frame_grads, weight_term, gain_in_grad, gain_mid_grad, kernel_grad)

def reference(frames, cotangent, lengths, weight_slots, owner_rows, gain_in, gain_mid, kernel):
    features = frames.shape[2]
    slot_count = owner_rows.shape[0]
    valid_slot = owner_rows >= 0
    inverse = jnp.zeros((features,), jnp.int32).at[jnp.where(valid_slot, owner_rows, features)].set(jnp.arange(slot_count, dtype=jnp.int32), mode='drop')
    weight = jnp.take(weight_slots, inverse, axis=0)
    groups = frames.shape[0] // UTT_DEV
    frames_grouped = frames.reshape(groups, UTT_DEV, LEN, features)
    cotangent_grouped = cotangent.reshape(groups, UTT_DEV, LEN, features)
    lengths_grouped = lengths.reshape(groups, UTT_DEV)

    def one_device(carry, inputs):
        frame_part, cotangent_part, length_part = inputs
        frame_grads, weight_term, gain_in_grad, gain_mid_grad, kernel_grad = device_pass(frame_part, cotangent_part, length_part, weight, gain_in, gain_mid, kernel)
        rounded = lax.optimization_barrier(weight_term.astype(jnp.bfloat16)).astype(jnp.float32)
        carry = (carry[0] + rounded, carry[1] + gain_in_grad, carry[2] + gain_mid_grad, carry[3] + kernel_grad)
        return (carry, frame_grads)
    start_carry = (jnp.zeros((features, 2 * features), jnp.float32), jnp.zeros((features,), jnp.float32), jnp.zeros((features,), jnp.float32), jnp.zeros(kernel.shape, jnp.float32))
    totals, frame_grads = lax.scan(one_device, start_carry, (frames_grouped, cotangent_grouped, lengths_grouped))
    safe_rows = jnp.where(valid_slot, owner_rows, 0)
    weight_grads = (jnp.take(totals[0], safe_rows, axis=0) * valid_slot.astype(jnp.float32)[:, None]).astype(jnp.bfloat16)
    return (frame_grads.reshape(frames.shape), weight_grads, totals[1], totals[2], totals[3])
```

```python
import functools
import jax
import jax.numpy as jnp
from jax import lax
from jax.experimental import pallas as pl
from jax.experimental.pallas import tpu as pltpu
from jax.sharding import PartitionSpec as P

MESH = pl.DeviceIdType.MESH
NX, NY, NZ = 4, 4, 8
PIECES = 3


def place():
    d = lax.axis_index("dp")
    f = lax.axis_index("fsdp")
    return f // 4, (f // 2) % 2, d // NZ, d % NZ, f % 2


def device(x, yh, yl, z, c):
    return (yl * NZ + z, (x * 2 + yh) * 2 + c)


def enter(peers):
    barrier = pltpu.get_barrier_semaphore()
    for peer in peers:
        pl.semaphore_signal(barrier, inc=1, device_id=peer, device_id_type=MESH)
    pl.semaphore_wait(barrier, len(peers))


def gather_kernel(w_ref, o_ref, local_sem, send, recv):
    x, yh, yl, z, c = place()
    xs = [x, (x + 3) % NX, (x + 1) % NX, (x + 2) % NX]
    zp, zm = (z + 1) % NZ, (z + 7) % NZ
    sib = device(x, yh, yl, z, 1 - c)
    to_xp, to_xm = device(xs[2], yh, yl, z, c), device(xs[1], yh, yl, z, c)
    to_ac = device(x, 1 - yh, 1 - yl, z, c)
    to_ys = device(x, yh, 1 - yl, z, c)
    to_zp, to_zm = device(x, yh, yl, zp, c), device(x, yh, yl, zm, c)
    third = w_ref.shape[1] // 3
    rows = w_ref.shape[0] // PIECES
    par = z % 2
    base = par * third

    def cols(start, size):
        return pl.ds(pl.multiple_of(start, third // 2), size)

    window = cols(base, 2 * third)
    halves = [cols(base, third), cols(base + third, third)]
    mine = cols(base + yl * third, third)
    other = cols(base + (1 - yl) * third, third)
    shared = [cols(base + par * third, third // 2), cols(base + par * third + third // 2, third // 2)]
    theirs = [cols((1 - par) * 2 * third, third // 2), cols((1 - par) * 2 * third + third // 2, third // 2)]

    def owner(k, other_row):
        return (xs[k] * 2 + (1 - yh if other_row else yh)) * 2 + c

    pending = []

    def push(index, q, src, dst, to):
        copy = pltpu.make_async_remote_copy(
            src_ref=src, dst_ref=dst, send_sem=send.at[index, q], recv_sem=recv.at[index, q],
            device_id=to, device_id_type=MESH,
        )
        copy.start()
        pending.append(copy)

    def piece(ref, q, span):
        return ref.at[pl.ds(q * rows, rows), span]

    def pass_on(index, q, who, span, to):
        ref = piece(o_ref.at[who], q, span)
        push(index, q, ref, ref, to)

    def arrive(index, q, who, span):
        ref = piece(o_ref.at[who], q, span)
        pltpu.make_async_remote_copy(
            src_ref=ref, dst_ref=ref, send_sem=send.at[index, q], recv_sem=recv.at[index, q],
            device_id=sib, device_id_type=MESH,
        ).wait_recv()

    enter([sib, to_xp, to_xm, to_ac, to_ys, to_zp, to_zm])
    me = owner(0, False)
    for q in range(PIECES):
        push(1, q, piece(w_ref, q, window), piece(o_ref.at[me], q, window), to_xp)
        push(2, q, piece(w_ref, q, window), piece(o_ref.at[me], q, window), to_xm)
        push(3, q, piece(w_ref, q, mine), piece(o_ref.at[me], q, mine), to_ac)
    keep = pltpu.make_async_copy(w_ref, o_ref.at[me], local_sem)
    keep.start()
    push(0, 0, w_ref, o_ref.at[me], sib)

    def z_out(slot, q, who):
        pass_on(13 + slot, q, who, shared[0], to_zp)
        pass_on(20 + slot, q, who, shared[1], to_zm)

    units = [(1, False), (2, False), (3, False), (0, True), (1, True), (2, True), (3, True)]

    def x_near(k, q):
        arrive(k, q, owner(k, False), window)
        pass_on(6 + k, q, owner(k, False), halves[k - 1], (to_xp, to_xm)[k - 1])
        pass_on(3 + k, q, owner(k, False), mine, to_ac)
        z_out(k - 1, q, owner(k, False))
        pass_on(26 + k, q, owner(k, False), window, sib)

    def x_far(q):
        arrive(7, q, owner(3, False), halves[0])
        arrive(8, q, owner(3, False), halves[1])
        pass_on(6, q, owner(3, False), mine, to_ac)
        z_out(2, q, owner(3, False))
        pass_on(29, q, owner(3, False), halves[0], sib)
        pass_on(30, q, owner(3, False), halves[1], sib)

    def across(k, q):
        arrive(3 + k, q, owner(k, True), other)
        pass_on(9 + k, q, owner(k, True), other, to_ys)
        pass_on(31 + k, q, owner(k, True), other, sib)

    def beside(k, q):
        arrive(9 + k, q, owner(k, True), mine)
        z_out(3 + k, q, owner(k, True))
        pass_on(35 + k, q, owner(k, True), mine, sib)

    def z_in(slot, q):
        who = owner(*units[slot])
        arrive(13 + slot, q, who, theirs[0])
        pass_on(39 + slot, q, who, theirs[0], sib)
        arrive(20 + slot, q, who, theirs[1])
        pass_on(46 + slot, q, who, theirs[1], sib)

    last = PIECES - 1
    for q in range(PIECES):
        across(0, q)
        x_near(1, q)
        x_near(2, q)
        beside(0, q)
        if q > 0:
            across(1, q - 1)
            across(2, q - 1)
    x_far(0)
    across(1, last)
    across(2, last)
    for q in range(PIECES):
        beside(1, q)
        beside(2, q)
        if q < last:
            x_far(q + 1)
        across(3, q)
        z_in(0, q)
        z_in(1, q)
        z_in(3, q)
    for q in range(PIECES):
        beside(3, q)
        z_in(2, q)
        z_in(4, q)
        z_in(5, q)
    for q in range(PIECES):
        z_in(6, q)

    def flip(who):
        return who + 1 - 2 * c

    full = o_ref.at[flip(me)]
    pltpu.make_async_remote_copy(
        src_ref=full, dst_ref=full, send_sem=send.at[0, 0], recv_sem=recv.at[0, 0],
        device_id=sib, device_id_type=MESH,
    ).wait_recv()
    for q in range(PIECES):
        arrive(27, q, flip(owner(1, False)), window)
        arrive(28, q, flip(owner(2, False)), window)
        arrive(29, q, flip(owner(3, False)), halves[0])
        arrive(30, q, flip(owner(3, False)), halves[1])
        for k in range(4):
            arrive(31 + k, q, flip(owner(k, True)), other)
            arrive(35 + k, q, flip(owner(k, True)), mine)
        for slot in range(7):
            arrive(39 + slot, q, flip(owner(*units[slot])), theirs[0])
            arrive(46 + slot, q, flip(owner(*units[slot])), theirs[1])
    keep.wait()
    for copy in pending:
        copy.wait_send()


def gather_rows(w, owners):
    cap, width = w.shape
    return pl.pallas_call(
        gather_kernel,
        out_shape=jax.ShapeDtypeStruct((owners, cap, width), w.dtype),
        in_specs=[pl.BlockSpec(memory_space=pl.ANY)],
        out_specs=pl.BlockSpec(memory_space=pl.ANY),
        scratch_shapes=[
            pltpu.SemaphoreType.DMA,
            pltpu.SemaphoreType.DMA((53, PIECES)),
            pltpu.SemaphoreType.DMA((53, PIECES)),
        ],
        compiler_params=pltpu.CompilerParams(collective_id=0, has_side_effects=True),
        name="gather_rows",
    )(w)


PARTS = 3
BLOCK = 72
LANES = 128
PART_AXES = ("xyz", "yzx", "zxy")


def wide(value):
    return value.astype(jnp.float32)


def split_index(i, lead):
    index = []
    for size in reversed(lead):
        index.append(i % size)
        i = i // size
    return tuple(reversed(index))


def add_into(dst, sources, lead):
    total = 1
    for size in lead:
        total *= size

    def one(i, carry):
        index = split_index(i, lead)
        value = wide(dst[index])
        for src in sources:
            value = value + wide(src[index])
        dst[index] = value.astype(dst.dtype)
        return carry

    if total == 1:
        one(0, 0)
    else:
        lax.fori_loop(0, total, one, 0)


def scatter_kernel(
    mine_t, grad, small, out, small_out,
    theirs_t, grad_both, sums, near_x, near_y, near_z, mid_x, mid_y, mid_z, far_x, far_y, far_z,
    small_sum, small_sib, small_z, small_x, small_y, finals, other_finals,
    sib_send, sib_recv, send, recv, small_send, small_recv, out_send, out_recv,
):
    x, yh, yl, z, c = place()
    y = yh * 2 + yl
    tokens, width = grad.shape
    half = width // 2
    part_cols = half // PARTS

    def at_x(i):
        return device(i % NX, yh, yl, z, c)

    def at_y(i):
        return device(x, (i % NY) // 2, i % 2, z, c)

    def at_z(i):
        return device(x, yh, yl, i % NZ, c)

    sib = device(x, yh, yl, z, 1 - c)
    pending = []

    def push(src, dst, send_sem, recv_sem, to):
        copy = pltpu.make_async_remote_copy(
            src_ref=src, dst_ref=dst, send_sem=send_sem, recv_sem=recv_sem,
            device_id=to, device_id_type=MESH,
        )
        copy.start()
        pending.append(copy)
        return copy

    def landed(ref, send_sem, recv_sem):
        pltpu.make_async_remote_copy(
            src_ref=ref, dst_ref=ref, send_sem=send_sem, recv_sem=recv_sem,
            device_id=sib, device_id_type=MESH,
        ).wait_recv()

    enter(
        [sib]
        + [at_x(x + i) for i in range(1, NX)]
        + [at_y(y + i) for i in range(1, NY)]
        + [at_z(z + i) for i in range(1, NZ)]
    )

    def half_cols(index):
        return pl.ds(pl.multiple_of(index * half, half), half)

    swap_t = push(mine_t, theirs_t, sib_send.at[0], sib_recv.at[0], sib)
    swap_g = push(grad.at[:, half_cols(1 - c)], grad_both.at[1], sib_send.at[1], sib_recv.at[1], sib)
    swap_s = push(small.at[:, 1 - c], small_sib, sib_send.at[2], sib_recv.at[2], sib)
    grad_both[0] = grad[:, half_cols(c)]
    swap_s.wait_recv()
    small_sum[...] = small[:, c] + small_sib[...]
    swap_g.wait_recv()
    swap_t.wait_recv()

    owner_rows = mine_t.shape[0] // (NX * 2)

    def make_terms(p):
        span = pl.ds(p * part_cols, part_cols)

        def one(o, carry):
            rows = pl.ds(pl.multiple_of(o * owner_rows, 32), owner_rows)
            term = jnp.dot(mine_t[rows, :], grad_both[0, :, span], preferred_element_type=jnp.float32)
            term = term + jnp.dot(theirs_t[rows, :], grad_both[1, :, span], preferred_element_type=jnp.float32)
            ox, oy = o // 2, o % 2
            for q in range(4):
                for t in range(4):
                    sums[p, ox, oy * 2 + t // 2, (t % 2) * 4 + q] = term[
                        q * BLOCK : (q + 1) * BLOCK, t * LANES : (t + 1) * LANES
                    ].astype(sums.dtype)
            return carry

        lax.fori_loop(0, NX * 2, one, 0)

    place_of = {"x": (x, NX, at_x), "y": (y, NY, at_y), "z": (z, NZ, at_z)}
    near = (near_x, near_y, near_z)
    middle = (mid_y, mid_z, mid_x)
    last = (far_z, far_x, far_y)

    def part_flow(p):
        left = ["x", "y", "z"]
        fixed = {}
        for stage, axis in enumerate(PART_AXES[p]):
            me, n, dev = place_of[axis]
            rest = [a for a in left if a != axis]
            lead = tuple(place_of[a][1] for a in rest)
            buffers = (near, middle, last)[stage][p]

            def chunk(i, part=None):
                index = []
                for a in ("x", "y", "z"):
                    if a in fixed:
                        index.append(fixed[a])
                    elif a == axis:
                        index.append(i % n)
                    elif part is not None and a == rest[0]:
                        size = place_of[a][1] // 2
                        index.append(pl.ds(part * size, size))
                    else:
                        index.append(slice(None))
                return sums.at[(p,) + tuple(index)]

            def landing(step, way, part=None):
                ref = buffers.at[step, way]
                if part is not None:
                    size = lead[0] // 2
                    ref = ref.at[pl.ds(part * size, size)]
                return ref

            steps = n // 2
            for step in range(steps):
                k = steps - step
                split = step == 0 and bool(rest)
                half_lead = (lead[0] // 2,) + lead[1:] if split else lead
                parts = (0, 1) if split else (None, None)
                ways = (0, 1) if (step > 0 or split) else (0,)
                sems = [(send.at[p, stage, step, w], recv.at[p, stage, step, w]) for w in (0, 1)]
                for w in ways:
                    sign = 1 if w == 0 else -1
                    push(chunk(me + n + sign * k, parts[w]), landing(step, w, parts[w]), *sems[w], dev(me + n + sign))
                yield
                for w in ways:
                    landed(landing(step, w, parts[w]), *sems[w])
                if step < steps - 1:
                    for w in ways:
                        sign = 1 if w == 0 else -1
                        add_into(chunk(me + n + sign * (k - 1), parts[w]), [landing(step, w, parts[w])], half_lead)
                else:
                    add_into(chunk(me), [landing(step, 0), landing(step, 1)], lead)
            fixed[axis] = me
            left.remove(axis)

    def small_flow():
        def spread(source, slots, me, n, dev, base):
            for i in range(1, n):
                push(
                    source((me + i) % n), slots.at[me],
                    small_send.at[base + i], small_recv.at[base + i], dev(me + i),
                )

        def collect(slots, me, n, base):
            for i in range(1, n):
                landed(slots.at[(me + n - i) % n], small_send.at[base + i], small_recv.at[base + i])

        small_z[z] = small_sum[z]
        spread(lambda i: small_sum.at[i], small_z, z, NZ, at_z, 0)
        yield
        collect(small_z, z, NZ, 0)
        total = small_z[0]
        for i in range(1, NZ):
            total = total + small_z[i]
        small_x[x] = total
        spread(lambda i: small_x.at[x], small_x, x, NX, at_x, 8)
        yield
        collect(small_x, x, NX, 8)
        total = small_x[0]
        for i in range(1, NX):
            total = total + small_x[i]
        small_y[y] = total
        spread(lambda i: small_y.at[y], small_y, y, NY, at_y, 12)
        yield
        collect(small_y, y, NY, 12)
        total = small_y[0]
        for i in range(1, NY):
            total = total + small_y[i]
        small_out[c, z] = total
        spread(lambda i: small_out.at[c, z], small_out.at[c], z, NZ, at_z, 16)
        yield
        collect(small_out.at[c], z, NZ, 16)
        push(small_out.at[c], small_out.at[c], small_send.at[0], small_recv.at[0], sib)
        yield
        landed(small_out.at[1 - c], small_send.at[0], small_recv.at[0])

    flows = [part_flow(p) for p in range(PARTS)] + [small_flow()]

    def resume(i):
        try:
            next(flows[i])
        except StopIteration:
            pass

    make_terms(2)
    resume(2)
    make_terms(1)
    resume(1)
    make_terms(0)
    resume(0)
    resume(3)
    for i in (2, 1, 0, 2, 2, 3, 1, 0, 3, 2):
        resume(i)
    for _ in range(4):
        for i in (1, 0, 2):
            resume(i)
    resume(3)
    for _ in range(3):
        for i in (1, 0, 2):
            resume(i)
    resume(3)
    resume(3)

    def final(layer, k):
        return finals.at[layer, k % NZ]

    for p in range(PARTS):
        finals[yl, z, p] = sums[p, x, y, z]
    to_ys = device(x, yh, 1 - yl, z, c)
    push(final(yl, z), final(yl, z), out_send.at[0, 0, 0], out_recv.at[0, 0, 0], to_ys)
    for layer_is_mine in (True,):
        push(final(yl, z), final(yl, z), out_send.at[1, 0, 0], out_recv.at[1, 0, 0], at_z(z + 1))
        push(final(yl, z), final(yl, z), out_send.at[1, 0, 1], out_recv.at[1, 0, 1], at_z(z + NZ - 1))
    landed(final(1 - yl, z), out_send.at[0, 0, 0], out_recv.at[0, 0, 0])
    push(final(1 - yl, z), final(1 - yl, z), out_send.at[1, 1, 0], out_recv.at[1, 1, 0], at_z(z + 1))
    push(final(1 - yl, z), final(1 - yl, z), out_send.at[1, 1, 1], out_recv.at[1, 1, 1], at_z(z + NZ - 1))

    def to_sibling(layer, k, index):
        @pl.when((k % 4) // 2 != c)
        def _():
            pltpu.make_async_remote_copy(
                src_ref=final(layer, k), dst_ref=other_finals.at[layer, k % NZ],
                send_sem=sib_send.at[4 + index], recv_sem=sib_recv.at[4 + index],
                device_id=sib, device_id_type=MESH,
            ).start()

    def sibling_done(layer, k, index):
        @pl.when((k % 4) // 2 != c)
        def _():
            pltpu.make_async_remote_copy(
                src_ref=final(layer, k), dst_ref=other_finals.at[layer, k % NZ],
                send_sem=sib_send.at[4 + index], recv_sem=sib_recv.at[4 + index],
                device_id=sib, device_id_type=MESH,
            ).wait_send()

        @pl.when((k % 4) // 2 == c)
        def _():
            landed(other_finals.at[layer, k % NZ], sib_send.at[4 + index], sib_recv.at[4 + index])

    layers = (yl, 1 - yl)
    for j in (0, 1):
        to_sibling(layers[j], z, j * NZ)
    for s in (1, 2, 3, 4):
        for j in (0, 1):
            for w in (0, 1):
                if s == 4 and w != j:
                    continue
                k = z + NZ - s if w == 0 else z + s
                landed(final(layers[j], k), out_send.at[s, j, w], out_recv.at[s, j, w])
                onward = s < 3 or (s == 3 and w == j)
                if onward:
                    push(
                        final(layers[j], k), final(layers[j], k),
                        out_send.at[s + 1, j, w], out_recv.at[s + 1, j, w],
                        at_z(z + 1) if w == 0 else at_z(z + NZ - 1),
                    )
                to_sibling(layers[j], k % NZ, j * NZ + (NZ - s if w == 0 else s))
    for j in (0, 1):
        for k in range(NZ):
            sibling_done(layers[j], (z + k) % NZ, j * NZ + k)

    for layer in (0, 1):
        for zh in (0, 1):
            for p in range(PARTS):
                column = p * part_cols + (layer * 2 + zh) * LANES
                for source, which in ((finals, c), (other_finals, 1 - c)):
                    block = jnp.concatenate(
                        [wide(source[layer, zh * 4 + 2 * c + r, p]) for r in (0, 1)], axis=0
                    )
                    start = pl.multiple_of(which * half + column, LANES)
                    out[:, pl.ds(start, LANES)] = block.astype(out.dtype)
    for copy in pending:
        copy.wait_send()


def scatter_rows(mine_t, grad, small, cap):
    slots, tokens = mine_t.shape
    width = grad.shape[1]
    bf, f32 = jnp.bfloat16, jnp.float32
    block = (BLOCK, LANES)
    vmem = pl.BlockSpec(memory_space=pltpu.VMEM)
    return pl.pallas_call(
        scatter_kernel,
        out_shape=(
            jax.ShapeDtypeStruct((cap, width), bf),
            jax.ShapeDtypeStruct((2, NZ) + small.shape[2:], f32),
        ),
        in_specs=[vmem] * 3,
        out_specs=(vmem, vmem),
        scratch_shapes=[
            pltpu.VMEM((slots, tokens), bf),
            pltpu.VMEM((2, tokens, width // 2), bf),
            pltpu.VMEM((PARTS, NX, NY, NZ) + block, bf),
            pltpu.VMEM((2, 2, NY, NZ) + block, bf),
            pltpu.VMEM((2, 2, NX, NZ) + block, bf),
            pltpu.VMEM((4, 2, NX, NY) + block, bf),
            pltpu.VMEM((2, 2, NY) + block, bf),
            pltpu.VMEM((2, 2, NZ) + block, bf),
            pltpu.VMEM((4, 2, NX) + block, bf),
            pltpu.VMEM((2, 2) + block, bf),
            pltpu.VMEM((2, 2) + block, bf),
            pltpu.VMEM((4, 2) + block, bf),
            pltpu.VMEM((NZ,) + small.shape[2:], f32),
            pltpu.VMEM((NZ,) + small.shape[2:], f32),
            pltpu.VMEM((NZ,) + small.shape[2:], f32),
            pltpu.VMEM((NX,) + small.shape[2:], f32),
            pltpu.VMEM((NY,) + small.shape[2:], f32),
            pltpu.VMEM((2, NZ, PARTS) + block, bf),
            pltpu.VMEM((2, NZ, PARTS) + block, bf),
            pltpu.SemaphoreType.DMA((20,)),
            pltpu.SemaphoreType.DMA((20,)),
            pltpu.SemaphoreType.DMA((PARTS, 3, 4, 2)),
            pltpu.SemaphoreType.DMA((PARTS, 3, 4, 2)),
            pltpu.SemaphoreType.DMA((24,)),
            pltpu.SemaphoreType.DMA((24,)),
            pltpu.SemaphoreType.DMA((5, 2, 2)),
            pltpu.SemaphoreType.DMA((5, 2, 2)),
        ],
        compiler_params=pltpu.CompilerParams(
            collective_id=1, has_side_effects=True, vmem_limit_bytes=48 << 20
        ),
        name="scatter_rows",
    )(mine_t, grad, small)


EPSILON = 1e-05


def norm_rows(values, scales):
    row_mean = jnp.mean(values, axis=-1, keepdims=True)
    centred = values - row_mean
    spread = jnp.mean(centred * centred, axis=-1, keepdims=True)
    return centred * lax.rsqrt(spread + EPSILON) * scales


def branch_tail(projected, gain_mid, kernel, frame_keep):
    features = gain_mid.shape[0]
    kernel_taps = kernel.shape[0]
    gated = (
        projected[..., :features]
        * jax.nn.sigmoid(projected[..., features:])
        * frame_keep[..., None]
    )
    length = gated.shape[1]
    left_pad = kernel_taps // 2
    padded = jnp.pad(gated, ((0, 0), (left_pad, kernel_taps - 1 - left_pad), (0, 0)))
    convolved = jnp.zeros_like(gated)
    for offset in range(kernel_taps):
        convolved = convolved + kernel[offset] * padded[:, offset : offset + length, :]
    mixed = norm_rows(convolved, gain_mid)
    return mixed * jax.nn.sigmoid(mixed) * frame_keep[..., None]


def per_device(frames, cotangent, lengths, weight_slots, owner_rows, gain_in, gain_mid, kernel):
    utterances, length, features = frames.shape
    token_rows = utterances * length
    slots = owner_rows.shape[0]
    cap = weight_slots.shape[0]
    taps = kernel.shape[0]
    frame_keep = (jnp.arange(length)[None, :] < lengths[:, None]).astype(jnp.float32)
    frames_wide = frames.astype(jnp.float32)
    normed, head_back = jax.vjp(norm_rows, frames_wide, gain_in)
    normed_flat = normed.astype(jnp.bfloat16).reshape(token_rows, features)
    gathered = gather_rows(weight_slots, slots // cap).reshape(slots, 2 * features)
    chosen = (jnp.arange(features, dtype=jnp.int32)[:, None] == owner_rows[None, :]).astype(jnp.bfloat16)
    in_slots = jnp.dot(normed_flat, chosen)
    in_slots_t = lax.dot_general(chosen, normed_flat, (((0,), (1,)), ((), ())))
    projected = jnp.dot(in_slots, gathered, preferred_element_type=jnp.float32)
    projected = projected.reshape(utterances, length, 2 * features)
    cotangent_wide = cotangent.astype(jnp.float32)

    def run_tail(projected_in, mid_scales, taps_in):
        return branch_tail(projected_in, mid_scales, taps_in, frame_keep)

    branch, tail_back = jax.vjp(run_tail, projected, gain_mid, kernel)
    projected_grad, gain_mid_grad, kernel_grad = tail_back(cotangent_wide)
    grad_flat = projected_grad.astype(jnp.bfloat16).reshape(token_rows, 2 * features)
    slot_grad = lax.dot_general(
        grad_flat, gathered, (((1,), (1,)), ((), ())), preferred_element_type=jnp.float32
    ).astype(jnp.bfloat16)
    normed_grad = lax.dot_general(
        slot_grad, chosen, (((1,), (1,)), ((), ())), preferred_element_type=jnp.float32
    )
    frames_back, gain_in_grad = head_back(normed_grad.reshape(utterances, length, features))
    frame_grads = (cotangent_wide + frames_back).astype(jnp.bfloat16)
    rows = taps + 2
    small = jnp.concatenate([gain_in_grad[None], gain_mid_grad[None], kernel_grad], axis=0)
    small = jnp.pad(small.reshape(-1), (0, 2 * NZ * 32 * LANES - rows * features))
    weight_grads, total = scatter_rows(in_slots_t, grad_flat, small.reshape(NZ, 2, 32, LANES), cap)
    total = total.transpose(1, 0, 2, 3).reshape(-1)[: rows * features].reshape(rows, features)
    return (frame_grads, weight_grads, total[0], total[1], total[2:])


def solution(mesh):
    in_specs = (
        P(("dp", "fsdp"), None, None),
        P(("dp", "fsdp"), None, None),
        P(("dp", "fsdp")),
        P("fsdp", None),
        P(),
        P(),
        P(),
        P(),
    )
    out_specs = (P(("dp", "fsdp"), None, None), P("fsdp", None), P(), P(), P())
    return jax.shard_map(
        per_device, mesh=mesh, in_specs=in_specs, out_specs=out_specs, check_vma=False
    )
```

```python
import functools
import jax
import jax.numpy as jnp
from jax import lax
from jax.experimental import pallas as pl
from jax.experimental.pallas import tpu as pltpu
from jax.sharding import PartitionSpec as P

MESH = pl.DeviceIdType.MESH
NX, NY, NZ = 4, 4, 8
PIECES = 3


def place():
    d = lax.axis_index("dp")
    f = lax.axis_index("fsdp")
    return f // 4, (f // 2) % 2, d // NZ, d % NZ, f % 2


def device(x, yh, yl, z, c):
    return (yl * NZ + z, (x * 2 + yh) * 2 + c)


def enter(peers):
    barrier = pltpu.get_barrier_semaphore()
    for peer in peers:
        pl.semaphore_signal(barrier, inc=1, device_id=peer, device_id_type=MESH)
    pl.semaphore_wait(barrier, len(peers))


def gather_kernel(w_ref, o_ref, local_sem, send, recv):
    x, yh, yl, z, c = place()
    xs = [x, (x + 3) % NX, (x + 1) % NX, (x + 2) % NX]
    zp, zm = (z + 1) % NZ, (z + 7) % NZ
    sib = device(x, yh, yl, z, 1 - c)
    to_xp, to_xm = device(xs[2], yh, yl, z, c), device(xs[1], yh, yl, z, c)
    to_ac = device(x, 1 - yh, 1 - yl, z, c)
    to_ys = device(x, yh, 1 - yl, z, c)
    to_zp, to_zm = device(x, yh, yl, zp, c), device(x, yh, yl, zm, c)
    third = w_ref.shape[1] // 3
    rows = w_ref.shape[0] // PIECES
    par = z % 2
    base = par * third

    def cols(start, size):
        return pl.ds(pl.multiple_of(start, third // 2), size)

    window = cols(base, 2 * third)
    halves = [cols(base, third), cols(base + third, third)]
    mine = cols(base + yl * third, third)
    other = cols(base + (1 - yl) * third, third)
    shared = [cols(base + par * third, third // 2), cols(base + par * third + third // 2, third // 2)]
    theirs = [cols((1 - par) * 2 * third, third // 2), cols((1 - par) * 2 * third + third // 2, third // 2)]

    def owner(k, other_row):
        return (xs[k] * 2 + (1 - yh if other_row else yh)) * 2 + c

    pending = []

    def push(index, q, src, dst, to):
        copy = pltpu.make_async_remote_copy(
            src_ref=src, dst_ref=dst, send_sem=send.at[index, q], recv_sem=recv.at[index, q],
            device_id=to, device_id_type=MESH,
        )
        copy.start()
        pending.append(copy)

    def piece(ref, q, span):
        return ref.at[pl.ds(q * rows, rows), span]

    def pass_on(index, q, who, span, to):
        ref = piece(o_ref.at[who], q, span)
        push(index, q, ref, ref, to)

    def arrive(index, q, who, span):
        ref = piece(o_ref.at[who], q, span)
        pltpu.make_async_remote_copy(
            src_ref=ref, dst_ref=ref, send_sem=send.at[index, q], recv_sem=recv.at[index, q],
            device_id=sib, device_id_type=MESH,
        ).wait_recv()

    enter([sib, to_xp, to_xm, to_ac, to_ys, to_zp, to_zm])
    me = owner(0, False)
    for q in range(PIECES):
        push(1, q, piece(w_ref, q, window), piece(o_ref.at[me], q, window), to_xp)
        push(2, q, piece(w_ref, q, window), piece(o_ref.at[me], q, window), to_xm)
        push(3, q, piece(w_ref, q, mine), piece(o_ref.at[me], q, mine), to_ac)
    keep = pltpu.make_async_copy(w_ref, o_ref.at[me], local_sem)
    keep.start()
    push(0, 0, w_ref, o_ref.at[me], sib)

    def z_out(slot, q, who):
        pass_on(13 + slot, q, who, shared[0], to_zp)
        pass_on(20 + slot, q, who, shared[1], to_zm)

    units = [(1, False), (2, False), (3, False), (0, True), (1, True), (2, True), (3, True)]

    def x_near(k, q):
        arrive(k, q, owner(k, False), window)
        pass_on(6 + k, q, owner(k, False), halves[k - 1], (to_xp, to_xm)[k - 1])
        pass_on(3 + k, q, owner(k, False), mine, to_ac)
        z_out(k - 1, q, owner(k, False))
        pass_on(26 + k, q, owner(k, False), window, sib)

    def x_far(q):
        arrive(7, q, owner(3, False), halves[0])
        arrive(8, q, owner(3, False), halves[1])
        pass_on(6, q, owner(3, False), mine, to_ac)
        z_out(2, q, owner(3, False))
        pass_on(29, q, owner(3, False), halves[0], sib)
        pass_on(30, q, owner(3, False), halves[1], sib)

    def across(k, q):
        arrive(3 + k, q, owner(k, True), other)
        pass_on(9 + k, q, owner(k, True), other, to_ys)
        pass_on(31 + k, q, owner(k, True), other, sib)

    def beside(k, q):
        arrive(9 + k, q, owner(k, True), mine)
        z_out(3 + k, q, owner(k, True))
        pass_on(35 + k, q, owner(k, True), mine, sib)

    def z_in(slot, q):
        who = owner(*units[slot])
        arrive(13 + slot, q, who, theirs[0])
        pass_on(39 + slot, q, who, theirs[0], sib)
        arrive(20 + slot, q, who, theirs[1])
        pass_on(46 + slot, q, who, theirs[1], sib)

    last = PIECES - 1
    for q in range(PIECES):
        across(0, q)
        x_near(1, q)
        x_near(2, q)
        beside(0, q)
        if q > 0:
            across(1, q - 1)
            across(2, q - 1)
    x_far(0)
    across(1, last)
    across(2, last)
    for q in range(PIECES):
        beside(1, q)
        beside(2, q)
        if q < last:
            x_far(q + 1)
        across(3, q)
        z_in(0, q)
        z_in(1, q)
        z_in(3, q)
    for q in range(PIECES):
        beside(3, q)
        z_in(2, q)
        z_in(4, q)
        z_in(5, q)
    for q in range(PIECES):
        z_in(6, q)

    def flip(who):
        return who + 1 - 2 * c

    full = o_ref.at[flip(me)]
    pltpu.make_async_remote_copy(
        src_ref=full, dst_ref=full, send_sem=send.at[0, 0], recv_sem=recv.at[0, 0],
        device_id=sib, device_id_type=MESH,
    ).wait_recv()
    for q in range(PIECES):
        arrive(27, q, flip(owner(1, False)), window)
        arrive(28, q, flip(owner(2, False)), window)
        arrive(29, q, flip(owner(3, False)), halves[0])
        arrive(30, q, flip(owner(3, False)), halves[1])
        for k in range(4):
            arrive(31 + k, q, flip(owner(k, True)), other)
            arrive(35 + k, q, flip(owner(k, True)), mine)
        for slot in range(7):
            arrive(39 + slot, q, flip(owner(*units[slot])), theirs[0])
            arrive(46 + slot, q, flip(owner(*units[slot])), theirs[1])
    keep.wait()
    for copy in pending:
        copy.wait_send()


def gather_rows(w, owners):
    cap, width = w.shape
    return pl.pallas_call(
        gather_kernel,
        out_shape=jax.ShapeDtypeStruct((owners, cap, width), w.dtype),
        in_specs=[pl.BlockSpec(memory_space=pl.ANY)],
        out_specs=pl.BlockSpec(memory_space=pl.ANY),
        scratch_shapes=[
            pltpu.SemaphoreType.DMA,
            pltpu.SemaphoreType.DMA((53, PIECES)),
            pltpu.SemaphoreType.DMA((53, PIECES)),
        ],
        compiler_params=pltpu.CompilerParams(collective_id=0, has_side_effects=True),
        name="gather_rows",
    )(w)


PARTS = 3
BLOCK = 72
LANES = 128
SMALL = 32
PART_AXES = ("xyz", "yzx", "zxy")


def wide(value):
    return value.astype(jnp.float32)


def split_index(i, lead):
    index = []
    for size in reversed(lead):
        index.append(i % size)
        i = i // size
    return tuple(reversed(index))


def add_into(dst, sources, lead):
    total = 1
    for size in lead:
        total *= size

    def one(i, carry):
        index = split_index(i, lead)
        value = wide(dst[index])
        for src in sources:
            value = value + wide(src[index])
        dst[index] = value.astype(dst.dtype)
        return carry

    if total == 1:
        one(0, 0)
    else:
        lax.fori_loop(0, total, one, 0)


def scatter_kernel(
    mine_t, grad, small, out, small_out,
    theirs_t, grad_both, sums, near_x, near_y, near_z, mid_x, mid_y, mid_z, far_x, far_y, far_z,
    small_sum, small_sib, small_z, small_x, small_y, finals, other_finals,
    sib_send, sib_recv, send, recv, small_send, small_recv, out_send, out_recv,
):
    x, yh, yl, z, c = place()
    y = yh * 2 + yl
    tokens, width = grad.shape
    half = width // 2
    part_cols = half // PARTS

    def at_x(i):
        return device(i % NX, yh, yl, z, c)

    def at_y(i):
        return device(x, (i % NY) // 2, i % 2, z, c)

    def at_z(i):
        return device(x, yh, yl, i % NZ, c)

    sib = device(x, yh, yl, z, 1 - c)
    pending = []

    def push(src, dst, send_sem, recv_sem, to):
        copy = pltpu.make_async_remote_copy(
            src_ref=src, dst_ref=dst, send_sem=send_sem, recv_sem=recv_sem,
            device_id=to, device_id_type=MESH,
        )
        copy.start()
        pending.append(copy)
        return copy

    def landed(ref, send_sem, recv_sem):
        pltpu.make_async_remote_copy(
            src_ref=ref, dst_ref=ref, send_sem=send_sem, recv_sem=recv_sem,
            device_id=sib, device_id_type=MESH,
        ).wait_recv()

    enter(
        [sib]
        + [at_x(x + i) for i in range(1, NX)]
        + [at_y(y + i) for i in range(1, NY)]
        + [at_z(z + i) for i in range(1, NZ)]
    )

    def half_cols(index):
        return pl.ds(pl.multiple_of(index * half, half), half)

    swap_t = push(mine_t, theirs_t, sib_send.at[0], sib_recv.at[0], sib)
    swap_g = push(grad.at[:, half_cols(1 - c)], grad_both.at[1], sib_send.at[1], sib_recv.at[1], sib)
    swap_s = push(small.at[:, 1 - c], small_sib, sib_send.at[2], sib_recv.at[2], sib)
    grad_both[0] = grad[:, half_cols(c)]
    swap_s.wait_recv()
    small_sum[...] = small[:, c] + small_sib[...]
    swap_g.wait_recv()
    swap_t.wait_recv()

    owner_rows = mine_t.shape[0] // (NX * 2)

    def make_terms(p):
        span = pl.ds(p * part_cols, part_cols)

        def one(o, carry):
            rows = pl.ds(pl.multiple_of(o * owner_rows, 32), owner_rows)
            term = jnp.dot(mine_t[rows, :], grad_both[0, :, span], preferred_element_type=jnp.float32)
            term = term + jnp.dot(theirs_t[rows, :], grad_both[1, :, span], preferred_element_type=jnp.float32)
            ox, oy = o // 2, o % 2
            for q in range(4):
                for t in range(4):
                    sums[p, ox, oy * 2 + t // 2, (t % 2) * 4 + q] = term[
                        q * BLOCK : (q + 1) * BLOCK, t * LANES : (t + 1) * LANES
                    ].astype(sums.dtype)
            return carry

        lax.fori_loop(0, NX * 2, one, 0)

    place_of = {"x": (x, NX, at_x), "y": (y, NY, at_y), "z": (z, NZ, at_z)}
    near = (near_x, near_y, near_z)
    middle = (mid_y, mid_z, mid_x)
    last = (far_z, far_x, far_y)

    def part_flow(p):
        left = ["x", "y", "z"]
        fixed = {}
        for stage, axis in enumerate(PART_AXES[p]):
            me, n, dev = place_of[axis]
            rest = [a for a in left if a != axis]
            lead = tuple(place_of[a][1] for a in rest)
            buffers = (near, middle, last)[stage][p]

            def chunk(i, part=None):
                index = []
                for a in ("x", "y", "z"):
                    if a in fixed:
                        index.append(fixed[a])
                    elif a == axis:
                        index.append(i % n)
                    elif part is not None and a == rest[0]:
                        size = place_of[a][1] // 2
                        index.append(pl.ds(part * size, size))
                    else:
                        index.append(slice(None))
                return sums.at[(p,) + tuple(index)]

            def landing(step, way, part=None):
                ref = buffers.at[step, way]
                if part is not None:
                    size = lead[0] // 2
                    ref = ref.at[pl.ds(part * size, size)]
                return ref

            steps = n // 2
            for step in range(steps):
                k = steps - step
                split = step == 0 and bool(rest)
                half_lead = (lead[0] // 2,) + lead[1:] if split else lead
                parts = (0, 1) if split else (None, None)
                ways = (0, 1) if (step > 0 or split) else (0,)
                sems = [(send.at[p, stage, step, w], recv.at[p, stage, step, w]) for w in (0, 1)]
                for w in ways:
                    sign = 1 if w == 0 else -1
                    push(chunk(me + n + sign * k, parts[w]), landing(step, w, parts[w]), *sems[w], dev(me + n + sign))
                yield
                for w in ways:
                    landed(landing(step, w, parts[w]), *sems[w])
                if step < steps - 1:
                    for w in ways:
                        sign = 1 if w == 0 else -1
                        add_into(chunk(me + n + sign * (k - 1), parts[w]), [landing(step, w, parts[w])], half_lead)
                else:
                    add_into(chunk(me), [landing(step, 0), landing(step, 1)], lead)
            fixed[axis] = me
            left.remove(axis)

    def small_flow():
        def spread(source, slots, me, n, dev, base):
            for i in range(1, n):
                push(
                    source((me + i) % n), slots.at[me],
                    small_send.at[base + i], small_recv.at[base + i], dev(me + i),
                )

        def collect(slots, me, n, base):
            for i in range(1, n):
                landed(slots.at[(me + n - i) % n], small_send.at[base + i], small_recv.at[base + i])

        small_z[z] = small_sum[z]
        spread(lambda i: small_sum.at[i], small_z, z, NZ, at_z, 0)
        yield
        collect(small_z, z, NZ, 0)
        total = small_z[0]
        for i in range(1, NZ):
            total = total + small_z[i]
        small_x[x] = total
        spread(lambda i: small_x.at[x], small_x, x, NX, at_x, 8)
        yield
        collect(small_x, x, NX, 8)
        total = small_x[0]
        for i in range(1, NX):
            total = total + small_x[i]
        small_y[y] = total
        spread(lambda i: small_y.at[y], small_y, y, NY, at_y, 12)
        yield
        collect(small_y, y, NY, 12)
        total = small_y[0]
        for i in range(1, NY):
            total = total + small_y[i]
        small_out[c, z] = total
        spread(lambda i: small_out.at[c, z], small_out.at[c], z, NZ, at_z, 16)
        yield
        collect(small_out.at[c], z, NZ, 16)
        push(small_out.at[c], small_out.at[c], small_send.at[0], small_recv.at[0], sib)
        yield
        landed(small_out.at[1 - c], small_send.at[0], small_recv.at[0])

    flows = [part_flow(p) for p in range(PARTS)] + [small_flow()]

    def resume(i):
        try:
            next(flows[i])
        except StopIteration:
            pass

    make_terms(2)
    resume(2)
    make_terms(1)
    resume(1)
    make_terms(0)
    resume(0)
    resume(3)
    for i in (2, 1, 0, 2, 2, 3, 1, 0, 3, 2):
        resume(i)
    for _ in range(4):
        for i in (1, 0, 2):
            resume(i)
    resume(3)
    for _ in range(3):
        for i in (1, 0, 2):
            resume(i)
    resume(3)
    resume(3)

    def final(layer, k):
        return finals.at[layer, k % NZ]

    for p in range(PARTS):
        finals[yl, z, p] = sums[p, x, y, z]
    to_ys = device(x, yh, 1 - yl, z, c)
    push(final(yl, z), final(yl, z), out_send.at[0, 0, 0], out_recv.at[0, 0, 0], to_ys)
    for layer_is_mine in (True,):
        push(final(yl, z), final(yl, z), out_send.at[1, 0, 0], out_recv.at[1, 0, 0], at_z(z + 1))
        push(final(yl, z), final(yl, z), out_send.at[1, 0, 1], out_recv.at[1, 0, 1], at_z(z + NZ - 1))
    landed(final(1 - yl, z), out_send.at[0, 0, 0], out_recv.at[0, 0, 0])
    push(final(1 - yl, z), final(1 - yl, z), out_send.at[1, 1, 0], out_recv.at[1, 1, 0], at_z(z + 1))
    push(final(1 - yl, z), final(1 - yl, z), out_send.at[1, 1, 1], out_recv.at[1, 1, 1], at_z(z + NZ - 1))

    def to_sibling(layer, k, index):
        @pl.when((k % 4) // 2 != c)
        def _():
            pltpu.make_async_remote_copy(
                src_ref=final(layer, k), dst_ref=other_finals.at[layer, k % NZ],
                send_sem=sib_send.at[4 + index], recv_sem=sib_recv.at[4 + index],
                device_id=sib, device_id_type=MESH,
            ).start()

    def sibling_done(layer, k, index):
        @pl.when((k % 4) // 2 != c)
        def _():
            pltpu.make_async_remote_copy(
                src_ref=final(layer, k), dst_ref=other_finals.at[layer, k % NZ],
                send_sem=sib_send.at[4 + index], recv_sem=sib_recv.at[4 + index],
                device_id=sib, device_id_type=MESH,
            ).wait_send()

        @pl.when((k % 4) // 2 == c)
        def _():
            landed(other_finals.at[layer, k % NZ], sib_send.at[4 + index], sib_recv.at[4 + index])

    layers = (yl, 1 - yl)
    for j in (0, 1):
        to_sibling(layers[j], z, j * NZ)
    for s in (1, 2, 3, 4):
        for j in (0, 1):
            for w in (0, 1):
                if s == 4 and w != j:
                    continue
                k = z + NZ - s if w == 0 else z + s
                landed(final(layers[j], k), out_send.at[s, j, w], out_recv.at[s, j, w])
                onward = s < 3 or (s == 3 and w == j)
                if onward:
                    push(
                        final(layers[j], k), final(layers[j], k),
                        out_send.at[s + 1, j, w], out_recv.at[s + 1, j, w],
                        at_z(z + 1) if w == 0 else at_z(z + NZ - 1),
                    )
                to_sibling(layers[j], k % NZ, j * NZ + (NZ - s if w == 0 else s))
    for j in (0, 1):
        for k in range(NZ):
            sibling_done(layers[j], (z + k) % NZ, j * NZ + k)

    for layer in (0, 1):
        for zh in (0, 1):
            for p in range(PARTS):
                column = p * part_cols + (layer * 2 + zh) * LANES
                for source, which in ((finals, c), (other_finals, 1 - c)):
                    block = jnp.concatenate(
                        [wide(source[layer, zh * 4 + 2 * c + r, p]) for r in (0, 1)], axis=0
                    )
                    start = pl.multiple_of(which * half + column, LANES)
                    out[:, pl.ds(start, LANES)] = block.astype(out.dtype)
    for copy in pending:
        copy.wait_send()


def scatter_rows(mine_t, grad, small, cap):
    slots, tokens = mine_t.shape
    width = grad.shape[1]
    bf, f32 = jnp.bfloat16, jnp.float32
    block = (BLOCK, LANES)
    vmem = pl.BlockSpec(memory_space=pltpu.VMEM)
    return pl.pallas_call(
        scatter_kernel,
        out_shape=(
            jax.ShapeDtypeStruct((cap, width), bf),
            jax.ShapeDtypeStruct((2, NZ) + small.shape[2:], f32),
        ),
        in_specs=[vmem] * 3,
        out_specs=(vmem, vmem),
        scratch_shapes=[
            pltpu.VMEM((slots, tokens), bf),
            pltpu.VMEM((2, tokens, width // 2), bf),
            pltpu.VMEM((PARTS, NX, NY, NZ) + block, bf),
            pltpu.VMEM((2, 2, NY, NZ) + block, bf),
            pltpu.VMEM((2, 2, NX, NZ) + block, bf),
            pltpu.VMEM((4, 2, NX, NY) + block, bf),
            pltpu.VMEM((2, 2, NY) + block, bf),
            pltpu.VMEM((2, 2, NZ) + block, bf),
            pltpu.VMEM((4, 2, NX) + block, bf),
            pltpu.VMEM((2, 2) + block, bf),
            pltpu.VMEM((2, 2) + block, bf),
            pltpu.VMEM((4, 2) + block, bf),
            pltpu.VMEM((NZ,) + small.shape[2:], f32),
            pltpu.VMEM((NZ,) + small.shape[2:], f32),
            pltpu.VMEM((NZ,) + small.shape[2:], f32),
            pltpu.VMEM((NX,) + small.shape[2:], f32),
            pltpu.VMEM((NY,) + small.shape[2:], f32),
            pltpu.VMEM((2, NZ, PARTS) + block, bf),
            pltpu.VMEM((2, NZ, PARTS) + block, bf),
            pltpu.SemaphoreType.DMA((20,)),
            pltpu.SemaphoreType.DMA((20,)),
            pltpu.SemaphoreType.DMA((PARTS, 3, 4, 2)),
            pltpu.SemaphoreType.DMA((PARTS, 3, 4, 2)),
            pltpu.SemaphoreType.DMA((24,)),
            pltpu.SemaphoreType.DMA((24,)),
            pltpu.SemaphoreType.DMA((5, 2, 2)),
            pltpu.SemaphoreType.DMA((5, 2, 2)),
        ],
        compiler_params=pltpu.CompilerParams(
            collective_id=1, has_side_effects=True, vmem_limit_bytes=48 << 20
        ),
        name="scatter_rows",
    )(mine_t, grad, small)


EPSILON = 1e-05

STEP = 32
SEG = 8
WIDE = 256


def contract_last(a, b):
    return lax.dot_general(a, b, (((1,), (1,)), ((), ())), preferred_element_type=jnp.float32)


def over_lanes(value, count):
    return jnp.sum(value, axis=-1, keepdims=True) * (1.0 / count)


def extend(ext, value, taps):
    before = taps // 2
    seg = lax.broadcasted_iota(jnp.int32, (before, SEG, LANES), 1)
    ext[pl.ds(before, STEP)] = value
    late = pltpu.roll(value[STEP - before :], 1, 1)
    ext[pl.ds(0, before)] = jnp.where(seg == 0, 0.0, late)
    early = pltpu.roll(value[:before], SEG - 1, 1)
    ext[pl.ds(before + STEP, before)] = jnp.where(seg == SEG - 1, 0.0, early)


def layer_kernel(
    length_ref, frames_ref, cot_ref, slots_hbm, owner_ref, gain_in_ref, gain_mid_ref, taps_ref,
    out_ref, slots_t_ref, grad_ref, small_ref,
    weight, chosen, natural, cots, normed, in_slots, means, inverses, left, gate, held, conv, deriv,
    ext_d, taps_wide, keep, acc_a, acc_b, back, weight_sem,
):
    features = frames_ref.shape[1]
    slabs = features // LANES
    taps = taps_ref.shape[0]
    slots = owner_ref.shape[1]
    blocks = features // WIDE
    f32 = jnp.float32

    def weight_copy(i):
        span = pl.ds(pl.multiple_of(i * WIDE, WIDE), WIDE)
        return pltpu.make_async_copy(slots_hbm.at[:, span], weight.at[:, span], weight_sem.at[i])

    for i in range(blocks):
        weight_copy(i).start()
        weight_copy(i + blocks).start()

    for k in range(slabs):
        lanes = pl.ds(k * LANES, LANES)
        natural[k] = frames_ref[:, lanes].astype(f32)
        cots[k] = cot_ref[:, lanes].astype(f32)
        taps_wide[k] = jnp.broadcast_to(taps_ref[:, lanes][:, None, :], (taps, SEG, LANES))
    step_of = lax.broadcasted_iota(jnp.int32, (STEP, SEG, LANES), 0)
    seg_of = lax.broadcasted_iota(jnp.int32, (STEP, SEG, LANES), 1)
    keep[...] = (seg_of * STEP + step_of < length_ref[0]).astype(f32)

    def row(ref, k, j):
        return ref[k, pl.ds(j, SEG, stride=STEP), :]

    def gain(ref, k):
        return ref[:, pl.ds(k * LANES, LANES)]

    def norm_pair(i, carry):
        parts = []
        for j in (2 * i, 2 * i + 1):
            values = [row(natural, k, j) for k in range(slabs)]
            total = values[0]
            for v in values[1:]:
                total = total + v
            mean = over_lanes(total, features)
            values = [v - mean for v in values]
            total = values[0] * values[0]
            for v in values[1:]:
                total = total + v * v
            inverse = lax.rsqrt(over_lanes(total, features) + EPSILON)
            means[j] = jnp.broadcast_to(mean, (SEG, LANES))
            inverses[j] = jnp.broadcast_to(inverse, (SEG, LANES))
            parts.append([v * inverse * gain(gain_in_ref, k) for k, v in enumerate(values)])
        for k in range(slabs):
            pair = jnp.concatenate([parts[0][k], parts[1][k]], axis=0)
            normed[pl.ds(pl.multiple_of(i * 16, 16), 16), pl.ds(k * LANES, LANES)] = pair.astype(normed.dtype)
        return carry

    lax.fori_loop(0, STEP // 2, norm_pair, 0)

    def choose(i, carry):
        span = pl.ds(pl.multiple_of(i * WIDE, WIDE), WIDE)
        rows = lax.broadcasted_iota(jnp.int32, (features, WIDE), 0)
        picked = jnp.where(rows == owner_ref[:, span], 1.0, 0.0).astype(chosen.dtype)
        chosen[:, span] = picked
        moved = jnp.dot(normed[...], picked, preferred_element_type=f32)
        in_slots[:, span] = moved.astype(in_slots.dtype)
        slots_t_ref[span, :] = jnp.transpose(moved).astype(slots_t_ref.dtype)
        return carry

    lax.fori_loop(0, slots // WIDE, choose, 0)

    acc_a[...] = jnp.zeros_like(acc_a)

    def tap_rows(ext, k, sign):
        def one(b, carry):
            base = b * SEG
            first = base if sign > 0 else base + 1
            lines = [ext[first + i] for i in range(taps + SEG - 1)]
            sums = [None] * SEG
            for t in range(taps):
                w = taps_wide[k, t if sign > 0 else taps - 1 - t]
                for i in range(SEG):
                    term = w * lines[i + t]
                    sums[i] = term if sums[i] is None else sums[i] + term
            for i in range(SEG):
                carry(base + i, sums[i])
            return 0
        return one

    def forward(i, carry):
        weight_copy(i).wait()
        weight_copy(i + blocks).wait()
        span_a = pl.ds(pl.multiple_of(i * WIDE, WIDE), WIDE)
        span_b = pl.ds(pl.multiple_of(features + i * WIDE, WIDE), WIDE)
        value = jnp.dot(in_slots[...], weight[:, span_a], preferred_element_type=f32)
        opened = jax.nn.sigmoid(jnp.dot(in_slots[...], weight[:, span_b], preferred_element_type=f32))
        for h in range(WIDE // LANES):
            k = i * (WIDE // LANES) + h
            a = value[:, h * LANES : (h + 1) * LANES].reshape(STEP, SEG, LANES)
            s = opened[:, h * LANES : (h + 1) * LANES].reshape(STEP, SEG, LANES)
            left[k] = a
            gate[k] = s
            extend(held.at[k], a * s * keep[...], taps)

            def put(j, v, k=k):
                conv[k, j] = v
                acc_a[j] = acc_a[j] + v

            run = tap_rows(held.at[k], k, 1)
            lax.fori_loop(0, STEP // SEG, lambda b, c: run(b, put), 0)
        return carry

    lax.fori_loop(0, blocks, forward, 0)

    acc_b[...] = jnp.zeros_like(acc_b)
    back[0] = jnp.broadcast_to(over_lanes(acc_a[...], features), (STEP, SEG, LANES))

    def centre(k, carry):
        v = conv[k] - back[0]
        conv[k] = v
        acc_b[...] += v * v
        return carry

    lax.fori_loop(0, slabs, centre, 0)
    back[1] = jnp.broadcast_to(lax.rsqrt(over_lanes(acc_b[...], features) + EPSILON), (STEP, SEG, LANES))
    acc_a[...] = jnp.zeros_like(acc_a)
    acc_b[...] = jnp.zeros_like(acc_b)

    def order_cot(j, carry):
        for k in range(slabs):
            deriv[k, j] = row(cots, k, j)
        return carry

    lax.fori_loop(0, STEP, order_cot, 0)

    small_rows = small_ref.shape[0] // slabs // SEG * SEG
    small_ref[...] = jnp.zeros_like(small_ref)

    def small_row(k, r):
        return pl.ds(pl.multiple_of(k * small_rows, SEG) + r, 1)

    def middle(k, carry):
        lanes = pl.ds(pl.multiple_of(k * LANES, LANES), LANES)
        g = gain_mid_ref[:, lanes]
        hat = conv[k] * back[1]
        mixed = hat * g
        s = jax.nn.sigmoid(mixed)
        d = deriv[k] * keep[...] * (s * (1.0 + mixed * (1.0 - s)))
        dh = d * hat
        small_ref[small_row(k, taps + 1), :] = jnp.sum(jnp.sum(dh, axis=0), axis=0, keepdims=True)
        conv[k] = hat
        d = d * g
        deriv[k] = d
        acc_a[...] += d
        acc_b[...] += dh * g
        return carry

    lax.fori_loop(0, slabs, middle, 0)
    acc_a[...] = jnp.broadcast_to(over_lanes(acc_a[...], features), (STEP, SEG, LANES))
    acc_b[...] = jnp.broadcast_to(over_lanes(acc_b[...], features), (STEP, SEG, LANES))

    def backward(k, carry):
        extend(ext_d, back[1] * (deriv[k] - acc_a[...] - conv[k] * acc_b[...]), taps)

        def put(j, v):
            deriv[k, j] = v * keep[j]

        run = tap_rows(ext_d, k, -1)
        lax.fori_loop(0, STEP // SEG, lambda b, c: run(b, put), 0)
        half = taps // 2
        for t0 in (0, half):
            def one(b, sums):
                base = b * SEG
                ds = [ext_d[half + base + i] for i in range(SEG)]
                lines = [held[k, base + t0 + i] for i in range(half + SEG - 1)]
                return tuple(
                    functools.reduce(lambda p, q: p + q, [ds[i] * lines[i + t] for i in range(SEG)], sums[t])
                    for t in range(half)
                )

            sums = lax.fori_loop(0, STEP // SEG, one, tuple(jnp.zeros((SEG, LANES), f32) for _ in range(half)))
            for t in range(half):
                small_ref[small_row(k, t0 + t), :] = jnp.sum(sums[t], axis=0, keepdims=True)
        d = deriv[k] * gate[k]
        lanes = pl.ds(pl.multiple_of(k * LANES, LANES), LANES)
        lanes_b = pl.ds(pl.multiple_of(features + k * LANES, LANES), LANES)
        tokens = STEP * SEG
        grad_ref[:, lanes] = d.reshape(tokens, LANES).astype(grad_ref.dtype)
        db = d * left[k] * (1.0 - gate[k])
        grad_ref[:, lanes_b] = db.reshape(tokens, LANES).astype(grad_ref.dtype)
        return carry

    lax.fori_loop(0, slabs, backward, 0)

    def slot_grads(i, carry):
        span = pl.ds(pl.multiple_of(i * WIDE, WIDE), WIDE)
        in_slots[:, span] = contract_last(grad_ref[...], weight[span, :]).astype(in_slots.dtype)
        return carry

    lax.fori_loop(0, slots // WIDE, slot_grads, 0)

    def feature_grads(i, carry):
        span = pl.ds(pl.multiple_of(i * WIDE, WIDE), WIDE)
        g = contract_last(in_slots[...], chosen[span, :])
        for h in range(WIDE // LANES):
            deriv[i * (WIDE // LANES) + h] = g[:, h * LANES : (h + 1) * LANES].reshape(STEP, SEG, LANES)
        return carry

    lax.fori_loop(0, blocks, feature_grads, 0)

    def first_norm(j, sums):
        hats = [(row(natural, k, j) - means[j]) * inverses[j] for k in range(slabs)]
        gs = [deriv[k, j] for k in range(slabs)]
        sums = tuple(s + g * h for s, g, h in zip(sums, gs, hats))
        gs = [g * gain(gain_in_ref, k) for k, g in enumerate(gs)]
        total, cross = gs[0], gs[0] * hats[0]
        for g, h in zip(gs[1:], hats[1:]):
            total, cross = total + g, cross + g * h
        total, cross = over_lanes(total, features), over_lanes(cross, features)
        for k in range(slabs):
            v = row(cots, k, j) + inverses[j] * (gs[k] - total - hats[k] * cross)
            cots[k, pl.ds(j, SEG, stride=STEP), :] = v
        return sums

    sums = lax.fori_loop(0, STEP, first_norm, tuple(jnp.zeros((SEG, LANES), f32) for _ in range(slabs)))
    for k in range(slabs):
        small_ref[pl.ds(k * small_rows + taps, 1), :] = jnp.sum(sums[k], axis=0, keepdims=True)
        out_ref[:, pl.ds(k * LANES, LANES)] = cots[k].astype(out_ref.dtype)


def run_layer(frames, cotangent, lengths, slots_weight, owner_rows, gain_in, gain_mid, taps, small_rows):
    tokens, features = frames.shape
    slots, width = slots_weight.shape
    slabs = features // LANES
    bf, f32 = jnp.bfloat16, jnp.float32
    vmem = pl.BlockSpec(memory_space=pltpu.VMEM)
    slab = (slabs, STEP, SEG, LANES)
    plane = (STEP, SEG, LANES)
    return pl.pallas_call(
        layer_kernel,
        out_shape=(
            jax.ShapeDtypeStruct((tokens, features), bf),
            jax.ShapeDtypeStruct((slots, tokens), bf),
            jax.ShapeDtypeStruct((tokens, width), bf),
            jax.ShapeDtypeStruct((small_rows, LANES), f32),
        ),
        in_specs=[pl.BlockSpec(memory_space=pltpu.SMEM), vmem, vmem, pl.BlockSpec(memory_space=pl.ANY)] + [vmem] * 4,
        out_specs=(vmem,) * 4,
        scratch_shapes=[
            pltpu.VMEM((slots, width), bf),
            pltpu.VMEM((features, slots), bf),
            pltpu.VMEM((slabs, tokens, LANES), f32),
            pltpu.VMEM((slabs, tokens, LANES), f32),
            pltpu.VMEM((tokens, features), bf),
            pltpu.VMEM((tokens, slots), bf),
            pltpu.VMEM(plane, f32),
            pltpu.VMEM(plane, f32),
            pltpu.VMEM(slab, f32),
            pltpu.VMEM(slab, f32),
            pltpu.VMEM((slabs, STEP + taps.shape[0], SEG, LANES), f32),
            pltpu.VMEM(slab, f32),
            pltpu.VMEM(slab, f32),
            pltpu.VMEM((STEP + taps.shape[0], SEG, LANES), f32),
            pltpu.VMEM((slabs, taps.shape[0], SEG, LANES), f32),
            pltpu.VMEM(plane, f32),
            pltpu.VMEM(plane, f32),
            pltpu.VMEM(plane, f32),
            pltpu.VMEM((2,) + plane, f32),
            pltpu.SemaphoreType.DMA((2 * features // WIDE,)),
        ],
        compiler_params=pltpu.CompilerParams(vmem_limit_bytes=60 << 20),
        cost_estimate=pl.CostEstimate(flops=14 * 10**9, bytes_accessed=25 * 10**6, transcendentals=10**6),
        name="conv_module",
    )(lengths, frames, cotangent, slots_weight, owner_rows[None], gain_in[None], gain_mid[None], taps)


def per_device(frames, cotangent, lengths, weight_slots, owner_rows, gain_in, gain_mid, kernel):
    utterances, length, features = frames.shape
    slots = owner_rows.shape[0]
    cap = weight_slots.shape[0]
    taps = kernel.shape[0]
    slabs = features // LANES
    gathered = gather_rows(weight_slots, slots // cap).reshape(slots, 2 * features)
    small_rows = NZ * 2 * SMALL
    frame_grads, slots_t, grad, small = run_layer(
        frames.reshape(length, features), cotangent.reshape(length, features), lengths, gathered,
        owner_rows, gain_in, gain_mid, kernel, small_rows,
    )
    weight_grads, total = scatter_rows(slots_t, grad, small.reshape(NZ, 2, SMALL, LANES), cap)
    each = small_rows // slabs // SEG * SEG
    total = total.transpose(1, 0, 2, 3).reshape(small_rows, LANES)[: slabs * each]
    total = total.reshape(slabs, each, LANES).transpose(1, 0, 2).reshape(each, features)
    return (frame_grads[None], weight_grads, total[taps], total[taps + 1], total[:taps])


def solution(mesh):
    in_specs = (
        P(("dp", "fsdp"), None, None),
        P(("dp", "fsdp"), None, None),
        P(("dp", "fsdp")),
        P("fsdp", None),
        P(),
        P(),
        P(),
        P(),
    )
    out_specs = (P(("dp", "fsdp"), None, None), P("fsdp", None), P(), P(), P())
    return jax.shard_map(
        per_device, mesh=mesh, in_specs=in_specs, out_specs=out_specs, check_vma=False
    )
```

```python
import functools
import jax
import jax.numpy as jnp
from jax import lax
from jax.experimental import pallas as pl
from jax.experimental.pallas import tpu as pltpu
from jax.sharding import PartitionSpec as P

MESH = pl.DeviceIdType.MESH
NX, NY, NZ = 4, 4, 8
PIECES = 3
PARTS = 3
BLOCK = 72
LANES = 128
SMALL = 32
EPSILON = 1e-05
STEP = 32
SEG = 8
WIDE = 256
PART_AXES = ("zxy", "xyz", "yxz")


def place():
    d = lax.axis_index("dp")
    f = lax.axis_index("fsdp")
    return f // 4, (f // 2) % 2, d // NZ, d % NZ, f % 2


def device(x, yh, yl, z, c):
    return (yl * NZ + z, (x * 2 + yh) * 2 + c)


def wide(value):
    return value.astype(jnp.float32)


def split_index(i, lead):
    index = []
    for size in reversed(lead):
        index.append(i % size)
        i = i // size
    return tuple(reversed(index))


def add_into(dst, sources, lead):
    total = 1
    for size in lead:
        total *= size

    def one(i, carry):
        index = split_index(i, lead)
        value = wide(dst[index])
        for src in sources:
            value = value + wide(src[index])
        dst[index] = value.astype(dst.dtype)
        return carry

    if total == 1:
        one(0, 0)
    else:
        lax.fori_loop(0, total, one, 0)


def contract_last(a, b):
    return lax.dot_general(a, b, (((1,), (1,)), ((), ())), preferred_element_type=jnp.float32)


def over_lanes(value, count):
    return jnp.sum(value, axis=-1, keepdims=True) * (1.0 / count)


def extend(ext, value, taps):
    before = taps // 2
    seg = lax.broadcasted_iota(jnp.int32, (before, SEG, LANES), 1)
    ext[pl.ds(before, STEP)] = value
    late = pltpu.roll(value[STEP - before :], 1, 1)
    ext[pl.ds(0, before)] = jnp.where(seg == 0, 0.0, late)
    early = pltpu.roll(value[:before], SEG - 1, 1)
    ext[pl.ds(before + STEP, before)] = jnp.where(seg == SEG - 1, 0.0, early)


def module_kernel(
    length_ref, frames_ref, cot_ref, w_ref, owner_ref, gain_in_ref, gain_mid_ref, taps_ref,
    out_ref, rows_ref, small_out,
    weight, natural, cots, normed, in_slots, slots_t, grad, means, inverses, left, gate, held,
    conv, deriv, ext_d, taps_wide, keep, acc_a, acc_b, back, small, small_split,
    theirs_t, theirs_g, sums, low, near_x, near_y, near_z, mid_0, mid_1, mid_2, far_0, far_1, far_2,
    small_sum, small_sib, small_z, small_x, small_y, finals, other_finals,
    keep_sem, w_send, w_recv, swap_send, swap_recv, send, recv, direct_send, direct_recv, small_send, small_recv,
    out_send, out_recv, sib_send, sib_recv,
):
    x, yh, yl, z, c = place()
    y = yh * 2 + yl
    f32 = jnp.float32
    features = frames_ref.shape[1]
    slabs = features // LANES
    taps = taps_ref.shape[0]
    slots = owner_ref.shape[1]
    blocks = features // WIDE
    tokens = STEP * SEG
    cap, width = w_ref.shape
    part_cols = features // PARTS

    def at_x(i):
        return device(i % NX, yh, yl, z, c)

    def at_y(i):
        return device(x, (i % NY) // 2, i % 2, z, c)

    def at_z(i):
        return device(x, yh, yl, i % NZ, c)

    sib = device(x, yh, yl, z, 1 - c)
    to_ac = device(x, 1 - yh, 1 - yl, z, c)
    to_ys = device(x, yh, 1 - yl, z, c)
    pending = []

    def push(src, dst, send_sem, recv_sem, to):
        copy = pltpu.make_async_remote_copy(
            src_ref=src, dst_ref=dst, send_sem=send_sem, recv_sem=recv_sem,
            device_id=to, device_id_type=MESH,
        )
        copy.start()
        pending.append(copy)
        return copy

    def landed(ref, send_sem, recv_sem):
        pltpu.make_async_remote_copy(
            src_ref=ref, dst_ref=ref, send_sem=send_sem, recv_sem=recv_sem,
            device_id=sib, device_id_type=MESH,
        ).wait_recv()

    peers = (
        [sib]
        + [at_x(x + i) for i in range(1, NX)]
        + [at_y(y + i) for i in range(1, NY)]
        + [at_z(z + i) for i in range(1, NZ)]
    )
    barrier = pltpu.get_barrier_semaphore()
    for peer in peers:
        pl.semaphore_signal(barrier, inc=1, device_id=peer, device_id_type=MESH)
    pl.semaphore_wait(barrier, len(peers))

    xs = [x, (x + 3) % NX, (x + 1) % NX, (x + 2) % NX]
    to_xp, to_xm, to_zp, to_zm = at_x(x + 1), at_x(x + 3), at_z(z + 1), at_z(z + NZ - 1)
    third = width // 3
    piece_rows = cap // PIECES
    par = z % 2
    base = par * third

    def cols(start, size):
        return pl.ds(pl.multiple_of(start, third // 2), size)

    window = cols(base, 2 * third)
    halves = [cols(base, third), cols(base + third, third)]
    mine = cols(base + yl * third, third)
    other = cols(base + (1 - yl) * third, third)
    shared = [cols(base + par * third, third // 2), cols(base + par * third + third // 2, third // 2)]
    theirs = [cols((1 - par) * 2 * third, third // 2), cols((1 - par) * 2 * third + third // 2, third // 2)]

    def owner(k, other_row):
        return (xs[k] * 2 + (1 - yh if other_row else yh)) * 2 + c

    def piece(ref, q, span):
        return ref.at[pl.ds(q * piece_rows, piece_rows), span]

    def w_push(index, q, src, dst, to):
        push(src, dst, w_send.at[index, q], w_recv.at[index, q], to)

    def pass_on(index, q, who, span, to):
        ref = piece(weight.at[who], q, span)
        w_push(index, q, ref, ref, to)

    def arrive(index, q, who, span):
        landed(piece(weight.at[who], q, span), w_send.at[index, q], w_recv.at[index, q])

    me = owner(0, False)
    x_copies = [
        [
            pltpu.make_async_remote_copy(
                src_ref=piece(w_ref, q, window), dst_ref=piece(weight.at[me], q, window),
                send_sem=w_send.at[index, q], recv_sem=w_recv.at[index, q],
                device_id=to, device_id_type=MESH,
            )
            for index, to in ((1, to_xp), (2, to_xm))
        ]
        for q in range(PIECES)
    ]

    def x_next(q):
        for copy in x_copies[q - 1]:
            copy.wait_send()
        for copy in x_copies[q]:
            copy.start()

    for copy in x_copies[0]:
        copy.start()
    pending.extend(x_copies[-1])
    for q in range(PIECES):
        w_push(3, q, piece(w_ref, q, mine), piece(weight.at[me], q, mine), to_ac)
    w_push(0, 0, w_ref, weight.at[me], sib)
    own_copy = pltpu.make_async_copy(w_ref, weight.at[me], keep_sem)
    own_copy.start()

    def z_out(slot, q, who):
        pass_on(13 + slot, q, who, shared[0], to_zp)
        pass_on(20 + slot, q, who, shared[1], to_zm)

    units = [(1, False), (2, False), (3, False), (0, True), (1, True), (2, True), (3, True)]

    def x_near(k, q):
        arrive(k, q, owner(k, False), window)
        pass_on(6 + k, q, owner(k, False), halves[k - 1], (to_xp, to_xm)[k - 1])
        pass_on(3 + k, q, owner(k, False), mine, to_ac)
        z_out(k - 1, q, owner(k, False))
        pass_on(26 + k, q, owner(k, False), window, sib)

    def x_far(q):
        arrive(7, q, owner(3, False), halves[0])
        arrive(8, q, owner(3, False), halves[1])
        pass_on(6, q, owner(3, False), mine, to_ac)
        z_out(2, q, owner(3, False))
        pass_on(29, q, owner(3, False), halves[0], sib)
        pass_on(30, q, owner(3, False), halves[1], sib)

    def across(k, q):
        arrive(3 + k, q, owner(k, True), other)
        pass_on(9 + k, q, owner(k, True), other, to_ys)
        pass_on(31 + k, q, owner(k, True), other, sib)

    def beside(k, q):
        arrive(9 + k, q, owner(k, True), mine)
        z_out(3 + k, q, owner(k, True))
        pass_on(35 + k, q, owner(k, True), mine, sib)

    def z_in(slot, q):
        who = owner(*units[slot])
        arrive(13 + slot, q, who, theirs[0])
        pass_on(39 + slot, q, who, theirs[0], sib)
        arrive(20 + slot, q, who, theirs[1])
        pass_on(46 + slot, q, who, theirs[1], sib)

    def flip(who):
        return who + 1 - 2 * c

    def from_sibling():
        landed(weight.at[flip(me)], w_send.at[0, 0], w_recv.at[0, 0])
        for q in range(PIECES):
            arrive(27, q, flip(owner(1, False)), window)
            arrive(28, q, flip(owner(2, False)), window)
            arrive(29, q, flip(owner(3, False)), halves[0])
            arrive(30, q, flip(owner(3, False)), halves[1])
            for k in range(4):
                arrive(31 + k, q, flip(owner(k, True)), other)
                arrive(35 + k, q, flip(owner(k, True)), mine)
            for slot in range(7):
                arrive(39 + slot, q, flip(owner(*units[slot])), theirs[0])
                arrive(46 + slot, q, flip(owner(*units[slot])), theirs[1])
        own_copy.wait()

    def row(ref, k, j):
        return ref[k, pl.ds(j, SEG, stride=STEP), :]

    def gain(ref, k):
        return ref[:, pl.ds(k * LANES, LANES)]

    def prepare():
        for k in range(slabs):
            lanes = pl.ds(k * LANES, LANES)
            natural[k] = wide(frames_ref[:, lanes])
            taps_wide[k] = jnp.broadcast_to(taps_ref[:, lanes][:, None, :], (taps, SEG, LANES))
        step_of = lax.broadcasted_iota(jnp.int32, (STEP, SEG, LANES), 0)
        seg_of = lax.broadcasted_iota(jnp.int32, (STEP, SEG, LANES), 1)
        keep[...] = (seg_of * STEP + step_of < length_ref[0]).astype(f32)

    def prepare_cots():
        for k in range(slabs):
            cots[k] = wide(cot_ref[:, pl.ds(k * LANES, LANES)])
        small[...] = jnp.zeros_like(small)

    def norm_pair(i, carry):
        parts = []
        for j in (2 * i, 2 * i + 1):
            values = [row(natural, k, j) for k in range(slabs)]
            total = values[0]
            for v in values[1:]:
                total = total + v
            mean = over_lanes(total, features)
            values = [v - mean for v in values]
            total = values[0] * values[0]
            for v in values[1:]:
                total = total + v * v
            inverse = lax.rsqrt(over_lanes(total, features) + EPSILON)
            means[j] = jnp.broadcast_to(mean, (SEG, LANES))
            inverses[j] = jnp.broadcast_to(inverse, (SEG, LANES))
            parts.append([v * inverse * gain(gain_in_ref, k) for k, v in enumerate(values)])
        for k in range(slabs):
            pair = jnp.concatenate([parts[0][k], parts[1][k]], axis=0)
            normed[pl.ds(pl.multiple_of(i * 16, 16), 16), pl.ds(k * LANES, LANES)] = pair.astype(normed.dtype)
        return carry

    def norm_some(i):
        lax.fori_loop(4 * i, 4 * i + 4, norm_pair, 0)

    def slab_mask(owned, k):
        return jnp.where((owned >= k * LANES) & (owned < (k + 1) * LANES), 1.0, 0.0).astype(normed.dtype)

    def choose(i):
        span = pl.ds(i * WIDE, WIDE)
        rows = lax.broadcasted_iota(jnp.int32, (LANES, WIDE), 0)
        owned = owner_ref[:, span]
        line = jnp.where(rows == owned % LANES, 1.0, 0.0).astype(normed.dtype)
        low[:, span] = line
        picked = jnp.concatenate([line * slab_mask(owned, k) for k in range(slabs)], axis=0)
        moved = jnp.dot(normed[...], picked, preferred_element_type=f32)
        in_slots[:, span] = moved.astype(in_slots.dtype)
        slots_t[span, :] = jnp.transpose(moved).astype(slots_t.dtype)

    slots_copy = pltpu.make_async_remote_copy(
        src_ref=slots_t, dst_ref=theirs_t, send_sem=swap_send.at[0], recv_sem=swap_recv.at[0],
        device_id=sib, device_id_type=MESH,
    )

    def swap_slots():
        slots_copy.start()

    part = functools.partial
    fill = [part(norm_some, i) for i in range(STEP // 8)]
    fill += [part(choose, i) for i in range(slots // WIDE)] + [swap_slots, prepare_cots]
    steps = []
    last = PIECES - 1
    for q in range(PIECES):
        if q < last:
            steps += [part(x_next, q + 1)]
        steps += [part(x_near, 1, q), part(x_near, 2, q), part(across, 0, q)]
        if q > 0:
            steps += [part(across, 1, q - 1), part(across, 2, q - 1), part(beside, 0, q - 1)]
    steps += [part(beside, 0, last)]
    steps += [part(x_far, 0), part(across, 1, last), part(across, 2, last)]
    for q in range(PIECES):
        steps += [part(beside, 1, q), part(beside, 2, q)]
        if q < last:
            steps += [part(x_far, q + 1)]
        steps += [part(across, 3, q), part(z_in, 0, q), part(z_in, 1, q), part(z_in, 3, q)]
    for q in range(PIECES):
        steps += [part(beside, 3, q), part(z_in, 2, q), part(z_in, 4, q), part(z_in, 5, q)]
    for q in range(PIECES):
        steps += [part(z_in, 6, q)]

    prepare()
    for task in fill[:2]:
        task()
    fill = fill[2:]
    for step in steps:
        step()
        if fill:
            fill.pop(0)()
    for task in fill:
        task()
    from_sibling()

    acc_a[...] = jnp.zeros_like(acc_a)

    def tap_rows(ext, k, sign, put):
        def one(b, carry):
            start = b * SEG
            first = start if sign > 0 else start + 1
            lines = [ext[first + i] for i in range(taps + SEG - 1)]
            totals = [None] * SEG
            for t in range(taps):
                w = taps_wide[k, t if sign > 0 else taps - 1 - t]
                for i in range(SEG):
                    term = w * lines[i + t]
                    totals[i] = term if totals[i] is None else totals[i] + term
            for i in range(SEG):
                put(start + i, totals[i])
            return carry

        lax.fori_loop(0, STEP // SEG, one, 0)

    def weight_cols(start):
        return weight[:, :, pl.ds(pl.multiple_of(start, WIDE), WIDE)].reshape(slots, WIDE)

    def forward(i, carry):
        value = jnp.dot(in_slots[...], weight_cols(i * WIDE), preferred_element_type=f32)
        opened = jnp.dot(in_slots[...], weight_cols(features + i * WIDE), preferred_element_type=f32)
        opened = jax.nn.sigmoid(opened)
        for h in range(WIDE // LANES):
            k = i * (WIDE // LANES) + h
            a = value[:, h * LANES : (h + 1) * LANES].reshape(STEP, SEG, LANES)
            s = opened[:, h * LANES : (h + 1) * LANES].reshape(STEP, SEG, LANES)
            left[k] = a
            gate[k] = s
            extend(held.at[k], a * s * keep[...], taps)

            def put(j, v, k=k):
                conv[k, j] = v
                acc_a[j] = acc_a[j] + v

            tap_rows(held.at[k], k, 1, put)
        return carry

    lax.fori_loop(0, blocks, forward, 0)

    acc_b[...] = jnp.zeros_like(acc_b)
    back[0] = jnp.broadcast_to(over_lanes(acc_a[...], features), (STEP, SEG, LANES))

    def centre(k, carry):
        v = conv[k] - back[0]
        conv[k] = v
        acc_b[...] += v * v
        return carry

    lax.fori_loop(0, slabs, centre, 0)
    back[1] = jnp.broadcast_to(lax.rsqrt(over_lanes(acc_b[...], features) + EPSILON), (STEP, SEG, LANES))
    acc_a[...] = jnp.zeros_like(acc_a)
    acc_b[...] = jnp.zeros_like(acc_b)

    def order_cot(j, carry):
        for k in range(slabs):
            deriv[k, j] = row(cots, k, j)
        return carry

    lax.fori_loop(0, STEP, order_cot, 0)
    small_rows = small.shape[0] // slabs // SEG * SEG

    def small_row(k, r):
        return pl.ds(pl.multiple_of(k * small_rows, SEG) + r, 1)

    def middle(k, carry):
        g = gain_mid_ref[:, pl.ds(pl.multiple_of(k * LANES, LANES), LANES)]
        hat = conv[k] * back[1]
        mixed = hat * g
        s = jax.nn.sigmoid(mixed)
        d = deriv[k] * keep[...] * (s * (1.0 + mixed * (1.0 - s)))
        dh = d * hat
        small[small_row(k, taps + 1), :] = jnp.sum(jnp.sum(dh, axis=0), axis=0, keepdims=True)
        conv[k] = hat
        d = d * g
        deriv[k] = d
        acc_a[...] += d
        acc_b[...] += dh * g
        return carry

    lax.fori_loop(0, slabs, middle, 0)
    acc_a[...] = jnp.broadcast_to(over_lanes(acc_a[...], features), (STEP, SEG, LANES))
    acc_b[...] = jnp.broadcast_to(over_lanes(acc_b[...], features), (STEP, SEG, LANES))

    def backward(k, carry):
        extend(ext_d, back[1] * (deriv[k] - acc_a[...] - conv[k] * acc_b[...]), taps)

        def put(j, v):
            deriv[k, j] = v * keep[j]

        tap_rows(ext_d, k, -1, put)
        half = taps // 2
        for t0 in (0, half):
            def one(b, totals):
                start = b * SEG
                ds = [ext_d[half + start + i] for i in range(SEG)]
                lines = [held[k, start + t0 + i] for i in range(half + SEG - 1)]
                return tuple(
                    functools.reduce(lambda p, q: p + q, [ds[i] * lines[i + t] for i in range(SEG)], totals[t])
                    for t in range(half)
                )

            totals = lax.fori_loop(0, STEP // SEG, one, tuple(jnp.zeros((SEG, LANES), f32) for _ in range(half)))
            for t in range(half):
                small[small_row(k, t0 + t), :] = jnp.sum(totals[t], axis=0, keepdims=True)
        d = deriv[k] * gate[k]
        lanes = pl.ds(pl.multiple_of(k * LANES, LANES), LANES)
        lanes_b = pl.ds(pl.multiple_of(features + k * LANES, LANES), LANES)
        grad[:, lanes] = d.reshape(tokens, LANES).astype(grad.dtype)
        db = d * left[k] * (1.0 - gate[k])
        grad[:, lanes_b] = db.reshape(tokens, LANES).astype(grad.dtype)
        return carry

    owner_rows = slots // (NX * 2)

    def half_cols(index, p):
        return pl.ds(pl.multiple_of(index * features + p * part_cols, part_cols), part_cols)

    def swap_part(p):
        return push(grad.at[:, half_cols(1 - c, p)], theirs_g.at[p], swap_send.at[1 + p], swap_recv.at[1 + p], sib)

    def make_terms(p):
        def one(ox, carry):
            rows = pl.ds(pl.multiple_of(ox * 2 * owner_rows, 64), 2 * owner_rows)
            term = jnp.dot(slots_t[rows, :], grad[:, half_cols(c, p)], preferred_element_type=f32)
            term = term + jnp.dot(theirs_t[rows, :], theirs_g[p], preferred_element_type=f32)
            for oy in range(2):
                for q in range(4):
                    for t in range(4):
                        first = (oy * 4 + q) * BLOCK
                        sums[p, ox, oy * 2 + t // 2, (t % 2) * 4 + q] = term[
                            first : first + BLOCK, t * LANES : (t + 1) * LANES
                        ].astype(sums.dtype)
            return carry

        lax.fori_loop(0, NX, one, 0)

    place_of = {"x": (x, NX, at_x), "y": (y, NY, at_y), "z": (z, NZ, at_z)}
    nears = {"x": near_x, "y": near_y, "z": near_z}
    direct_landing = ((mid_0, far_0), (mid_1, far_1), (mid_2, far_2))

    def part_flow(p):
        first, second, third_axis = PART_AXES[p]
        fixed = {}

        def chunk(axis, i, cut=None, half=None):
            index = []
            for a in ("x", "y", "z"):
                if a in fixed:
                    index.append(fixed[a])
                elif a == axis:
                    index.append(i % place_of[a][1])
                elif a == cut:
                    size = place_of[a][1] // 2
                    index.append(pl.ds(half * size, size))
                else:
                    index.append(slice(None))
            return sums.at[(p,) + tuple(index)]

        at, n, dev = place_of[first]
        rest = [a for a in ("x", "y", "z") if a != first]
        lead = tuple(place_of[a][1] for a in rest)
        half_size = lead[0] // 2
        hops = n // 2
        for step in range(hops):
            k = hops - step
            split = step == 0
            lines = []
            for w in (0, 1):
                sign = 1 if w == 0 else -1
                ref = nears[first].at[step, w]
                cut = (rest[0], w) if split else (None, None)
                if split:
                    ref = ref.at[pl.ds(w * half_size, half_size)]
                lines.append((sign, ref, cut, (send.at[p, step, w], recv.at[p, step, w])))
            for sign, ref, cut, sems in lines:
                push(chunk(first, at + n + sign * k, *cut), ref, *sems, dev(at + n + sign))
            yield
            for sign, ref, cut, sems in lines:
                landed(ref, *sems)
            if step < hops - 1:
                shape = (half_size,) + lead[1:] if split else lead
                for sign, ref, cut, sems in lines:
                    add_into(chunk(first, at + n + sign * (k - 1), *cut), [ref], shape)
            else:
                add_into(chunk(first, at), [ref for _, ref, _, _ in lines], lead)
        fixed[first] = at

        for stage, axis in enumerate((second, third_axis)):
            at, n, dev = place_of[axis]
            buffers = direct_landing[p][stage]
            for i in range(1, n):
                push(
                    chunk(axis, at + i), buffers.at[at],
                    direct_send.at[p, stage, i], direct_recv.at[p, stage, i], dev(at + i),
                )
            yield
            sources = [buffers.at[(at + n - i) % n] for i in range(1, n)]
            for i, ref in enumerate(sources):
                landed(ref, direct_send.at[p, stage, i + 1], direct_recv.at[p, stage, i + 1])
            add_into(chunk(axis, at), sources, (place_of[third_axis][1],) if stage == 0 else ())
            fixed[axis] = at

        finals[p, yl, z] = sums[p, x, y, z]
        for i in range(1, NZ):
            push(finals.at[p, yl, z], finals.at[p, yl, z], out_send.at[p, i], out_recv.at[p, i], at_z(z + i))
        yield
        for i in range(1, NZ):
            landed(finals.at[p, yl, (z + NZ - i) % NZ], out_send.at[p, i], out_recv.at[p, i])
        push(finals.at[p, yl], finals.at[p, yl], out_send.at[p, 0], out_recv.at[p, 0], to_ys)

        def pairs(layer, core, store):
            return [store.at[p, layer, pl.ds(zh * 4 + 2 * core, 2)] for zh in (0, 1)]

        def to_sibling(j, layer):
            for zh, (src, dst) in enumerate(zip(pairs(layer, 1 - c, finals), pairs(layer, 1 - c, other_finals))):
                push(src, dst, sib_send.at[p, j, zh], sib_recv.at[p, j, zh], sib)

        to_sibling(0, yl)
        yield
        landed(finals.at[p, 1 - yl], out_send.at[p, 0], out_recv.at[p, 0])
        to_sibling(1, 1 - yl)
        yield
        for j, layer in ((0, yl), (1, 1 - yl)):
            for zh, ref in enumerate(pairs(layer, c, other_finals)):
                landed(ref, sib_send.at[p, j, zh], sib_recv.at[p, j, zh])

    def small_flow():
        def spread(source, held_in, at, n, dev, first):
            for i in range(1, n):
                push(
                    source((at + i) % n), held_in.at[at],
                    small_send.at[first + i], small_recv.at[first + i], dev(at + i),
                )

        def collect(held_in, at, n, first):
            for i in range(1, n):
                landed(held_in.at[(at + n - i) % n], small_send.at[first + i], small_recv.at[first + i])

        def total_of(held_in, n):
            total = held_in[0]
            for i in range(1, n):
                total = total + held_in[i]
            return total

        for half in (0, 1):
            for k in range(NZ):
                small_split[half, k] = small[pl.ds((k * 2 + half) * SMALL, SMALL), :]
        push(small_split.at[1 - c], small_sib, small_send.at[8], small_recv.at[8], sib)
        yield
        landed(small_sib, small_send.at[8], small_recv.at[8])
        small_sum[...] = small_split[c] + small_sib[...]
        small_z[z] = small_sum[z]
        spread(lambda i: small_sum.at[i], small_z, z, NZ, at_z, 0)
        yield
        collect(small_z, z, NZ, 0)
        small_x[x] = total_of(small_z, NZ)
        spread(lambda i: small_x.at[x], small_x, x, NX, at_x, 8)
        yield
        collect(small_x, x, NX, 8)
        small_y[y] = total_of(small_x, NX)
        spread(lambda i: small_y.at[y], small_y, y, NY, at_y, 12)
        yield
        collect(small_y, y, NY, 12)
        small_out[c, z] = total_of(small_y, NY)
        spread(lambda i: small_out.at[c, z], small_out.at[c], z, NZ, at_z, 16)
        yield
        collect(small_out.at[c], z, NZ, 16)
        push(small_out.at[c], small_out.at[c], small_send.at[0], small_recv.at[0], sib)
        yield
        landed(small_out.at[1 - c], small_send.at[0], small_recv.at[0])

    flows = [part_flow(p) for p in range(PARTS)] + [small_flow()]
    over = [False] * len(flows)

    def resume(*which):
        for i in which:
            if not over[i]:
                try:
                    next(flows[i])
                except StopIteration:
                    over[i] = True

    part_slabs = slabs // PARTS

    def backward_some(p):
        lax.fori_loop(p * part_slabs, (p + 1) * part_slabs, backward, 0)

    def start_part(p):
        swap = swap_part(p)
        if p == 0:
            slots_copy.wait()
        swap.wait_recv()
        make_terms(p)
        resume(p)

    def slot_grads(i, carry):
        rows = weight[pl.ds(i * 2, 2)].reshape(2 * cap, width)
        g = contract_last(rows, grad[...])
        slots_t[pl.ds(pl.multiple_of(i * 2 * cap, 32), 2 * cap), :] = g.astype(slots_t.dtype)
        return carry

    def slot_some(lo, hi):
        lax.fori_loop(lo, hi, slot_grads, 0)

    def feature_grads(i, carry):
        owned = owner_ref[...]
        picked = jnp.concatenate([low[...] * slab_mask(owned, 2 * i + h) for h in (0, 1)], axis=0)
        g = jnp.transpose(jnp.dot(picked, slots_t[...], preferred_element_type=f32))
        for h in range(WIDE // LANES):
            deriv[i * (WIDE // LANES) + h] = g[:, h * LANES : (h + 1) * LANES].reshape(STEP, SEG, LANES)
        return carry

    def feature_some(lo, hi):
        lax.fori_loop(lo, hi, feature_grads, 0)

    def first_norm(j, totals):
        hats = [(row(natural, k, j) - means[j]) * inverses[j] for k in range(slabs)]
        gs = [deriv[k, j] for k in range(slabs)]
        totals = tuple(s + g * h for s, g, h in zip(totals, gs, hats))
        gs = [g * gain(gain_in_ref, k) for k, g in enumerate(gs)]
        total, cross = gs[0], gs[0] * hats[0]
        for g, h in zip(gs[1:], hats[1:]):
            total, cross = total + g, cross + g * h
        total, cross = over_lanes(total, features), over_lanes(cross, features)
        for k in range(slabs):
            v = row(cots, k, j) + inverses[j] * (gs[k] - total - hats[k] * cross)
            cots[k, pl.ds(j, SEG, stride=STEP), :] = v
        return totals

    backward_some(0)
    start_part(0)
    backward_some(1)
    start_part(1)
    resume(0)
    backward_some(2)
    start_part(2)
    resume(0)
    slot_some(0, 2)
    resume(1)
    slot_some(2, 4)
    resume(0, 2)
    slot_some(4, 8)
    resume(0)
    feature_some(0, 2)
    resume(1)
    feature_some(2, 4)
    resume(2, 0)
    feature_some(4, 6)
    resume(1)
    totals = tuple(jnp.zeros((SEG, LANES), f32) for _ in range(slabs))
    totals = lax.fori_loop(0, STEP // 2, first_norm, totals)
    resume(2, 0)
    totals = lax.fori_loop(STEP // 2, STEP, first_norm, totals)
    for k in range(slabs):
        small[pl.ds(k * small_rows + taps, 1), :] = jnp.sum(totals[k], axis=0, keepdims=True)
    resume(3, 1, 3, 2, 3, 0)
    for k in range(slabs):
        out_ref[:, pl.ds(k * LANES, LANES)] = cots[k].astype(out_ref.dtype)
    resume(3, 1, 2)
    while not all(over):
        resume(3, 0, 3, 1, 2)

    for layer in (0, 1):
        for zh in (0, 1):
            for p in range(PARTS):
                column = p * part_cols + (layer * 2 + zh) * LANES
                for source, which in ((finals, c), (other_finals, 1 - c)):
                    block = jnp.concatenate(
                        [wide(source[p, layer, zh * 4 + 2 * c + r]) for r in (0, 1)], axis=0
                    )
                    start = pl.multiple_of(which * features + column, LANES)
                    rows_ref[:, pl.ds(start, LANES)] = block.astype(rows_ref.dtype)
    for copy in pending:
        copy.wait_send()


def run_module(frames, cotangent, lengths, weight_slots, owner_rows, gain_in, gain_mid, taps):
    tokens, features = frames.shape
    cap, width = weight_slots.shape
    slots = owner_rows.shape[0]
    slabs = features // LANES
    count = taps.shape[0]
    bf, f32 = jnp.bfloat16, jnp.float32
    vmem = pl.BlockSpec(memory_space=pltpu.VMEM)
    slab = (slabs, STEP, SEG, LANES)
    plane = (STEP, SEG, LANES)
    block = (BLOCK, LANES)
    small = (SMALL, LANES)
    dma = pltpu.SemaphoreType.DMA
    return pl.pallas_call(
        module_kernel,
        out_shape=(
            jax.ShapeDtypeStruct((tokens, features), bf),
            jax.ShapeDtypeStruct((cap, width), bf),
            jax.ShapeDtypeStruct((2, NZ) + small, f32),
        ),
        in_specs=[pl.BlockSpec(memory_space=pltpu.SMEM)] + [vmem] * 7,
        out_specs=(vmem,) * 3,
        scratch_shapes=[
            pltpu.VMEM((slots // cap, cap, width), bf),
            pltpu.VMEM((slabs, tokens, LANES), f32),
            pltpu.VMEM((slabs, tokens, LANES), f32),
            pltpu.VMEM((tokens, features), bf),
            pltpu.VMEM((tokens, slots), bf),
            pltpu.VMEM((slots, tokens), bf),
            pltpu.VMEM((tokens, width), bf),
            pltpu.VMEM(plane, f32),
            pltpu.VMEM(plane, f32),
            pltpu.VMEM(slab, f32),
            pltpu.VMEM(slab, f32),
            pltpu.VMEM((slabs, STEP + count, SEG, LANES), f32),
            pltpu.VMEM(slab, f32),
            pltpu.VMEM(slab, f32),
            pltpu.VMEM((STEP + count, SEG, LANES), f32),
            pltpu.VMEM((slabs, count, SEG, LANES), f32),
            pltpu.VMEM(plane, f32),
            pltpu.VMEM(plane, f32),
            pltpu.VMEM(plane, f32),
            pltpu.VMEM((2,) + plane, f32),
            pltpu.VMEM((2 * NZ * SMALL, LANES), f32),
            pltpu.VMEM((2, NZ) + small, f32),
            pltpu.VMEM((slots, tokens), bf),
            pltpu.VMEM((PARTS, tokens, features // PARTS), bf),
            pltpu.VMEM((PARTS, NX, NY, NZ) + block, bf),
            pltpu.VMEM((LANES, slots), bf),
            pltpu.VMEM((2, 2, NY, NZ) + block, bf),
            pltpu.VMEM((2, 2, NX, NZ) + block, bf),
            pltpu.VMEM((4, 2, NX, NY) + block, bf),
            pltpu.VMEM((NX, NY) + block, bf),
            pltpu.VMEM((NY, NZ) + block, bf),
            pltpu.VMEM((NX, NZ) + block, bf),
            pltpu.VMEM((NY,) + block, bf),
            pltpu.VMEM((NZ,) + block, bf),
            pltpu.VMEM((NZ,) + block, bf),
            pltpu.VMEM((NZ,) + small, f32),
            pltpu.VMEM((NZ,) + small, f32),
            pltpu.VMEM((NZ,) + small, f32),
            pltpu.VMEM((NX,) + small, f32),
            pltpu.VMEM((NY,) + small, f32),
            pltpu.VMEM((PARTS, 2, NZ) + block, bf),
            pltpu.VMEM((PARTS, 2, NZ) + block, bf),
            dma,
            dma((53, PIECES)),
            dma((53, PIECES)),
            dma((1 + PARTS,)),
            dma((1 + PARTS,)),
            dma((PARTS, 4, 2)),
            dma((PARTS, 4, 2)),
            dma((PARTS, 2, NZ)),
            dma((PARTS, 2, NZ)),
            dma((24,)),
            dma((24,)),
            dma((PARTS, NZ)),
            dma((PARTS, NZ)),
            dma((PARTS, 2, 2)),
            dma((PARTS, 2, 2)),
        ],
        compiler_params=pltpu.CompilerParams(
            collective_id=0, has_side_effects=True, vmem_limit_bytes=63 << 20
        ),
        name="conv_module",
    )(lengths, frames, cotangent, weight_slots, owner_rows[None], gain_in[None], gain_mid[None], taps)


def per_device(frames, cotangent, lengths, weight_slots, owner_rows, gain_in, gain_mid, kernel):
    utterances, length, features = frames.shape
    taps = kernel.shape[0]
    slabs = features // LANES
    frame_grads, weight_grads, total = run_module(
        frames.reshape(length, features), cotangent.reshape(length, features), lengths, weight_slots,
        owner_rows, gain_in, gain_mid, kernel,
    )
    small_rows = 2 * NZ * SMALL
    each = small_rows // slabs // SEG * SEG
    total = total.transpose(1, 0, 2, 3).reshape(small_rows, LANES)[: slabs * each]
    total = total.reshape(slabs, each, LANES).transpose(1, 0, 2).reshape(each, features)
    return (frame_grads[None], weight_grads, total[taps], total[taps + 1], total[:taps])


def solution(mesh):
    in_specs = (
        P(("dp", "fsdp"), None, None),
        P(("dp", "fsdp"), None, None),
        P(("dp", "fsdp")),
        P("fsdp", None),
        P(),
        P(),
        P(),
        P(),
    )
    out_specs = (P(("dp", "fsdp"), None, None), P("fsdp", None), P(), P(), P())
    return jax.shard_map(
        per_device, mesh=mesh, in_specs=in_specs, out_specs=out_specs, check_vma=False
    )
```

```python
import functools
import jax
import jax.numpy as jnp
from jax import lax
from jax.experimental import pallas as pl
from jax.experimental.pallas import tpu as pltpu
from jax.sharding import PartitionSpec as P

MESH = pl.DeviceIdType.MESH
NX, NY, NZ = 4, 4, 8
PIECES = 3
PARTS = 3
BLOCK = 72
LANES = 128
SMALL = 32
EPSILON = 1e-05
STEP = 32
SEG = 8
WIDE = 256
PART_AXES = ("zxy", "xyz", "yxz")


def place():
    d = lax.axis_index("dp")
    f = lax.axis_index("fsdp")
    return f // 4, (f // 2) % 2, d // NZ, d % NZ, f % 2


def device(x, yh, yl, z, c):
    return (yl * NZ + z, (x * 2 + yh) * 2 + c)


def wide(value):
    return value.astype(jnp.float32)


def split_index(i, lead):
    index = []
    for size in reversed(lead):
        index.append(i % size)
        i = i // size
    return tuple(reversed(index))


def add_into(dst, sources, lead):
    total = 1
    for size in lead:
        total *= size

    def one(i, carry):
        index = split_index(i, lead)
        value = wide(dst[index])
        for src in sources:
            value = value + wide(src[index])
        dst[index] = value.astype(dst.dtype)
        return carry

    if total == 1:
        one(0, 0)
    else:
        lax.fori_loop(0, total, one, 0)


def contract_last(a, b):
    return lax.dot_general(a, b, (((1,), (1,)), ((), ())), preferred_element_type=jnp.float32)


def over_lanes(value, count):
    return jnp.sum(value, axis=-1, keepdims=True) * (1.0 / count)


def extend(ext, value, taps):
    before = taps // 2
    seg = lax.broadcasted_iota(jnp.int32, (before, SEG, LANES), 1)
    ext[pl.ds(before, STEP)] = value
    late = pltpu.roll(value[STEP - before :], 1, 1)
    ext[pl.ds(0, before)] = jnp.where(seg == 0, 0.0, late)
    early = pltpu.roll(value[:before], SEG - 1, 1)
    ext[pl.ds(before + STEP, before)] = jnp.where(seg == SEG - 1, 0.0, early)


def module_kernel(
    length_ref, frames_hbm, cot_hbm, w_ref, owner_ref, gain_in_ref, gain_mid_ref, taps_ref,
    out_ref, rows_ref, small_out, gin_out,
    frames_ref, cot_ref, gin, gin_sib, gin_z, gin_x, gin_y, load_sem, gin_send, gin_recv,
    weight, natural, cots, normed, in_slots, slots_t, grad, means, inverses, left, gate, held,
    conv, deriv, ext_d, taps_wide, keep, acc_a, acc_b, back, small, small_split,
    theirs_t, theirs_g, sums, low, near_x, near_y, near_z, mid_0, mid_1, mid_2, far_0, far_1, far_2,
    small_sum, small_sib, small_z, small_x, small_y, finals, other_finals,
    keep_sem, w_send, w_recv, swap_send, swap_recv, send, recv, direct_send, direct_recv, small_send, small_recv,
    out_send, out_recv, sib_send, sib_recv,
):
    load_frames = pltpu.make_async_copy(frames_hbm, frames_ref, load_sem.at[0])
    load_cot = pltpu.make_async_copy(cot_hbm, cot_ref, load_sem.at[1])
    load_frames.start()
    load_cot.start()
    x, yh, yl, z, c = place()
    y = yh * 2 + yl
    f32 = jnp.float32
    features = frames_hbm.shape[1]
    slabs = features // LANES
    taps = taps_ref.shape[0]
    slots = owner_ref.shape[1]
    blocks = features // WIDE
    tokens = STEP * SEG
    cap, width = w_ref.shape
    part_cols = features // PARTS

    def at_x(i):
        return device(i % NX, yh, yl, z, c)

    def at_y(i):
        return device(x, (i % NY) // 2, i % 2, z, c)

    def at_z(i):
        return device(x, yh, yl, i % NZ, c)

    sib = device(x, yh, yl, z, 1 - c)
    to_ac = device(x, 1 - yh, 1 - yl, z, c)
    to_ys = device(x, yh, 1 - yl, z, c)
    pending = []

    def push(src, dst, send_sem, recv_sem, to):
        copy = pltpu.make_async_remote_copy(
            src_ref=src, dst_ref=dst, send_sem=send_sem, recv_sem=recv_sem,
            device_id=to, device_id_type=MESH,
        )
        copy.start()
        pending.append(copy)
        return copy

    def landed(ref, send_sem, recv_sem):
        pltpu.make_async_remote_copy(
            src_ref=ref, dst_ref=ref, send_sem=send_sem, recv_sem=recv_sem,
            device_id=sib, device_id_type=MESH,
        ).wait_recv()

    peers = (
        [sib]
        + [at_x(x + i) for i in range(1, NX)]
        + [at_y(y + i) for i in range(1, NY)]
        + [at_z(z + i) for i in range(1, NZ)]
    )
    barrier = pltpu.get_barrier_semaphore()
    for peer in peers:
        pl.semaphore_signal(barrier, inc=1, device_id=peer, device_id_type=MESH)
    pl.semaphore_wait(barrier, len(peers))

    xs = [x, (x + 3) % NX, (x + 1) % NX, (x + 2) % NX]
    to_xp, to_xm, to_zp, to_zm = at_x(x + 1), at_x(x + 3), at_z(z + 1), at_z(z + NZ - 1)
    span_x = width * 7 // 12
    span_y = span_x // 2
    rest_z = width - span_x
    span_z = rest_z // 2
    piece_rows = cap // PIECES
    par = z % 2
    base = par * rest_z

    def cols(start, size):
        return pl.ds(pl.multiple_of(start, LANES), size)

    window = cols(base, span_x)
    halves = [cols(base, span_y), cols(base + span_y, span_y)]
    mine = cols(base + yl * span_y, span_y)
    other = cols(base + (1 - yl) * span_y, span_y)
    shared = [cols(par * span_x, span_z), cols(par * span_x + span_z, span_z)]
    theirs = [cols((1 - par) * span_x, span_z), cols((1 - par) * span_x + span_z, span_z)]

    def owner(k, other_row):
        return (xs[k] * 2 + (1 - yh if other_row else yh)) * 2 + c

    def piece(ref, q, span):
        return ref.at[pl.ds(q * piece_rows, piece_rows), span]

    def w_push(index, q, src, dst, to):
        push(src, dst, w_send.at[index, q], w_recv.at[index, q], to)

    def pass_on(index, q, who, span, to):
        ref = piece(weight.at[who], q, span)
        w_push(index, q, ref, ref, to)

    def arrive(index, q, who, span):
        landed(piece(weight.at[who], q, span), w_send.at[index, q], w_recv.at[index, q])

    me = owner(0, False)
    x_copies = [
        [
            pltpu.make_async_remote_copy(
                src_ref=piece(w_ref, q, window), dst_ref=piece(weight.at[me], q, window),
                send_sem=w_send.at[index, q], recv_sem=w_recv.at[index, q],
                device_id=to, device_id_type=MESH,
            )
            for index, to in ((1, to_xp), (2, to_xm))
        ]
        for q in range(PIECES)
    ]

    def x_next(q):
        for copy in x_copies[q - 1]:
            copy.wait_send()
        for copy in x_copies[q]:
            copy.start()

    for copy in x_copies[0]:
        copy.start()
    pending.extend(x_copies[-1])
    for q in range(PIECES):
        w_push(3, q, piece(w_ref, q, mine), piece(weight.at[me], q, mine), to_ac)
    w_push(0, 0, w_ref, weight.at[me], sib)
    own_copy = pltpu.make_async_copy(w_ref, weight.at[me], keep_sem)
    own_copy.start()

    def z_out(slot, q, who):
        pass_on(13 + slot, q, who, shared[0], to_zp)
        pass_on(20 + slot, q, who, shared[1], to_zm)

    units = [(1, False), (2, False), (3, False), (0, True), (1, True), (2, True), (3, True)]

    def x_near(k, q):
        arrive(k, q, owner(k, False), window)
        pass_on(6 + k, q, owner(k, False), halves[k - 1], (to_xp, to_xm)[k - 1])
        pass_on(3 + k, q, owner(k, False), mine, to_ac)
        z_out(k - 1, q, owner(k, False))
        pass_on(26 + k, q, owner(k, False), window, sib)

    def x_far(q):
        arrive(7, q, owner(3, False), halves[0])
        arrive(8, q, owner(3, False), halves[1])
        pass_on(6, q, owner(3, False), mine, to_ac)
        z_out(2, q, owner(3, False))
        pass_on(29, q, owner(3, False), halves[0], sib)
        pass_on(30, q, owner(3, False), halves[1], sib)

    def across(k, q):
        arrive(3 + k, q, owner(k, True), other)
        pass_on(9 + k, q, owner(k, True), other, to_ys)
        pass_on(31 + k, q, owner(k, True), other, sib)

    def beside(k, q):
        arrive(9 + k, q, owner(k, True), mine)
        z_out(3 + k, q, owner(k, True))
        pass_on(35 + k, q, owner(k, True), mine, sib)

    def z_in(slot, q):
        who = owner(*units[slot])
        arrive(13 + slot, q, who, theirs[0])
        pass_on(39 + slot, q, who, theirs[0], sib)
        arrive(20 + slot, q, who, theirs[1])
        pass_on(46 + slot, q, who, theirs[1], sib)

    def flip(who):
        return who + 1 - 2 * c

    def from_sibling():
        landed(weight.at[flip(me)], w_send.at[0, 0], w_recv.at[0, 0])
        for q in range(PIECES):
            arrive(27, q, flip(owner(1, False)), window)
            arrive(28, q, flip(owner(2, False)), window)
            arrive(29, q, flip(owner(3, False)), halves[0])
            arrive(30, q, flip(owner(3, False)), halves[1])
            for k in range(4):
                arrive(31 + k, q, flip(owner(k, True)), other)
                arrive(35 + k, q, flip(owner(k, True)), mine)
            for slot in range(7):
                arrive(39 + slot, q, flip(owner(*units[slot])), theirs[0])
                arrive(46 + slot, q, flip(owner(*units[slot])), theirs[1])
        own_copy.wait()

    def row(ref, k, j):
        return ref[k, pl.ds(j, SEG, stride=STEP), :]

    def gain(ref, k):
        return ref[:, pl.ds(k * LANES, LANES)]

    def prepare():
        load_frames.wait()
        for k in range(slabs):
            lanes = pl.ds(k * LANES, LANES)
            natural[k] = wide(frames_ref[:, lanes])
            taps_wide[k] = jnp.broadcast_to(taps_ref[:, lanes][:, None, :], (taps, SEG, LANES))
        step_of = lax.broadcasted_iota(jnp.int32, (STEP, SEG, LANES), 0)
        seg_of = lax.broadcasted_iota(jnp.int32, (STEP, SEG, LANES), 1)
        keep[...] = (seg_of * STEP + step_of < length_ref[0]).astype(f32)

    def prepare_cots():
        load_cot.wait()
        for k in range(slabs):
            cots[k] = wide(cot_ref[:, pl.ds(k * LANES, LANES)])
        small[...] = jnp.zeros_like(small)

    def norm_pair(i, carry):
        parts = []
        for j in (2 * i, 2 * i + 1):
            values = [row(natural, k, j) for k in range(slabs)]
            total = values[0]
            for v in values[1:]:
                total = total + v
            mean = over_lanes(total, features)
            values = [v - mean for v in values]
            total = values[0] * values[0]
            for v in values[1:]:
                total = total + v * v
            inverse = lax.rsqrt(over_lanes(total, features) + EPSILON)
            means[j] = jnp.broadcast_to(mean, (SEG, LANES))
            inverses[j] = jnp.broadcast_to(inverse, (SEG, LANES))
            parts.append([v * inverse * gain(gain_in_ref, k) for k, v in enumerate(values)])
        for k in range(slabs):
            pair = jnp.concatenate([parts[0][k], parts[1][k]], axis=0)
            normed[pl.ds(pl.multiple_of(i * 16, 16), 16), pl.ds(k * LANES, LANES)] = pair.astype(normed.dtype)
        return carry

    def norm_some(i):
        lax.fori_loop(4 * i, 4 * i + 4, norm_pair, 0)

    def slab_mask(owned, k):
        return jnp.where((owned >= k * LANES) & (owned < (k + 1) * LANES), 1.0, 0.0).astype(normed.dtype)

    def choose(i):
        span = pl.ds(i * WIDE, WIDE)
        rows = lax.broadcasted_iota(jnp.int32, (LANES, WIDE), 0)
        owned = owner_ref[:, span]
        line = jnp.where(rows == owned % LANES, 1.0, 0.0).astype(normed.dtype)
        low[:, span] = line
        picked = jnp.concatenate([line * slab_mask(owned, k) for k in range(slabs)], axis=0)
        moved = jnp.dot(normed[...], picked, preferred_element_type=f32)
        in_slots[:, span] = moved.astype(in_slots.dtype)
        slots_t[span, :] = jnp.transpose(moved).astype(slots_t.dtype)

    slots_copy = pltpu.make_async_remote_copy(
        src_ref=slots_t, dst_ref=theirs_t, send_sem=swap_send.at[0], recv_sem=swap_recv.at[0],
        device_id=sib, device_id_type=MESH,
    )

    def swap_slots():
        slots_copy.start()

    part = functools.partial
    fill = [part(norm_some, i) for i in range(STEP // 8)]
    fill += [part(choose, i) for i in range(slots // WIDE)] + [swap_slots, prepare_cots]
    steps = []
    for q in range(PIECES):
        if q + 1 < PIECES:
            steps += [part(x_next, q + 1)]
        steps += [part(x_near, 1, q), part(x_near, 2, q)]
        if q == 0:
            steps += [part(across, 0, r) for r in range(PIECES)]
        else:
            steps += [part(x_far, q - 1), part(across, 1, q - 1), part(across, 2, q - 1)]
        if q == 1:
            steps += [part(beside, 0, r) for r in range(PIECES)]
        if q > 1:
            steps += [part(across, 3, q - 2), part(beside, 1, q - 2), part(beside, 2, q - 2)]
    last = PIECES - 1
    steps += [part(x_far, last), part(across, 1, last), part(across, 2, last)]
    for q in range(last - 1, PIECES):
        steps += [part(across, 3, q), part(beside, 1, q), part(beside, 2, q)]
    for q in range(PIECES):
        steps += [part(beside, 3, q)]
    steps += [part(z_in, slot, q) for slot in (0, 1, 3, 2, 4, 5, 6) for q in range(PIECES)]

    prepare()
    for task in fill[:2]:
        task()
    fill = fill[2:]
    for step in steps:
        step()
        if fill:
            fill.pop(0)()
    for task in fill:
        task()
    from_sibling()

    acc_a[...] = jnp.zeros_like(acc_a)

    def tap_rows(ext, k, sign, put):
        def one(b, carry):
            start = b * SEG
            first = start if sign > 0 else start + 1
            lines = [ext[first + i] for i in range(taps + SEG - 1)]
            totals = [None] * SEG
            for t in range(taps):
                w = taps_wide[k, t if sign > 0 else taps - 1 - t]
                for i in range(SEG):
                    term = w * lines[i + t]
                    totals[i] = term if totals[i] is None else totals[i] + term
            for i in range(SEG):
                put(start + i, totals[i])
            return carry

        lax.fori_loop(0, STEP // SEG, one, 0)

    def weight_cols(start):
        return weight[:, :, pl.ds(pl.multiple_of(start, WIDE), WIDE)].reshape(slots, WIDE)

    def forward(i, carry):
        value = jnp.dot(in_slots[...], weight_cols(i * WIDE), preferred_element_type=f32)
        opened = jnp.dot(in_slots[...], weight_cols(features + i * WIDE), preferred_element_type=f32)
        opened = jax.nn.sigmoid(opened)
        for h in range(WIDE // LANES):
            k = i * (WIDE // LANES) + h
            a = value[:, h * LANES : (h + 1) * LANES].reshape(STEP, SEG, LANES)
            s = opened[:, h * LANES : (h + 1) * LANES].reshape(STEP, SEG, LANES)
            left[k] = a
            gate[k] = s
            extend(held.at[k], a * s * keep[...], taps)

            def put(j, v, k=k):
                conv[k, j] = v
                acc_a[j] = acc_a[j] + v

            tap_rows(held.at[k], k, 1, put)
        return carry

    lax.fori_loop(0, blocks, forward, 0)

    acc_b[...] = jnp.zeros_like(acc_b)
    back[0] = jnp.broadcast_to(over_lanes(acc_a[...], features), (STEP, SEG, LANES))

    def centre(k, carry):
        v = conv[k] - back[0]
        conv[k] = v
        acc_b[...] += v * v
        return carry

    lax.fori_loop(0, slabs, centre, 0)
    back[1] = jnp.broadcast_to(lax.rsqrt(over_lanes(acc_b[...], features) + EPSILON), (STEP, SEG, LANES))
    acc_a[...] = jnp.zeros_like(acc_a)
    acc_b[...] = jnp.zeros_like(acc_b)

    def order_cot(j, carry):
        for k in range(slabs):
            deriv[k, j] = row(cots, k, j)
        return carry

    lax.fori_loop(0, STEP, order_cot, 0)
    small_rows = small.shape[0] // slabs // SEG * SEG

    def small_row(k, r):
        return pl.ds(pl.multiple_of(k * small_rows, SEG) + r, 1)

    def middle(k, carry):
        g = gain_mid_ref[:, pl.ds(pl.multiple_of(k * LANES, LANES), LANES)]
        hat = conv[k] * back[1]
        mixed = hat * g
        s = jax.nn.sigmoid(mixed)
        d = deriv[k] * keep[...] * (s * (1.0 + mixed * (1.0 - s)))
        dh = d * hat
        small[small_row(k, taps + 1), :] = jnp.sum(jnp.sum(dh, axis=0), axis=0, keepdims=True)
        conv[k] = hat
        d = d * g
        deriv[k] = d
        acc_a[...] += d
        acc_b[...] += dh * g
        return carry

    lax.fori_loop(0, slabs, middle, 0)
    acc_a[...] = jnp.broadcast_to(over_lanes(acc_a[...], features), (STEP, SEG, LANES))
    acc_b[...] = jnp.broadcast_to(over_lanes(acc_b[...], features), (STEP, SEG, LANES))

    def backward(k, carry):
        extend(ext_d, back[1] * (deriv[k] - acc_a[...] - conv[k] * acc_b[...]), taps)

        def put(j, v):
            deriv[k, j] = v * keep[j]

        tap_rows(ext_d, k, -1, put)
        half = taps // 2
        for t0 in (0, half):
            def one(b, totals):
                start = b * SEG
                ds = [ext_d[half + start + i] for i in range(SEG)]
                lines = [held[k, start + t0 + i] for i in range(half + SEG - 1)]
                return tuple(
                    functools.reduce(lambda p, q: p + q, [ds[i] * lines[i + t] for i in range(SEG)], totals[t])
                    for t in range(half)
                )

            totals = lax.fori_loop(0, STEP // SEG, one, tuple(jnp.zeros((SEG, LANES), f32) for _ in range(half)))
            for t in range(half):
                small[small_row(k, t0 + t), :] = jnp.sum(totals[t], axis=0, keepdims=True)
        d = deriv[k] * gate[k]
        lanes = pl.ds(pl.multiple_of(k * LANES, LANES), LANES)
        lanes_b = pl.ds(pl.multiple_of(features + k * LANES, LANES), LANES)
        grad[:, lanes] = d.reshape(tokens, LANES).astype(grad.dtype)
        db = d * left[k] * (1.0 - gate[k])
        grad[:, lanes_b] = db.reshape(tokens, LANES).astype(grad.dtype)
        return carry

    owner_rows = slots // (NX * 2)

    def half_cols(index, p):
        return pl.ds(pl.multiple_of(index * features + p * part_cols, part_cols), part_cols)

    def swap_part(p):
        return push(grad.at[:, half_cols(1 - c, p)], theirs_g.at[p], swap_send.at[1 + p], swap_recv.at[1 + p], sib)

    def make_terms(p):
        def one(ox, carry):
            rows = pl.ds(pl.multiple_of(ox * 2 * owner_rows, 64), 2 * owner_rows)
            term = jnp.dot(slots_t[rows, :], grad[:, half_cols(c, p)], preferred_element_type=f32)
            term = term + jnp.dot(theirs_t[rows, :], theirs_g[p], preferred_element_type=f32)
            for oy in range(2):
                for q in range(4):
                    for t in range(4):
                        first = (oy * 4 + q) * BLOCK
                        sums[p, ox, oy * 2 + t // 2, (t % 2) * 4 + q] = term[
                            first : first + BLOCK, t * LANES : (t + 1) * LANES
                        ].astype(sums.dtype)
            return carry

        lax.fori_loop(0, NX, one, 0)

    place_of = {"x": (x, NX, at_x), "y": (y, NY, at_y), "z": (z, NZ, at_z)}
    nears = {"x": near_x, "y": near_y, "z": near_z}
    direct_landing = ((mid_0, far_0), (mid_1, far_1), (mid_2, far_2))

    def part_flow(p):
        first, second, third_axis = PART_AXES[p]
        fixed = {}

        def chunk(axis, i, cut=None, half=None):
            index = []
            for a in ("x", "y", "z"):
                if a in fixed:
                    index.append(fixed[a])
                elif a == axis:
                    index.append(i % place_of[a][1])
                elif a == cut:
                    size = place_of[a][1] // 2
                    index.append(pl.ds(half * size, size))
                else:
                    index.append(slice(None))
            return sums.at[(p,) + tuple(index)]

        at, n, dev = place_of[first]
        rest = [a for a in ("x", "y", "z") if a != first]
        lead = tuple(place_of[a][1] for a in rest)
        half_size = lead[0] // 2
        hops = n // 2
        for step in range(hops):
            k = hops - step
            split = step == 0
            lines = []
            for w in (0, 1):
                sign = 1 if w == 0 else -1
                ref = nears[first].at[step, w]
                cut = (rest[0], w) if split else (None, None)
                if split:
                    ref = ref.at[pl.ds(w * half_size, half_size)]
                lines.append((sign, ref, cut, (send.at[p, step, w], recv.at[p, step, w])))
            for sign, ref, cut, sems in lines:
                push(chunk(first, at + n + sign * k, *cut), ref, *sems, dev(at + n + sign))
            yield
            for sign, ref, cut, sems in lines:
                landed(ref, *sems)
            if step < hops - 1:
                shape = (half_size,) + lead[1:] if split else lead
                for sign, ref, cut, sems in lines:
                    add_into(chunk(first, at + n + sign * (k - 1), *cut), [ref], shape)
            else:
                add_into(chunk(first, at), [ref for _, ref, _, _ in lines], lead)
        fixed[first] = at

        for stage, axis in enumerate((second, third_axis)):
            at, n, dev = place_of[axis]
            buffers = direct_landing[p][stage]
            for i in range(1, n):
                push(
                    chunk(axis, at + i), buffers.at[at],
                    direct_send.at[p, stage, i], direct_recv.at[p, stage, i], dev(at + i),
                )
            yield
            sources = [buffers.at[(at + n - i) % n] for i in range(1, n)]
            for i, ref in enumerate(sources):
                landed(ref, direct_send.at[p, stage, i + 1], direct_recv.at[p, stage, i + 1])
            add_into(chunk(axis, at), sources, (place_of[third_axis][1],) if stage == 0 else ())
            fixed[axis] = at

        finals[p, yl, z] = sums[p, x, y, z]
        for i in range(1, NZ):
            push(finals.at[p, yl, z], finals.at[p, yl, z], out_send.at[p, i], out_recv.at[p, i], at_z(z + i))
        yield
        for i in range(1, NZ):
            landed(finals.at[p, yl, (z + NZ - i) % NZ], out_send.at[p, i], out_recv.at[p, i])
        push(finals.at[p, yl], finals.at[p, yl], out_send.at[p, 0], out_recv.at[p, 0], to_ys)

        def pairs(layer, core, store):
            return [store.at[p, layer, pl.ds(zh * 4 + 2 * core, 2)] for zh in (0, 1)]

        def to_sibling(j, layer):
            for zh, (src, dst) in enumerate(zip(pairs(layer, 1 - c, finals), pairs(layer, 1 - c, other_finals))):
                push(src, dst, sib_send.at[p, j, zh], sib_recv.at[p, j, zh], sib)

        to_sibling(0, yl)
        yield
        landed(finals.at[p, 1 - yl], out_send.at[p, 0], out_recv.at[p, 0])
        to_sibling(1, 1 - yl)
        yield
        for j, layer in ((0, yl), (1, 1 - yl)):
            for zh, ref in enumerate(pairs(layer, c, other_finals)):
                landed(ref, sib_send.at[p, j, zh], sib_recv.at[p, j, zh])

    def small_flow():
        def spread(source, held_in, at, n, dev, first):
            for i in range(1, n):
                push(
                    source((at + i) % n), held_in.at[at],
                    small_send.at[first + i], small_recv.at[first + i], dev(at + i),
                )

        def collect(held_in, at, n, first):
            for i in range(1, n):
                landed(held_in.at[(at + n - i) % n], small_send.at[first + i], small_recv.at[first + i])

        def total_of(held_in, n):
            total = held_in[0]
            for i in range(1, n):
                total = total + held_in[i]
            return total

        for half in (0, 1):
            for k in range(NZ):
                small_split[half, k] = small[pl.ds((k * 2 + half) * SMALL, SMALL), :]
        push(small_split.at[1 - c], small_sib, small_send.at[8], small_recv.at[8], sib)
        yield
        landed(small_sib, small_send.at[8], small_recv.at[8])
        small_sum[...] = small_split[c] + small_sib[...]
        small_z[z] = small_sum[z]
        spread(lambda i: small_sum.at[i], small_z, z, NZ, at_z, 0)
        yield
        collect(small_z, z, NZ, 0)
        small_x[x] = total_of(small_z, NZ)
        spread(lambda i: small_x.at[x], small_x, x, NX, at_x, 8)
        yield
        collect(small_x, x, NX, 8)
        small_y[y] = total_of(small_x, NX)
        spread(lambda i: small_y.at[y], small_y, y, NY, at_y, 12)
        yield
        collect(small_y, y, NY, 12)
        small_out[c, z] = total_of(small_y, NY)
        spread(lambda i: small_out.at[c, z], small_out.at[c], z, NZ, at_z, 16)
        yield
        collect(small_out.at[c], z, NZ, 16)
        push(small_out.at[c], small_out.at[c], small_send.at[0], small_recv.at[0], sib)
        yield
        landed(small_out.at[1 - c], small_send.at[0], small_recv.at[0])

    def gain_in_flow():
        push(gin, gin_sib, gin_send.at[0, 0], gin_recv.at[0, 0], sib)
        yield
        landed(gin_sib, gin_send.at[0, 0], gin_recv.at[0, 0])
        total = gin[...] + gin_sib[...]
        for stage, (axis, store) in enumerate((("z", gin_z), ("x", gin_x), ("y", gin_y)), 1):
            at, n, dev = place_of[axis]
            store[at] = total
            for i in range(1, n):
                push(store.at[at], store.at[at], gin_send.at[stage, i], gin_recv.at[stage, i], dev(at + i))
            yield
            for i in range(1, n):
                landed(store.at[(at + n - i) % n], gin_send.at[stage, i], gin_recv.at[stage, i])
            total = store[0]
            for i in range(1, n):
                total = total + store[i]
        gin_out[...] = total

    flows = [part_flow(p) for p in range(PARTS)] + [small_flow(), gain_in_flow()]
    over = [False] * len(flows)

    def resume(*which):
        for i in which:
            if not over[i]:
                try:
                    next(flows[i])
                except StopIteration:
                    over[i] = True

    part_slabs = slabs // PARTS

    def backward_some(p):
        lax.fori_loop(p * part_slabs, (p + 1) * part_slabs, backward, 0)

    def start_part(p):
        swap = swap_part(p)
        if p == 0:
            slots_copy.wait()
        swap.wait_recv()
        make_terms(p)
        resume(p)

    def slot_grads(i, carry):
        rows = weight[pl.ds(i * 2, 2)].reshape(2 * cap, width)
        g = contract_last(rows, grad[...])
        slots_t[pl.ds(pl.multiple_of(i * 2 * cap, 32), 2 * cap), :] = g.astype(slots_t.dtype)
        return carry

    def slot_some(lo, hi):
        lax.fori_loop(lo, hi, slot_grads, 0)

    def feature_grads(i, carry):
        owned = owner_ref[...]
        picked = jnp.concatenate([low[...] * slab_mask(owned, 2 * i + h) for h in (0, 1)], axis=0)
        g = jnp.transpose(jnp.dot(picked, slots_t[...], preferred_element_type=f32))
        for h in range(WIDE // LANES):
            deriv[i * (WIDE // LANES) + h] = g[:, h * LANES : (h + 1) * LANES].reshape(STEP, SEG, LANES)
        return carry

    def feature_some(lo, hi):
        lax.fori_loop(lo, hi, feature_grads, 0)

    def first_norm(j, totals):
        hats = [(row(natural, k, j) - means[j]) * inverses[j] for k in range(slabs)]
        gs = [deriv[k, j] for k in range(slabs)]
        totals = tuple(s + g * h for s, g, h in zip(totals, gs, hats))
        gs = [g * gain(gain_in_ref, k) for k, g in enumerate(gs)]
        total, cross = gs[0], gs[0] * hats[0]
        for g, h in zip(gs[1:], hats[1:]):
            total, cross = total + g, cross + g * h
        total, cross = over_lanes(total, features), over_lanes(cross, features)
        for k in range(slabs):
            v = row(cots, k, j) + inverses[j] * (gs[k] - total - hats[k] * cross)
            cots[k, pl.ds(j, SEG, stride=STEP), :] = v
        return totals

    gin[...] = jnp.zeros_like(gin)
    backward_some(0)
    start_part(0)
    backward_some(1)
    start_part(1)
    resume(0)
    backward_some(2)
    start_part(2)
    resume(0, 3)
    slot_some(0, 3)
    resume(1, 3)
    slot_some(3, 6)
    resume(0, 2, 3)
    slot_some(6, 8)
    feature_some(0, 1)
    resume(0, 3)
    feature_some(1, 3)
    resume(1)
    feature_some(3, 5)
    resume(2, 0, 3)
    feature_some(5, 6)
    totals = tuple(jnp.zeros((SEG, LANES), f32) for _ in range(slabs))
    totals = lax.fori_loop(0, STEP // 2, first_norm, totals)
    resume(1, 3)
    totals = lax.fori_loop(STEP // 2, STEP, first_norm, totals)
    for k in range(slabs):
        gin[pl.ds(k, 1), :] = jnp.sum(totals[k], axis=0, keepdims=True)
    resume(4, 2, 0, 4, 1, 2, 4)
    for k in range(slabs):
        out_ref[:, pl.ds(k * LANES, LANES)] = cots[k].astype(out_ref.dtype)
    resume(0, 4, 3)
    while not all(over):
        resume(1, 2, 4, 0, 3)

    for layer in (0, 1):
        for zh in (0, 1):
            for p in range(PARTS):
                column = p * part_cols + (layer * 2 + zh) * LANES
                for source, which in ((finals, c), (other_finals, 1 - c)):
                    block = jnp.concatenate(
                        [wide(source[p, layer, zh * 4 + 2 * c + r]) for r in (0, 1)], axis=0
                    )
                    start = pl.multiple_of(which * features + column, LANES)
                    rows_ref[:, pl.ds(start, LANES)] = block.astype(rows_ref.dtype)
    for copy in pending:
        copy.wait_send()


def run_module(frames, cotangent, lengths, weight_slots, owner_rows, gain_in, gain_mid, taps):
    tokens, features = frames.shape
    cap, width = weight_slots.shape
    slots = owner_rows.shape[0]
    slabs = features // LANES
    count = taps.shape[0]
    bf, f32 = jnp.bfloat16, jnp.float32
    vmem = pl.BlockSpec(memory_space=pltpu.VMEM)
    slab = (slabs, STEP, SEG, LANES)
    plane = (STEP, SEG, LANES)
    block = (BLOCK, LANES)
    small = (SMALL, LANES)
    gin = (pl.cdiv(slabs, SEG) * SEG, LANES)
    dma = pltpu.SemaphoreType.DMA
    return pl.pallas_call(
        module_kernel,
        out_shape=(
            jax.ShapeDtypeStruct((tokens, features), bf),
            jax.ShapeDtypeStruct((cap, width), bf),
            jax.ShapeDtypeStruct((2, NZ) + small, f32),
            jax.ShapeDtypeStruct(gin, f32),
        ),
        in_specs=[pl.BlockSpec(memory_space=pltpu.SMEM)] + [pl.BlockSpec(memory_space=pl.ANY)] * 3 + [vmem] * 4,
        out_specs=(vmem,) * 4,
        scratch_shapes=[
            pltpu.VMEM((tokens, features), bf),
            pltpu.VMEM((tokens, features), bf),
            pltpu.VMEM(gin, f32),
            pltpu.VMEM(gin, f32),
            pltpu.VMEM((NZ,) + gin, f32),
            pltpu.VMEM((NX,) + gin, f32),
            pltpu.VMEM((NY,) + gin, f32),
            dma((2,)),
            dma((4, NZ)),
            dma((4, NZ)),
            pltpu.VMEM((slots // cap, cap, width), bf),
            pltpu.VMEM((slabs, tokens, LANES), f32),
            pltpu.VMEM((slabs, tokens, LANES), f32),
            pltpu.VMEM((tokens, features), bf),
            pltpu.VMEM((tokens, slots), bf),
            pltpu.VMEM((slots, tokens), bf),
            pltpu.VMEM((tokens, width), bf),
            pltpu.VMEM(plane, f32),
            pltpu.VMEM(plane, f32),
            pltpu.VMEM(slab, f32),
            pltpu.VMEM(slab, f32),
            pltpu.VMEM((slabs, STEP + count, SEG, LANES), f32),
            pltpu.VMEM(slab, f32),
            pltpu.VMEM(slab, f32),
            pltpu.VMEM((STEP + count, SEG, LANES), f32),
            pltpu.VMEM((slabs, count, SEG, LANES), f32),
            pltpu.VMEM(plane, f32),
            pltpu.VMEM(plane, f32),
            pltpu.VMEM(plane, f32),
            pltpu.VMEM((2,) + plane, f32),
            pltpu.VMEM((2 * NZ * SMALL, LANES), f32),
            pltpu.VMEM((2, NZ) + small, f32),
            pltpu.VMEM((slots, tokens), bf),
            pltpu.VMEM((PARTS, tokens, features // PARTS), bf),
            pltpu.VMEM((PARTS, NX, NY, NZ) + block, bf),
            pltpu.VMEM((LANES, slots), bf),
            pltpu.VMEM((2, 2, NY, NZ) + block, bf),
            pltpu.VMEM((2, 2, NX, NZ) + block, bf),
            pltpu.VMEM((4, 2, NX, NY) + block, bf),
            pltpu.VMEM((NX, NY) + block, bf),
            pltpu.VMEM((NY, NZ) + block, bf),
            pltpu.VMEM((NX, NZ) + block, bf),
            pltpu.VMEM((NY,) + block, bf),
            pltpu.VMEM((NZ,) + block, bf),
            pltpu.VMEM((NZ,) + block, bf),
            pltpu.VMEM((NZ,) + small, f32),
            pltpu.VMEM((NZ,) + small, f32),
            pltpu.VMEM((NZ,) + small, f32),
            pltpu.VMEM((NX,) + small, f32),
            pltpu.VMEM((NY,) + small, f32),
            pltpu.VMEM((PARTS, 2, NZ) + block, bf),
            pltpu.VMEM((PARTS, 2, NZ) + block, bf),
            dma,
            dma((53, PIECES)),
            dma((53, PIECES)),
            dma((1 + PARTS,)),
            dma((1 + PARTS,)),
            dma((PARTS, 4, 2)),
            dma((PARTS, 4, 2)),
            dma((PARTS, 2, NZ)),
            dma((PARTS, 2, NZ)),
            dma((24,)),
            dma((24,)),
            dma((PARTS, NZ)),
            dma((PARTS, NZ)),
            dma((PARTS, 2, 2)),
            dma((PARTS, 2, 2)),
        ],
        compiler_params=pltpu.CompilerParams(
            collective_id=0, has_side_effects=True, vmem_limit_bytes=63 << 20
        ),
        name="conv_module",
    )(lengths, frames, cotangent, weight_slots, owner_rows[None], gain_in[None], gain_mid[None], taps)


def per_device(frames, cotangent, lengths, weight_slots, owner_rows, gain_in, gain_mid, kernel):
    utterances, length, features = frames.shape
    taps = kernel.shape[0]
    slabs = features // LANES
    frame_grads, weight_grads, total, gain_in_total = run_module(
        frames.reshape(length, features), cotangent.reshape(length, features), lengths, weight_slots,
        owner_rows, gain_in, gain_mid, kernel,
    )
    small_rows = 2 * NZ * SMALL
    each = small_rows // slabs // SEG * SEG
    total = total.transpose(1, 0, 2, 3).reshape(small_rows, LANES)[: slabs * each]
    total = total.reshape(slabs, each, LANES).transpose(1, 0, 2).reshape(each, features)
    gain_in_total = gain_in_total[:slabs].reshape(features)
    return (frame_grads[None], weight_grads, gain_in_total, total[taps + 1], total[:taps])


def solution(mesh):
    in_specs = (
        P(("dp", "fsdp"), None, None),
        P(("dp", "fsdp"), None, None),
        P(("dp", "fsdp")),
        P("fsdp", None),
        P(),
        P(),
        P(),
        P(),
    )
    out_specs = (P(("dp", "fsdp"), None, None), P("fsdp", None), P(), P(), P())
    return jax.shard_map(
        per_device, mesh=mesh, in_specs=in_specs, out_specs=out_specs, check_vma=False
    )
```

```python
import functools
import jax
import jax.numpy as jnp
from jax import lax
from jax.experimental import pallas as pl
from jax.experimental.pallas import tpu as pltpu
from jax.sharding import PartitionSpec as P

MESH = pl.DeviceIdType.MESH
NX, NY, NZ = 4, 4, 8
PIECES = 3
PARTS = 3
BLOCK = 72
LANES = 128
SMALL = 32
EPSILON = 1e-05
STEP = 32
SEG = 8
WIDE = 256
PART_AXES = ("zxy", "xyz", "yxz")


def place():
    d = lax.axis_index("dp")
    f = lax.axis_index("fsdp")
    return f // 4, (f // 2) % 2, d // NZ, d % NZ, f % 2


def device(x, yh, yl, z, c):
    return (yl * NZ + z, (x * 2 + yh) * 2 + c)


def wide(value):
    return value.astype(jnp.float32)


def split_index(i, lead):
    index = []
    for size in reversed(lead):
        index.append(i % size)
        i = i // size
    return tuple(reversed(index))


def add_into(dst, sources, lead):
    total = 1
    for size in lead:
        total *= size

    def one(i, carry):
        index = split_index(i, lead)
        value = wide(dst[index])
        for src in sources:
            value = value + wide(src[index])
        dst[index] = value.astype(dst.dtype)
        return carry

    if total == 1:
        one(0, 0)
    else:
        lax.fori_loop(0, total, one, 0)


def contract_last(a, b):
    return lax.dot_general(a, b, (((1,), (1,)), ((), ())), preferred_element_type=jnp.float32)


def over_lanes(value, count):
    return jnp.sum(value, axis=-1, keepdims=True) * (1.0 / count)


def extend(ext, value, taps):
    before = taps // 2
    seg = lax.broadcasted_iota(jnp.int32, (before, SEG, LANES), 1)
    ext[pl.ds(before, STEP)] = value
    late = pltpu.roll(value[STEP - before :], 1, 1)
    ext[pl.ds(0, before)] = jnp.where(seg == 0, 0.0, late)
    early = pltpu.roll(value[:before], SEG - 1, 1)
    ext[pl.ds(before + STEP, before)] = jnp.where(seg == SEG - 1, 0.0, early)


def module_kernel(
    length_ref, frames_hbm, cot_hbm, w_ref, owner_ref, gain_in_ref, gain_mid_ref, taps_ref,
    out_ref, rows_ref, taps_out, gains_out, gin_out,
    small_out, frames_ref, cot_ref, gin, gin_sib, gin_z, gin_x, gin_y, load_sem, gin_send, gin_recv,
    weight, natural, cots, normed, in_slots, slots_t, grad, means, inverses, left, gate, held,
    conv, deriv, ext_d, taps_wide, keep, acc_a, acc_b, back, small, small_split,
    theirs_t, theirs_g, sums, low, near_x, near_y, near_z, mid_0, mid_1, mid_2, far_0, far_1, far_2,
    small_sum, small_sib, small_z, small_x, small_y, finals, other_finals,
    keep_sem, w_send, w_recv, swap_send, swap_recv, send, recv, direct_send, direct_recv, small_send, small_recv,
    out_send, out_recv, sib_send, sib_recv,
):
    load_frames = pltpu.make_async_copy(frames_hbm, frames_ref, load_sem.at[0])
    load_cot = pltpu.make_async_copy(cot_hbm, cot_ref, load_sem.at[1])
    load_frames.start()
    load_cot.start()
    x, yh, yl, z, c = place()
    y = yh * 2 + yl
    f32 = jnp.float32
    features = frames_hbm.shape[1]
    slabs = features // LANES
    taps = taps_ref.shape[0]
    slots = owner_ref.shape[0]
    blocks = features // WIDE
    tokens = STEP * SEG
    cap, width = w_ref.shape
    part_cols = features // PARTS

    def at_x(i):
        return device(i % NX, yh, yl, z, c)

    def at_y(i):
        return device(x, (i % NY) // 2, i % 2, z, c)

    def at_z(i):
        return device(x, yh, yl, i % NZ, c)

    sib = device(x, yh, yl, z, 1 - c)
    to_ac = device(x, 1 - yh, 1 - yl, z, c)
    to_ys = device(x, yh, 1 - yl, z, c)
    pending = []

    def push(src, dst, send_sem, recv_sem, to):
        copy = pltpu.make_async_remote_copy(
            src_ref=src, dst_ref=dst, send_sem=send_sem, recv_sem=recv_sem,
            device_id=to, device_id_type=MESH,
        )
        copy.start()
        pending.append(copy)
        return copy

    def landed(ref, send_sem, recv_sem):
        pltpu.make_async_remote_copy(
            src_ref=ref, dst_ref=ref, send_sem=send_sem, recv_sem=recv_sem,
            device_id=sib, device_id_type=MESH,
        ).wait_recv()

    peers = (
        [sib]
        + [at_x(x + i) for i in range(1, NX)]
        + [at_y(y + i) for i in range(1, NY)]
        + [at_z(z + i) for i in range(1, NZ)]
    )
    barrier = pltpu.get_barrier_semaphore()
    for peer in peers:
        pl.semaphore_signal(barrier, inc=1, device_id=peer, device_id_type=MESH)
    pl.semaphore_wait(barrier, len(peers))

    xs = [x, (x + 3) % NX, (x + 1) % NX, (x + 2) % NX]
    to_xp, to_xm, to_zp, to_zm = at_x(x + 1), at_x(x + 3), at_z(z + 1), at_z(z + NZ - 1)
    span_x = width * 7 // 12
    span_y = span_x // 2
    rest_z = width - span_x
    span_z = rest_z // 2
    piece_rows = cap // PIECES
    par = z % 2
    base = par * rest_z

    def cols(start, size):
        return pl.ds(pl.multiple_of(start, LANES), size)

    window = cols(base, span_x)
    halves = [cols(base, span_y), cols(base + span_y, span_y)]
    mine = cols(base + yl * span_y, span_y)
    other = cols(base + (1 - yl) * span_y, span_y)
    shared = [cols(par * span_x, span_z), cols(par * span_x + span_z, span_z)]
    theirs = [cols((1 - par) * span_x, span_z), cols((1 - par) * span_x + span_z, span_z)]

    def owner(k, other_row):
        return (xs[k] * 2 + (1 - yh if other_row else yh)) * 2 + c

    def piece(ref, q, span):
        return ref.at[pl.ds(q * piece_rows, piece_rows), span]

    def w_push(index, q, src, dst, to):
        push(src, dst, w_send.at[index, q], w_recv.at[index, q], to)

    def pass_on(index, q, who, span, to):
        ref = piece(weight.at[who], q, span)
        w_push(index, q, ref, ref, to)

    def arrive(index, q, who, span):
        landed(piece(weight.at[who], q, span), w_send.at[index, q], w_recv.at[index, q])

    me = owner(0, False)
    x_copies = [
        [
            pltpu.make_async_remote_copy(
                src_ref=piece(w_ref, q, window), dst_ref=piece(weight.at[me], q, window),
                send_sem=w_send.at[index, q], recv_sem=w_recv.at[index, q],
                device_id=to, device_id_type=MESH,
            )
            for index, to in ((1, to_xp), (2, to_xm))
        ]
        for q in range(PIECES)
    ]

    def x_next(q):
        for copy in x_copies[q - 1]:
            copy.wait_send()
        for copy in x_copies[q]:
            copy.start()

    for copy in x_copies[0]:
        copy.start()
    pending.extend(x_copies[-1])
    for q in range(PIECES):
        w_push(3, q, piece(w_ref, q, mine), piece(weight.at[me], q, mine), to_ac)
    w_push(0, 0, w_ref, weight.at[me], sib)
    own_copy = pltpu.make_async_copy(w_ref, weight.at[me], keep_sem)
    own_copy.start()

    def z_out(slot, q, who):
        pass_on(13 + slot, q, who, shared[0], to_zp)
        pass_on(20 + slot, q, who, shared[1], to_zm)

    units = [(1, False), (2, False), (3, False), (0, True), (1, True), (2, True), (3, True)]

    def x_near(k, q):
        arrive(k, q, owner(k, False), window)
        pass_on(6 + k, q, owner(k, False), halves[k - 1], (to_xp, to_xm)[k - 1])
        pass_on(3 + k, q, owner(k, False), mine, to_ac)
        z_out(k - 1, q, owner(k, False))
        pass_on(26 + k, q, owner(k, False), window, sib)

    def x_far(q):
        arrive(7, q, owner(3, False), halves[0])
        arrive(8, q, owner(3, False), halves[1])
        pass_on(6, q, owner(3, False), mine, to_ac)
        z_out(2, q, owner(3, False))
        pass_on(29, q, owner(3, False), halves[0], sib)
        pass_on(30, q, owner(3, False), halves[1], sib)

    def across(k, q):
        arrive(3 + k, q, owner(k, True), other)
        pass_on(9 + k, q, owner(k, True), other, to_ys)
        pass_on(31 + k, q, owner(k, True), other, sib)

    def beside(k, q):
        arrive(9 + k, q, owner(k, True), mine)
        z_out(3 + k, q, owner(k, True))
        pass_on(35 + k, q, owner(k, True), mine, sib)

    def z_in(slot, q):
        who = owner(*units[slot])
        arrive(13 + slot, q, who, theirs[0])
        pass_on(39 + slot, q, who, theirs[0], sib)
        arrive(20 + slot, q, who, theirs[1])
        pass_on(46 + slot, q, who, theirs[1], sib)

    def flip(who):
        return who + 1 - 2 * c

    def from_sibling():
        landed(weight.at[flip(me)], w_send.at[0, 0], w_recv.at[0, 0])
        for q in range(PIECES):
            arrive(27, q, flip(owner(1, False)), window)
            arrive(28, q, flip(owner(2, False)), window)
            arrive(29, q, flip(owner(3, False)), halves[0])
            arrive(30, q, flip(owner(3, False)), halves[1])
            for k in range(4):
                arrive(31 + k, q, flip(owner(k, True)), other)
                arrive(35 + k, q, flip(owner(k, True)), mine)
            for slot in range(7):
                arrive(39 + slot, q, flip(owner(*units[slot])), theirs[0])
                arrive(46 + slot, q, flip(owner(*units[slot])), theirs[1])
        own_copy.wait()

    def row(ref, k, j):
        return ref[k, pl.ds(j, SEG, stride=STEP), :]

    def gain(ref, k):
        return ref[pl.ds(k * LANES, LANES)].reshape(1, LANES)

    def prepare():
        load_frames.wait()
        for k in range(slabs):
            lanes = pl.ds(k * LANES, LANES)
            natural[k] = wide(frames_ref[:, lanes])
            taps_wide[k] = jnp.broadcast_to(taps_ref[:, lanes][:, None, :], (taps, SEG, LANES))
        step_of = lax.broadcasted_iota(jnp.int32, (STEP, SEG, LANES), 0)
        seg_of = lax.broadcasted_iota(jnp.int32, (STEP, SEG, LANES), 1)
        keep[...] = (seg_of * STEP + step_of < length_ref[0]).astype(f32)

    def prepare_cots():
        load_cot.wait()
        for k in range(slabs):
            cots[k] = wide(cot_ref[:, pl.ds(k * LANES, LANES)])
        small[...] = jnp.zeros_like(small)

    def norm_pair(i, carry):
        parts = []
        for j in (2 * i, 2 * i + 1):
            values = [row(natural, k, j) for k in range(slabs)]
            total = values[0]
            for v in values[1:]:
                total = total + v
            mean = over_lanes(total, features)
            values = [v - mean for v in values]
            total = values[0] * values[0]
            for v in values[1:]:
                total = total + v * v
            inverse = lax.rsqrt(over_lanes(total, features) + EPSILON)
            means[j] = jnp.broadcast_to(mean, (SEG, LANES))
            inverses[j] = jnp.broadcast_to(inverse, (SEG, LANES))
            parts.append([v * inverse * gain(gain_in_ref, k) for k, v in enumerate(values)])
        for k in range(slabs):
            pair = jnp.concatenate([parts[0][k], parts[1][k]], axis=0)
            normed[pl.ds(pl.multiple_of(i * 16, 16), 16), pl.ds(k * LANES, LANES)] = pair.astype(normed.dtype)
        return carry

    def norm_some(i):
        lax.fori_loop(4 * i, 4 * i + 4, norm_pair, 0)

    def slab_mask(owned, k):
        return jnp.where((owned >= k * LANES) & (owned < (k + 1) * LANES), 1.0, 0.0).astype(normed.dtype)

    def choose(i):
        span = pl.ds(i * WIDE, WIDE)
        rows = lax.broadcasted_iota(jnp.int32, (LANES, WIDE), 0)
        owned = owner_ref[span].reshape(1, WIDE)
        line = jnp.where(rows == owned % LANES, 1.0, 0.0).astype(normed.dtype)
        low[:, span] = line
        picked = jnp.concatenate([line * slab_mask(owned, k) for k in range(slabs)], axis=0)
        moved = jnp.dot(normed[...], picked, preferred_element_type=f32)
        in_slots[:, span] = moved.astype(in_slots.dtype)
        slots_t[span, :] = jnp.transpose(moved).astype(slots_t.dtype)

    slots_copy = pltpu.make_async_remote_copy(
        src_ref=slots_t, dst_ref=theirs_t, send_sem=swap_send.at[0], recv_sem=swap_recv.at[0],
        device_id=sib, device_id_type=MESH,
    )

    def swap_slots():
        slots_copy.start()

    part = functools.partial
    fill = [part(norm_some, i) for i in range(STEP // 8)]
    fill += [part(choose, i) for i in range(slots // WIDE)] + [swap_slots, prepare_cots]
    steps = []
    for q in range(PIECES):
        if q + 1 < PIECES:
            steps += [part(x_next, q + 1)]
        steps += [part(x_near, 1, q), part(x_near, 2, q)]
        if q == 0:
            steps += [part(across, 0, r) for r in range(PIECES)]
        else:
            steps += [part(x_far, q - 1), part(across, 1, q - 1), part(across, 2, q - 1)]
        if q == 1:
            steps += [part(beside, 0, r) for r in range(PIECES)]
        if q > 1:
            steps += [part(across, 3, q - 2), part(beside, 1, q - 2), part(beside, 2, q - 2)]
    last = PIECES - 1
    steps += [part(x_far, last), part(across, 1, last), part(across, 2, last)]
    for q in range(last - 1, PIECES):
        steps += [part(across, 3, q), part(beside, 1, q), part(beside, 2, q)]
    for q in range(PIECES):
        steps += [part(beside, 3, q)]
    steps += [part(z_in, slot, q) for slot in (0, 1, 3, 2, 4, 5, 6) for q in range(PIECES)]

    prepare()
    for task in fill[:2]:
        task()
    fill = fill[2:]
    for step in steps:
        step()
        if fill:
            fill.pop(0)()
    for task in fill:
        task()
    from_sibling()

    acc_a[...] = jnp.zeros_like(acc_a)

    def tap_rows(ext, k, sign, put):
        def one(b, carry):
            start = b * SEG
            first = start if sign > 0 else start + 1
            lines = [ext[first + i] for i in range(taps + SEG - 1)]
            totals = [None] * SEG
            for t in range(taps):
                w = taps_wide[k, t if sign > 0 else taps - 1 - t]
                for i in range(SEG):
                    term = w * lines[i + t]
                    totals[i] = term if totals[i] is None else totals[i] + term
            for i in range(SEG):
                put(start + i, totals[i])
            return carry

        lax.fori_loop(0, STEP // SEG, one, 0)

    def weight_cols(start):
        return weight[:, :, pl.ds(pl.multiple_of(start, WIDE), WIDE)].reshape(slots, WIDE)

    def forward(i, carry):
        value = jnp.dot(in_slots[...], weight_cols(i * WIDE), preferred_element_type=f32)
        opened = jnp.dot(in_slots[...], weight_cols(features + i * WIDE), preferred_element_type=f32)
        opened = jax.nn.sigmoid(opened)
        for h in range(WIDE // LANES):
            k = i * (WIDE // LANES) + h
            a = value[:, h * LANES : (h + 1) * LANES].reshape(STEP, SEG, LANES)
            s = opened[:, h * LANES : (h + 1) * LANES].reshape(STEP, SEG, LANES)
            left[k] = a
            gate[k] = s
            extend(held.at[k], a * s * keep[...], taps)

            def put(j, v, k=k):
                conv[k, j] = v
                acc_a[j] = acc_a[j] + v

            tap_rows(held.at[k], k, 1, put)
        return carry

    lax.fori_loop(0, blocks, forward, 0)

    acc_b[...] = jnp.zeros_like(acc_b)
    back[0] = jnp.broadcast_to(over_lanes(acc_a[...], features), (STEP, SEG, LANES))

    def centre(k, carry):
        v = conv[k] - back[0]
        conv[k] = v
        acc_b[...] += v * v
        return carry

    lax.fori_loop(0, slabs, centre, 0)
    back[1] = jnp.broadcast_to(lax.rsqrt(over_lanes(acc_b[...], features) + EPSILON), (STEP, SEG, LANES))
    acc_a[...] = jnp.zeros_like(acc_a)
    acc_b[...] = jnp.zeros_like(acc_b)

    def order_cot(j, carry):
        for k in range(slabs):
            deriv[k, j] = row(cots, k, j)
        return carry

    lax.fori_loop(0, STEP, order_cot, 0)
    small_rows = small.shape[0] // slabs // SEG * SEG

    def small_row(k, r):
        return pl.ds(pl.multiple_of(k * small_rows, SEG) + r, 1)

    def middle(k, carry):
        g = gain_mid_ref[pl.ds(pl.multiple_of(k * LANES, LANES), LANES)].reshape(1, LANES)
        hat = conv[k] * back[1]
        mixed = hat * g
        s = jax.nn.sigmoid(mixed)
        d = deriv[k] * keep[...] * (s * (1.0 + mixed * (1.0 - s)))
        dh = d * hat
        small[small_row(k, taps + 1), :] = jnp.sum(jnp.sum(dh, axis=0), axis=0, keepdims=True)
        conv[k] = hat
        d = d * g
        deriv[k] = d
        acc_a[...] += d
        acc_b[...] += dh * g
        return carry

    lax.fori_loop(0, slabs, middle, 0)
    acc_a[...] = jnp.broadcast_to(over_lanes(acc_a[...], features), (STEP, SEG, LANES))
    acc_b[...] = jnp.broadcast_to(over_lanes(acc_b[...], features), (STEP, SEG, LANES))

    def backward(k, carry):
        extend(ext_d, back[1] * (deriv[k] - acc_a[...] - conv[k] * acc_b[...]), taps)

        def put(j, v):
            deriv[k, j] = v * keep[j]

        tap_rows(ext_d, k, -1, put)
        half = taps // 2
        for t0 in (0, half):
            def one(b, totals):
                start = b * SEG
                ds = [ext_d[half + start + i] for i in range(SEG)]
                lines = [held[k, start + t0 + i] for i in range(half + SEG - 1)]
                return tuple(
                    functools.reduce(lambda p, q: p + q, [ds[i] * lines[i + t] for i in range(SEG)], totals[t])
                    for t in range(half)
                )

            totals = lax.fori_loop(0, STEP // SEG, one, tuple(jnp.zeros((SEG, LANES), f32) for _ in range(half)))
            for t in range(half):
                small[small_row(k, t0 + t), :] = jnp.sum(totals[t], axis=0, keepdims=True)
        d = deriv[k] * gate[k]
        lanes = pl.ds(pl.multiple_of(k * LANES, LANES), LANES)
        lanes_b = pl.ds(pl.multiple_of(features + k * LANES, LANES), LANES)
        grad[:, lanes] = d.reshape(tokens, LANES).astype(grad.dtype)
        db = d * left[k] * (1.0 - gate[k])
        grad[:, lanes_b] = db.reshape(tokens, LANES).astype(grad.dtype)
        return carry

    owner_rows = slots // (NX * 2)

    def half_cols(index, p):
        return pl.ds(pl.multiple_of(index * features + p * part_cols, part_cols), part_cols)

    def swap_part(p):
        return push(grad.at[:, half_cols(1 - c, p)], theirs_g.at[p], swap_send.at[1 + p], swap_recv.at[1 + p], sib)

    def make_terms(p):
        def one(ox, carry):
            rows = pl.ds(pl.multiple_of(ox * 2 * owner_rows, 64), 2 * owner_rows)
            term = jnp.dot(slots_t[rows, :], grad[:, half_cols(c, p)], preferred_element_type=f32)
            term = term + jnp.dot(theirs_t[rows, :], theirs_g[p], preferred_element_type=f32)
            for oy in range(2):
                for q in range(4):
                    for t in range(4):
                        first = (oy * 4 + q) * BLOCK
                        sums[p, ox, oy * 2 + t // 2, (t % 2) * 4 + q] = term[
                            first : first + BLOCK, t * LANES : (t + 1) * LANES
                        ].astype(sums.dtype)
            return carry

        lax.fori_loop(0, NX, one, 0)

    place_of = {"x": (x, NX, at_x), "y": (y, NY, at_y), "z": (z, NZ, at_z)}
    nears = {"x": near_x, "y": near_y, "z": near_z}
    direct_landing = ((mid_0, far_0), (mid_1, far_1), (mid_2, far_2))

    def part_flow(p):
        first, second, third_axis = PART_AXES[p]
        fixed = {}

        def chunk(axis, i, cut=None, half=None):
            index = []
            for a in ("x", "y", "z"):
                if a in fixed:
                    index.append(fixed[a])
                elif a == axis:
                    index.append(i % place_of[a][1])
                elif a == cut:
                    size = place_of[a][1] // 2
                    index.append(pl.ds(half * size, size))
                else:
                    index.append(slice(None))
            return sums.at[(p,) + tuple(index)]

        at, n, dev = place_of[first]
        rest = [a for a in ("x", "y", "z") if a != first]
        lead = tuple(place_of[a][1] for a in rest)
        half_size = lead[0] // 2
        hops = n // 2
        for step in range(hops):
            k = hops - step
            split = step == 0
            lines = []
            for w in (0, 1):
                sign = 1 if w == 0 else -1
                ref = nears[first].at[step, w]
                cut = (rest[0], w) if split else (None, None)
                if split:
                    ref = ref.at[pl.ds(w * half_size, half_size)]
                lines.append((sign, ref, cut, (send.at[p, step, w], recv.at[p, step, w])))
            for sign, ref, cut, sems in lines:
                push(chunk(first, at + n + sign * k, *cut), ref, *sems, dev(at + n + sign))
            yield
            for sign, ref, cut, sems in lines:
                landed(ref, *sems)
            if step < hops - 1:
                shape = (half_size,) + lead[1:] if split else lead
                for sign, ref, cut, sems in lines:
                    add_into(chunk(first, at + n + sign * (k - 1), *cut), [ref], shape)
            else:
                add_into(chunk(first, at), [ref for _, ref, _, _ in lines], lead)
        fixed[first] = at

        for stage, axis in enumerate((second, third_axis)):
            at, n, dev = place_of[axis]
            buffers = direct_landing[p][stage]
            for i in range(1, n):
                push(
                    chunk(axis, at + i), buffers.at[at],
                    direct_send.at[p, stage, i], direct_recv.at[p, stage, i], dev(at + i),
                )
            yield
            sources = [buffers.at[(at + n - i) % n] for i in range(1, n)]
            for i, ref in enumerate(sources):
                landed(ref, direct_send.at[p, stage, i + 1], direct_recv.at[p, stage, i + 1])
            add_into(chunk(axis, at), sources, (place_of[third_axis][1],) if stage == 0 else ())
            fixed[axis] = at

        finals[p, yl, z] = sums[p, x, y, z]
        for i in range(1, NZ):
            push(finals.at[p, yl, z], finals.at[p, yl, z], out_send.at[p, i], out_recv.at[p, i], at_z(z + i))
        yield
        for i in range(1, NZ):
            landed(finals.at[p, yl, (z + NZ - i) % NZ], out_send.at[p, i], out_recv.at[p, i])
        push(finals.at[p, yl], finals.at[p, yl], out_send.at[p, 0], out_recv.at[p, 0], to_ys)

        def pairs(layer, core, store):
            return [store.at[p, layer, pl.ds(zh * 4 + 2 * core, 2)] for zh in (0, 1)]

        def to_sibling(j, layer):
            for zh, (src, dst) in enumerate(zip(pairs(layer, 1 - c, finals), pairs(layer, 1 - c, other_finals))):
                push(src, dst, sib_send.at[p, j, zh], sib_recv.at[p, j, zh], sib)

        to_sibling(0, yl)
        yield
        landed(finals.at[p, 1 - yl], out_send.at[p, 0], out_recv.at[p, 0])
        to_sibling(1, 1 - yl)
        yield
        for j, layer in ((0, yl), (1, 1 - yl)):
            for zh, ref in enumerate(pairs(layer, c, other_finals)):
                landed(ref, sib_send.at[p, j, zh], sib_recv.at[p, j, zh])

    def small_flow():
        def spread(source, held_in, at, n, dev, first):
            for i in range(1, n):
                push(
                    source((at + i) % n), held_in.at[at],
                    small_send.at[first + i], small_recv.at[first + i], dev(at + i),
                )

        def collect(held_in, at, n, first):
            for i in range(1, n):
                landed(held_in.at[(at + n - i) % n], small_send.at[first + i], small_recv.at[first + i])

        def total_of(held_in, n):
            total = held_in[0]
            for i in range(1, n):
                total = total + held_in[i]
            return total

        for half in (0, 1):
            for k in range(NZ):
                small_split[half, k] = small[pl.ds((k * 2 + half) * SMALL, SMALL), :]
        push(small_split.at[1 - c], small_sib, small_send.at[8], small_recv.at[8], sib)
        yield
        landed(small_sib, small_send.at[8], small_recv.at[8])
        small_sum[...] = small_split[c] + small_sib[...]
        small_z[z] = small_sum[z]
        spread(lambda i: small_sum.at[i], small_z, z, NZ, at_z, 0)
        yield
        collect(small_z, z, NZ, 0)
        small_x[x] = total_of(small_z, NZ)
        spread(lambda i: small_x.at[x], small_x, x, NX, at_x, 8)
        yield
        collect(small_x, x, NX, 8)
        small_y[y] = total_of(small_x, NX)
        spread(lambda i: small_y.at[y], small_y, y, NY, at_y, 12)
        yield
        collect(small_y, y, NY, 12)
        small_out[c, z] = total_of(small_y, NY)
        spread(lambda i: small_out.at[c, z], small_out.at[c], z, NZ, at_z, 16)
        yield
        collect(small_out.at[c], z, NZ, 16)
        push(small_out.at[c], small_out.at[c], small_send.at[0], small_recv.at[0], sib)
        yield
        landed(small_out.at[1 - c], small_send.at[0], small_recv.at[0])

    def gain_in_flow():
        push(gin, gin_sib, gin_send.at[0, 0], gin_recv.at[0, 0], sib)
        yield
        landed(gin_sib, gin_send.at[0, 0], gin_recv.at[0, 0])
        total = gin[...] + gin_sib[...]
        for stage, (axis, store) in enumerate((("z", gin_z), ("x", gin_x), ("y", gin_y)), 1):
            at, n, dev = place_of[axis]
            store[at] = total
            for i in range(1, n):
                push(store.at[at], store.at[at], gin_send.at[stage, i], gin_recv.at[stage, i], dev(at + i))
            yield
            for i in range(1, n):
                landed(store.at[(at + n - i) % n], gin_send.at[stage, i], gin_recv.at[stage, i])
            total = store[0]
            for i in range(1, n):
                total = total + store[i]
        gin_out[...] = total

    flows = [part_flow(p) for p in range(PARTS)] + [small_flow(), gain_in_flow()]
    over = [False] * len(flows)

    def resume(*which):
        for i in which:
            if not over[i]:
                try:
                    next(flows[i])
                except StopIteration:
                    over[i] = True

    part_slabs = slabs // PARTS

    def backward_some(p):
        lax.fori_loop(p * part_slabs, (p + 1) * part_slabs, backward, 0)

    def start_part(p):
        swap = swap_part(p)
        if p == 0:
            slots_copy.wait()
        swap.wait_recv()
        make_terms(p)
        resume(p)

    def slot_grads(i, carry):
        rows = weight[pl.ds(i * 2, 2)].reshape(2 * cap, width)
        g = contract_last(rows, grad[...])
        slots_t[pl.ds(pl.multiple_of(i * 2 * cap, 32), 2 * cap), :] = g.astype(slots_t.dtype)
        return carry

    def slot_some(lo, hi):
        lax.fori_loop(lo, hi, slot_grads, 0)

    def feature_grads(i, carry):
        owned = owner_ref[...].reshape(1, slots)
        picked = jnp.concatenate([low[...] * slab_mask(owned, 2 * i + h) for h in (0, 1)], axis=0)
        g = jnp.transpose(jnp.dot(picked, slots_t[...], preferred_element_type=f32))
        for h in range(WIDE // LANES):
            deriv[i * (WIDE // LANES) + h] = g[:, h * LANES : (h + 1) * LANES].reshape(STEP, SEG, LANES)
        return carry

    def feature_some(lo, hi):
        lax.fori_loop(lo, hi, feature_grads, 0)

    def first_norm(j, totals):
        hats = [(row(natural, k, j) - means[j]) * inverses[j] for k in range(slabs)]
        gs = [deriv[k, j] for k in range(slabs)]
        totals = tuple(s + g * h for s, g, h in zip(totals, gs, hats))
        gs = [g * gain(gain_in_ref, k) for k, g in enumerate(gs)]
        total, cross = gs[0], gs[0] * hats[0]
        for g, h in zip(gs[1:], hats[1:]):
            total, cross = total + g, cross + g * h
        total, cross = over_lanes(total, features), over_lanes(cross, features)
        for k in range(slabs):
            v = row(cots, k, j) + inverses[j] * (gs[k] - total - hats[k] * cross)
            cots[k, pl.ds(j, SEG, stride=STEP), :] = v
        return totals

    gin[...] = jnp.zeros_like(gin)
    backward_some(0)
    start_part(0)
    backward_some(1)
    start_part(1)
    resume(0)
    backward_some(2)
    start_part(2)
    resume(0, 3)
    slot_some(0, 3)
    resume(1, 3)
    slot_some(3, 6)
    resume(0, 2, 3)
    slot_some(6, 8)
    feature_some(0, 1)
    resume(0, 3)
    feature_some(1, 3)
    resume(1)
    feature_some(3, 5)
    resume(2, 0, 3)
    feature_some(5, 6)
    totals = tuple(jnp.zeros((SEG, LANES), f32) for _ in range(slabs))
    totals = lax.fori_loop(0, STEP // 2, first_norm, totals)
    resume(1, 3)
    totals = lax.fori_loop(STEP // 2, STEP, first_norm, totals)
    for k in range(slabs):
        gin[pl.ds(k, 1), :] = jnp.sum(totals[k], axis=0, keepdims=True)
    resume(4, 2, 0, 4, 1, 2, 4)
    for k in range(slabs):
        out_ref[:, pl.ds(k * LANES, LANES)] = cots[k].astype(out_ref.dtype)
    resume(0, 4, 3)
    while not all(over):
        resume(1, 2, 4, 0, 3)

    for layer in (0, 1):
        for zh in (0, 1):
            for p in range(PARTS):
                column = p * part_cols + (layer * 2 + zh) * LANES
                for source, which in ((finals, c), (other_finals, 1 - c)):
                    block = jnp.concatenate(
                        [wide(source[p, layer, zh * 4 + 2 * c + r]) for r in (0, 1)], axis=0
                    )
                    start = pl.multiple_of(which * features + column, LANES)
                    rows_ref[:, pl.ds(start, LANES)] = block.astype(rows_ref.dtype)
    for k in range(slabs):
        lanes = pl.ds(k * LANES, LANES)
        for m in range(small_rows // SEG):
            group = (k * small_rows) // SEG + m
            which, line = group // (SMALL // SEG), (group % (SMALL // SEG)) * SEG
            value = small_out[which % 2, which // 2, pl.ds(line, SEG), :]
            if m < taps // SEG:
                taps_out[pl.ds(m * SEG, SEG), lanes] = value
            else:
                gains_out[:, lanes] = value
    for copy in pending:
        copy.wait_send()


def run_module(frames, cotangent, lengths, weight_slots, owner_rows, gain_in, gain_mid, taps):
    tokens, features = frames.shape
    cap, width = weight_slots.shape
    slots = owner_rows.shape[0]
    slabs = features // LANES
    count = taps.shape[0]
    bf, f32 = jnp.bfloat16, jnp.float32
    vmem = pl.BlockSpec(memory_space=pltpu.VMEM)
    slab = (slabs, STEP, SEG, LANES)
    plane = (STEP, SEG, LANES)
    block = (BLOCK, LANES)
    small = (SMALL, LANES)
    gin = (pl.cdiv(slabs, SEG) * SEG, LANES)
    dma = pltpu.SemaphoreType.DMA
    return pl.pallas_call(
        module_kernel,
        out_shape=(
            jax.ShapeDtypeStruct((tokens, features), bf),
            jax.ShapeDtypeStruct((cap, width), bf),
            jax.ShapeDtypeStruct((count, features), f32),
            jax.ShapeDtypeStruct((SEG, features), f32),
            jax.ShapeDtypeStruct(gin, f32),
        ),
        in_specs=[pl.BlockSpec(memory_space=pltpu.SMEM)] + [pl.BlockSpec(memory_space=pl.ANY)] * 3 + [vmem] * 4,
        out_specs=(vmem,) * 5,
        scratch_shapes=[
            pltpu.VMEM((2, NZ) + small, f32),
            pltpu.VMEM((tokens, features), bf),
            pltpu.VMEM((tokens, features), bf),
            pltpu.VMEM(gin, f32),
            pltpu.VMEM(gin, f32),
            pltpu.VMEM((NZ,) + gin, f32),
            pltpu.VMEM((NX,) + gin, f32),
            pltpu.VMEM((NY,) + gin, f32),
            dma((2,)),
            dma((4, NZ)),
            dma((4, NZ)),
            pltpu.VMEM((slots // cap, cap, width), bf),
            pltpu.VMEM((slabs, tokens, LANES), f32),
            pltpu.VMEM((slabs, tokens, LANES), f32),
            pltpu.VMEM((tokens, features), bf),
            pltpu.VMEM((tokens, slots), bf),
            pltpu.VMEM((slots, tokens), bf),
            pltpu.VMEM((tokens, width), bf),
            pltpu.VMEM(plane, f32),
            pltpu.VMEM(plane, f32),
            pltpu.VMEM(slab, f32),
            pltpu.VMEM(slab, f32),
            pltpu.VMEM((slabs, STEP + count, SEG, LANES), f32),
            pltpu.VMEM(slab, f32),
            pltpu.VMEM(slab, f32),
            pltpu.VMEM((STEP + count, SEG, LANES), f32),
            pltpu.VMEM((slabs, count, SEG, LANES), f32),
            pltpu.VMEM(plane, f32),
            pltpu.VMEM(plane, f32),
            pltpu.VMEM(plane, f32),
            pltpu.VMEM((2,) + plane, f32),
            pltpu.VMEM((2 * NZ * SMALL, LANES), f32),
            pltpu.VMEM((2, NZ) + small, f32),
            pltpu.VMEM((slots, tokens), bf),
            pltpu.VMEM((PARTS, tokens, features // PARTS), bf),
            pltpu.VMEM((PARTS, NX, NY, NZ) + block, bf),
            pltpu.VMEM((LANES, slots), bf),
            pltpu.VMEM((2, 2, NY, NZ) + block, bf),
            pltpu.VMEM((2, 2, NX, NZ) + block, bf),
            pltpu.VMEM((4, 2, NX, NY) + block, bf),
            pltpu.VMEM((NX, NY) + block, bf),
            pltpu.VMEM((NY, NZ) + block, bf),
            pltpu.VMEM((NX, NZ) + block, bf),
            pltpu.VMEM((NY,) + block, bf),
            pltpu.VMEM((NZ,) + block, bf),
            pltpu.VMEM((NZ,) + block, bf),
            pltpu.VMEM((NZ,) + small, f32),
            pltpu.VMEM((NZ,) + small, f32),
            pltpu.VMEM((NZ,) + small, f32),
            pltpu.VMEM((NX,) + small, f32),
            pltpu.VMEM((NY,) + small, f32),
            pltpu.VMEM((PARTS, 2, NZ) + block, bf),
            pltpu.VMEM((PARTS, 2, NZ) + block, bf),
            dma,
            dma((53, PIECES)),
            dma((53, PIECES)),
            dma((1 + PARTS,)),
            dma((1 + PARTS,)),
            dma((PARTS, 4, 2)),
            dma((PARTS, 4, 2)),
            dma((PARTS, 2, NZ)),
            dma((PARTS, 2, NZ)),
            dma((24,)),
            dma((24,)),
            dma((PARTS, NZ)),
            dma((PARTS, NZ)),
            dma((PARTS, 2, 2)),
            dma((PARTS, 2, 2)),
        ],
        compiler_params=pltpu.CompilerParams(
            collective_id=0, has_side_effects=True, vmem_limit_bytes=63 << 20
        ),
        name="conv_module",
    )(lengths, frames, cotangent, weight_slots, owner_rows, gain_in, gain_mid, taps)


def per_device(frames, cotangent, lengths, weight_slots, owner_rows, gain_in, gain_mid, kernel):
    utterances, length, features = frames.shape
    slabs = features // LANES
    frame_grads, weight_grads, taps_total, gains_total, gain_in_total = run_module(
        frames.reshape(length, features), cotangent.reshape(length, features), lengths, weight_slots,
        owner_rows, gain_in, gain_mid, kernel,
    )
    gain_in_total = gain_in_total[:slabs].reshape(features)
    return (frame_grads[None], weight_grads, gain_in_total, gains_total[1], taps_total)


def solution(mesh):
    in_specs = (
        P(("dp", "fsdp"), None, None),
        P(("dp", "fsdp"), None, None),
        P(("dp", "fsdp")),
        P("fsdp", None),
        P(),
        P(),
        P(),
        P(),
    )
    out_specs = (P(("dp", "fsdp"), None, None), P("fsdp", None), P(), P(), P())
    return jax.shard_map(
        per_device, mesh=mesh, in_specs=in_specs, out_specs=out_specs, check_vma=False
    )
```

```python
import functools
import jax
import jax.numpy as jnp
from jax import lax
from jax.experimental import pallas as pl
from jax.experimental.pallas import tpu as pltpu
from jax.sharding import PartitionSpec as P

MESH = pl.DeviceIdType.MESH
NX, NY, NZ = 4, 4, 8
PIECES = 3
PARTS = 3
BLOCK = 72
LANES = 128
SMALL = 32
EPSILON = 1e-05
STEP = 32
SEG = 8
WIDE = 256
PART_AXES = ("zxy", "xyz", "yxz")


def place():
    d = lax.axis_index("dp")
    f = lax.axis_index("fsdp")
    return f // 4, (f // 2) % 2, d // NZ, d % NZ, f % 2


def device(x, yh, yl, z, c):
    return (yl * NZ + z, (x * 2 + yh) * 2 + c)


def wide(value):
    return value.astype(jnp.float32)


def split_index(i, lead):
    index = []
    for size in reversed(lead):
        index.append(i % size)
        i = i // size
    return tuple(reversed(index))


def add_into(dst, sources, lead):
    total = 1
    for size in lead:
        total *= size

    def one(i, carry):
        index = split_index(i, lead)
        value = wide(dst[index])
        for src in sources:
            value = value + wide(src[index])
        dst[index] = value.astype(dst.dtype)
        return carry

    if total == 1:
        one(0, 0)
    else:
        lax.fori_loop(0, total, one, 0)


def contract_last(a, b):
    return lax.dot_general(a, b, (((1,), (1,)), ((), ())), preferred_element_type=jnp.float32)


def over_lanes(value, count):
    return jnp.sum(value, axis=-1, keepdims=True) * (1.0 / count)


def extend(ext, value, taps):
    before = taps // 2
    seg = lax.broadcasted_iota(jnp.int32, (before, SEG, LANES), 1)
    ext[pl.ds(before, STEP)] = value
    late = pltpu.roll(value[STEP - before :], 1, 1)
    ext[pl.ds(0, before)] = jnp.where(seg == 0, 0.0, late)
    early = pltpu.roll(value[:before], SEG - 1, 1)
    ext[pl.ds(before + STEP, before)] = jnp.where(seg == SEG - 1, 0.0, early)


def module_kernel(
    length_ref, frames_hbm, cot_hbm, w_ref, owner_ref, gain_in_ref, gain_mid_ref, taps_ref,
    out_ref, rows_ref, taps_out, gain_mid_out, gain_in_out,
    small_out, frames_ref, cot_ref, gin, gin_sib, gin_z, gin_x, gin_y, load_sem, gin_send, gin_recv,
    weight, natural, cots, normed, in_slots, slots_t, grad, means, inverses, left, gate, held,
    conv, deriv, ext_d, taps_wide, keep, acc_a, acc_b, back, small, small_split,
    theirs_t, theirs_g, sums, low, near_x, near_y, near_z, mid_0, mid_1, mid_2, far_0, far_1, far_2,
    small_sum, small_sib, small_z, small_x, small_y, finals, other_finals,
    keep_sem, w_send, w_recv, swap_send, swap_recv, send, recv, direct_send, direct_recv, small_send, small_recv,
    out_send, out_recv, sib_send, sib_recv,
):
    load_frames = pltpu.make_async_copy(frames_hbm, frames_ref, load_sem.at[0])
    load_cot = pltpu.make_async_copy(cot_hbm, cot_ref, load_sem.at[1])
    load_frames.start()
    load_cot.start()
    x, yh, yl, z, c = place()
    y = yh * 2 + yl
    f32 = jnp.float32
    features = frames_hbm.shape[1]
    slabs = features // LANES
    taps = taps_ref.shape[0]
    slots = owner_ref.shape[0]
    blocks = features // WIDE
    tokens = STEP * SEG
    cap, width = w_ref.shape
    part_cols = features // PARTS

    def at_x(i):
        return device(i % NX, yh, yl, z, c)

    def at_y(i):
        return device(x, (i % NY) // 2, i % 2, z, c)

    def at_z(i):
        return device(x, yh, yl, i % NZ, c)

    sib = device(x, yh, yl, z, 1 - c)
    to_ac = device(x, 1 - yh, 1 - yl, z, c)
    to_ys = device(x, yh, 1 - yl, z, c)
    pending = []

    def push(src, dst, send_sem, recv_sem, to):
        copy = pltpu.make_async_remote_copy(
            src_ref=src, dst_ref=dst, send_sem=send_sem, recv_sem=recv_sem,
            device_id=to, device_id_type=MESH,
        )
        copy.start()
        pending.append(copy)
        return copy

    def landed(ref, send_sem, recv_sem):
        pltpu.make_async_remote_copy(
            src_ref=ref, dst_ref=ref, send_sem=send_sem, recv_sem=recv_sem,
            device_id=sib, device_id_type=MESH,
        ).wait_recv()

    peers = (
        [sib]
        + [at_x(x + i) for i in range(1, NX)]
        + [at_y(y + i) for i in range(1, NY)]
        + [at_z(z + i) for i in range(1, NZ)]
    )
    barrier = pltpu.get_barrier_semaphore()
    for peer in peers:
        pl.semaphore_signal(barrier, inc=1, device_id=peer, device_id_type=MESH)
    pl.semaphore_wait(barrier, len(peers))

    xs = [x, (x + 3) % NX, (x + 1) % NX, (x + 2) % NX]
    to_xp, to_xm, to_zp, to_zm = at_x(x + 1), at_x(x + 3), at_z(z + 1), at_z(z + NZ - 1)
    span_x = width * 7 // 12
    span_y = span_x // 2
    rest_z = width - span_x
    span_z = rest_z // 2
    piece_rows = cap // PIECES
    par = z % 2
    base = par * rest_z

    def cols(start, size):
        return pl.ds(pl.multiple_of(start, LANES), size)

    window = cols(base, span_x)
    halves = [cols(base, span_y), cols(base + span_y, span_y)]
    mine = cols(base + yl * span_y, span_y)
    other = cols(base + (1 - yl) * span_y, span_y)
    shared = [cols(par * span_x, span_z), cols(par * span_x + span_z, span_z)]
    theirs = [cols((1 - par) * span_x, span_z), cols((1 - par) * span_x + span_z, span_z)]

    def owner(k, other_row):
        return (xs[k] * 2 + (1 - yh if other_row else yh)) * 2 + c

    def piece(ref, q, span):
        return ref.at[pl.ds(q * piece_rows, piece_rows), span]

    def w_push(index, q, src, dst, to):
        push(src, dst, w_send.at[index, q], w_recv.at[index, q], to)

    def pass_on(index, q, who, span, to):
        ref = piece(weight.at[who], q, span)
        w_push(index, q, ref, ref, to)

    def arrive(index, q, who, span):
        landed(piece(weight.at[who], q, span), w_send.at[index, q], w_recv.at[index, q])

    me = owner(0, False)
    x_copies = [
        [
            pltpu.make_async_remote_copy(
                src_ref=piece(w_ref, q, window), dst_ref=piece(weight.at[me], q, window),
                send_sem=w_send.at[index, q], recv_sem=w_recv.at[index, q],
                device_id=to, device_id_type=MESH,
            )
            for index, to in ((1, to_xp), (2, to_xm))
        ]
        for q in range(PIECES)
    ]

    def x_next(q):
        for copy in x_copies[q - 1]:
            copy.wait_send()
        for copy in x_copies[q]:
            copy.start()

    for copy in x_copies[0]:
        copy.start()
    pending.extend(x_copies[-1])
    for q in range(PIECES):
        w_push(3, q, piece(w_ref, q, mine), piece(weight.at[me], q, mine), to_ac)
    w_push(0, 0, w_ref, weight.at[me], sib)
    own_copy = pltpu.make_async_copy(w_ref, weight.at[me], keep_sem)
    own_copy.start()

    def z_out(slot, q, who):
        pass_on(13 + slot, q, who, shared[0], to_zp)
        pass_on(20 + slot, q, who, shared[1], to_zm)

    units = [(1, False), (2, False), (3, False), (0, True), (1, True), (2, True), (3, True)]

    def x_near(k, q):
        arrive(k, q, owner(k, False), window)
        pass_on(6 + k, q, owner(k, False), halves[k - 1], (to_xp, to_xm)[k - 1])
        pass_on(3 + k, q, owner(k, False), mine, to_ac)
        z_out(k - 1, q, owner(k, False))
        pass_on(26 + k, q, owner(k, False), window, sib)

    def x_far(q):
        arrive(7, q, owner(3, False), halves[0])
        arrive(8, q, owner(3, False), halves[1])
        pass_on(6, q, owner(3, False), mine, to_ac)
        z_out(2, q, owner(3, False))
        pass_on(29, q, owner(3, False), halves[0], sib)
        pass_on(30, q, owner(3, False), halves[1], sib)

    def across(k, q):
        arrive(3 + k, q, owner(k, True), other)
        pass_on(9 + k, q, owner(k, True), other, to_ys)
        pass_on(31 + k, q, owner(k, True), other, sib)

    def beside(k, q):
        arrive(9 + k, q, owner(k, True), mine)
        z_out(3 + k, q, owner(k, True))
        pass_on(35 + k, q, owner(k, True), mine, sib)

    def z_in(slot, q):
        who = owner(*units[slot])
        arrive(13 + slot, q, who, theirs[0])
        pass_on(39 + slot, q, who, theirs[0], sib)
        arrive(20 + slot, q, who, theirs[1])
        pass_on(46 + slot, q, who, theirs[1], sib)

    def flip(who):
        return who + 1 - 2 * c

    def from_sibling():
        landed(weight.at[flip(me)], w_send.at[0, 0], w_recv.at[0, 0])
        for q in range(PIECES):
            arrive(27, q, flip(owner(1, False)), window)
            arrive(28, q, flip(owner(2, False)), window)
            arrive(29, q, flip(owner(3, False)), halves[0])
            arrive(30, q, flip(owner(3, False)), halves[1])
            for k in range(4):
                arrive(31 + k, q, flip(owner(k, True)), other)
                arrive(35 + k, q, flip(owner(k, True)), mine)
            for slot in range(7):
                arrive(39 + slot, q, flip(owner(*units[slot])), theirs[0])
                arrive(46 + slot, q, flip(owner(*units[slot])), theirs[1])
        own_copy.wait()

    def row(ref, k, j):
        return ref[k, pl.ds(j, SEG, stride=STEP), :]

    def gain(ref, k):
        return ref[pl.ds(k * LANES, LANES)].reshape(1, LANES)

    def prepare():
        load_frames.wait()
        for k in range(slabs):
            lanes = pl.ds(k * LANES, LANES)
            natural[k] = wide(frames_ref[:, lanes])
            taps_wide[k] = jnp.broadcast_to(taps_ref[:, lanes][:, None, :], (taps, SEG, LANES))
        step_of = lax.broadcasted_iota(jnp.int32, (STEP, SEG, LANES), 0)
        seg_of = lax.broadcasted_iota(jnp.int32, (STEP, SEG, LANES), 1)
        keep[...] = (seg_of * STEP + step_of < length_ref[0]).astype(f32)

    def prepare_cots():
        load_cot.wait()
        for k in range(slabs):
            cots[k] = wide(cot_ref[:, pl.ds(k * LANES, LANES)])
        small[...] = jnp.zeros_like(small)

    def norm_pair(i, carry):
        parts = []
        for j in (2 * i, 2 * i + 1):
            values = [row(natural, k, j) for k in range(slabs)]
            total = values[0]
            for v in values[1:]:
                total = total + v
            mean = over_lanes(total, features)
            values = [v - mean for v in values]
            total = values[0] * values[0]
            for v in values[1:]:
                total = total + v * v
            inverse = lax.rsqrt(over_lanes(total, features) + EPSILON)
            means[j] = jnp.broadcast_to(mean, (SEG, LANES))
            inverses[j] = jnp.broadcast_to(inverse, (SEG, LANES))
            parts.append([v * inverse * gain(gain_in_ref, k) for k, v in enumerate(values)])
        for k in range(slabs):
            pair = jnp.concatenate([parts[0][k], parts[1][k]], axis=0)
            normed[pl.ds(pl.multiple_of(i * 16, 16), 16), pl.ds(k * LANES, LANES)] = pair.astype(normed.dtype)
        return carry

    def norm_some(i):
        lax.fori_loop(4 * i, 4 * i + 4, norm_pair, 0)

    def slab_mask(owned, k):
        return jnp.where((owned >= k * LANES) & (owned < (k + 1) * LANES), 1.0, 0.0).astype(normed.dtype)

    def choose(i):
        span = pl.ds(i * WIDE, WIDE)
        rows = lax.broadcasted_iota(jnp.int32, (LANES, WIDE), 0)
        owned = owner_ref[span].reshape(1, WIDE)
        line = jnp.where(rows == owned % LANES, 1.0, 0.0).astype(normed.dtype)
        low[:, span] = line
        picked = jnp.concatenate([line * slab_mask(owned, k) for k in range(slabs)], axis=0)
        moved = jnp.dot(normed[...], picked, preferred_element_type=f32)
        in_slots[:, span] = moved.astype(in_slots.dtype)
        slots_t[span, :] = jnp.transpose(moved).astype(slots_t.dtype)

    slots_copy = pltpu.make_async_remote_copy(
        src_ref=slots_t, dst_ref=theirs_t, send_sem=swap_send.at[0], recv_sem=swap_recv.at[0],
        device_id=sib, device_id_type=MESH,
    )

    def swap_slots():
        slots_copy.start()

    part = functools.partial
    fill = [part(norm_some, i) for i in range(STEP // 8)]
    fill += [part(choose, i) for i in range(slots // WIDE)] + [swap_slots, prepare_cots]
    steps = []
    for q in range(PIECES):
        if q + 1 < PIECES:
            steps += [part(x_next, q + 1)]
        steps += [part(x_near, 1, q), part(x_near, 2, q)]
        if q == 0:
            steps += [part(across, 0, r) for r in range(PIECES)]
        else:
            steps += [part(x_far, q - 1), part(across, 1, q - 1), part(across, 2, q - 1)]
        if q == 1:
            steps += [part(beside, 0, r) for r in range(PIECES)]
        if q > 1:
            steps += [part(across, 3, q - 2), part(beside, 1, q - 2), part(beside, 2, q - 2)]
    last = PIECES - 1
    steps += [part(x_far, last), part(across, 1, last), part(across, 2, last)]
    for q in range(last - 1, PIECES):
        steps += [part(across, 3, q), part(beside, 1, q), part(beside, 2, q)]
    for q in range(PIECES):
        steps += [part(beside, 3, q)]
    steps += [part(z_in, slot, q) for slot in (0, 1, 3, 2, 4, 5, 6) for q in range(PIECES)]

    prepare()
    for task in fill[:2]:
        task()
    fill = fill[2:]
    for step in steps:
        step()
        if fill:
            fill.pop(0)()
    for task in fill:
        task()
    from_sibling()

    acc_a[...] = jnp.zeros_like(acc_a)

    def tap_rows(ext, k, sign, put):
        def one(b, carry):
            start = b * SEG
            first = start if sign > 0 else start + 1
            lines = [ext[first + i] for i in range(taps + SEG - 1)]
            totals = [None] * SEG
            for t in range(taps):
                w = taps_wide[k, t if sign > 0 else taps - 1 - t]
                for i in range(SEG):
                    term = w * lines[i + t]
                    totals[i] = term if totals[i] is None else totals[i] + term
            for i in range(SEG):
                put(start + i, totals[i])
            return carry

        lax.fori_loop(0, STEP // SEG, one, 0)

    def weight_cols(start):
        return weight[:, :, pl.ds(pl.multiple_of(start, WIDE), WIDE)].reshape(slots, WIDE)

    def forward(i, carry):
        value = jnp.dot(in_slots[...], weight_cols(i * WIDE), preferred_element_type=f32)
        opened = jnp.dot(in_slots[...], weight_cols(features + i * WIDE), preferred_element_type=f32)
        opened = jax.nn.sigmoid(opened)
        for h in range(WIDE // LANES):
            k = i * (WIDE // LANES) + h
            a = value[:, h * LANES : (h + 1) * LANES].reshape(STEP, SEG, LANES)
            s = opened[:, h * LANES : (h + 1) * LANES].reshape(STEP, SEG, LANES)
            left[k] = a
            gate[k] = s
            extend(held.at[k], a * s * keep[...], taps)

            def put(j, v, k=k):
                conv[k, j] = v
                acc_a[j] = acc_a[j] + v

            tap_rows(held.at[k], k, 1, put)
        return carry

    lax.fori_loop(0, blocks, forward, 0)

    acc_b[...] = jnp.zeros_like(acc_b)
    back[0] = jnp.broadcast_to(over_lanes(acc_a[...], features), (STEP, SEG, LANES))

    def centre(k, carry):
        v = conv[k] - back[0]
        conv[k] = v
        acc_b[...] += v * v
        return carry

    lax.fori_loop(0, slabs, centre, 0)
    back[1] = jnp.broadcast_to(lax.rsqrt(over_lanes(acc_b[...], features) + EPSILON), (STEP, SEG, LANES))
    acc_a[...] = jnp.zeros_like(acc_a)
    acc_b[...] = jnp.zeros_like(acc_b)

    def order_cot(j, carry):
        for k in range(slabs):
            deriv[k, j] = row(cots, k, j)
        return carry

    lax.fori_loop(0, STEP, order_cot, 0)
    small_rows = small.shape[0] // slabs // SEG * SEG

    def small_row(k, r):
        return pl.ds(pl.multiple_of(k * small_rows, SEG) + r, 1)

    def middle(k, carry):
        g = gain_mid_ref[pl.ds(pl.multiple_of(k * LANES, LANES), LANES)].reshape(1, LANES)
        hat = conv[k] * back[1]
        mixed = hat * g
        s = jax.nn.sigmoid(mixed)
        d = deriv[k] * keep[...] * (s * (1.0 + mixed * (1.0 - s)))
        dh = d * hat
        small[small_row(k, taps + 1), :] = jnp.sum(jnp.sum(dh, axis=0), axis=0, keepdims=True)
        conv[k] = hat
        d = d * g
        deriv[k] = d
        acc_a[...] += d
        acc_b[...] += dh * g
        return carry

    lax.fori_loop(0, slabs, middle, 0)
    acc_a[...] = jnp.broadcast_to(over_lanes(acc_a[...], features), (STEP, SEG, LANES))
    acc_b[...] = jnp.broadcast_to(over_lanes(acc_b[...], features), (STEP, SEG, LANES))

    def backward(k, carry):
        extend(ext_d, back[1] * (deriv[k] - acc_a[...] - conv[k] * acc_b[...]), taps)

        def put(j, v):
            deriv[k, j] = v * keep[j]

        tap_rows(ext_d, k, -1, put)
        half = taps // 2
        for t0 in (0, half):
            def one(b, totals):
                start = b * SEG
                ds = [ext_d[half + start + i] for i in range(SEG)]
                lines = [held[k, start + t0 + i] for i in range(half + SEG - 1)]
                return tuple(
                    functools.reduce(lambda p, q: p + q, [ds[i] * lines[i + t] for i in range(SEG)], totals[t])
                    for t in range(half)
                )

            totals = lax.fori_loop(0, STEP // SEG, one, tuple(jnp.zeros((SEG, LANES), f32) for _ in range(half)))
            for t in range(half):
                small[small_row(k, t0 + t), :] = jnp.sum(totals[t], axis=0, keepdims=True)
        d = deriv[k] * gate[k]
        lanes = pl.ds(pl.multiple_of(k * LANES, LANES), LANES)
        lanes_b = pl.ds(pl.multiple_of(features + k * LANES, LANES), LANES)
        grad[:, lanes] = d.reshape(tokens, LANES).astype(grad.dtype)
        db = d * left[k] * (1.0 - gate[k])
        grad[:, lanes_b] = db.reshape(tokens, LANES).astype(grad.dtype)
        return carry

    owner_rows = slots // (NX * 2)

    def half_cols(index, p):
        return pl.ds(pl.multiple_of(index * features + p * part_cols, part_cols), part_cols)

    def swap_part(p):
        return push(grad.at[:, half_cols(1 - c, p)], theirs_g.at[p], swap_send.at[1 + p], swap_recv.at[1 + p], sib)

    def make_terms(p):
        def one(ox, carry):
            rows = pl.ds(pl.multiple_of(ox * 2 * owner_rows, 64), 2 * owner_rows)
            term = jnp.dot(slots_t[rows, :], grad[:, half_cols(c, p)], preferred_element_type=f32)
            term = term + jnp.dot(theirs_t[rows, :], theirs_g[p], preferred_element_type=f32)
            for oy in range(2):
                for q in range(4):
                    for t in range(4):
                        first = (oy * 4 + q) * BLOCK
                        sums[p, ox, oy * 2 + t // 2, (t % 2) * 4 + q] = term[
                            first : first + BLOCK, t * LANES : (t + 1) * LANES
                        ].astype(sums.dtype)
            return carry

        lax.fori_loop(0, NX, one, 0)

    place_of = {"x": (x, NX, at_x), "y": (y, NY, at_y), "z": (z, NZ, at_z)}
    nears = {"x": near_x, "y": near_y, "z": near_z}
    direct_landing = ((mid_0, far_0), (mid_1, far_1), (mid_2, far_2))

    def part_flow(p):
        first, second, third_axis = PART_AXES[p]
        fixed = {}

        def chunk(axis, i, cut=None, half=None):
            index = []
            for a in ("x", "y", "z"):
                if a in fixed:
                    index.append(fixed[a])
                elif a == axis:
                    index.append(i % place_of[a][1])
                elif a == cut:
                    size = place_of[a][1] // 2
                    index.append(pl.ds(half * size, size))
                else:
                    index.append(slice(None))
            return sums.at[(p,) + tuple(index)]

        at, n, dev = place_of[first]
        rest = [a for a in ("x", "y", "z") if a != first]
        lead = tuple(place_of[a][1] for a in rest)
        half_size = lead[0] // 2
        hops = n // 2
        for step in range(hops):
            k = hops - step
            split = step == 0
            lines = []
            for w in (0, 1):
                sign = 1 if w == 0 else -1
                ref = nears[first].at[step, w]
                cut = (rest[0], w) if split else (None, None)
                if split:
                    ref = ref.at[pl.ds(w * half_size, half_size)]
                lines.append((sign, ref, cut, (send.at[p, step, w], recv.at[p, step, w])))
            for sign, ref, cut, sems in lines:
                push(chunk(first, at + n + sign * k, *cut), ref, *sems, dev(at + n + sign))
            yield
            for sign, ref, cut, sems in lines:
                landed(ref, *sems)
            if step < hops - 1:
                shape = (half_size,) + lead[1:] if split else lead
                for sign, ref, cut, sems in lines:
                    add_into(chunk(first, at + n + sign * (k - 1), *cut), [ref], shape)
            else:
                add_into(chunk(first, at), [ref for _, ref, _, _ in lines], lead)
        fixed[first] = at

        for stage, axis in enumerate((second, third_axis)):
            at, n, dev = place_of[axis]
            buffers = direct_landing[p][stage]
            for i in range(1, n):
                push(
                    chunk(axis, at + i), buffers.at[at],
                    direct_send.at[p, stage, i], direct_recv.at[p, stage, i], dev(at + i),
                )
            yield
            sources = [buffers.at[(at + n - i) % n] for i in range(1, n)]
            for i, ref in enumerate(sources):
                landed(ref, direct_send.at[p, stage, i + 1], direct_recv.at[p, stage, i + 1])
            add_into(chunk(axis, at), sources, (place_of[third_axis][1],) if stage == 0 else ())
            fixed[axis] = at

        finals[p, yl, z] = sums[p, x, y, z]
        for i in range(1, NZ):
            push(finals.at[p, yl, z], finals.at[p, yl, z], out_send.at[p, i], out_recv.at[p, i], at_z(z + i))
        yield
        for i in range(1, NZ):
            landed(finals.at[p, yl, (z + NZ - i) % NZ], out_send.at[p, i], out_recv.at[p, i])
        push(finals.at[p, yl], finals.at[p, yl], out_send.at[p, 0], out_recv.at[p, 0], to_ys)

        def pairs(layer, core, store):
            return [store.at[p, layer, pl.ds(zh * 4 + 2 * core, 2)] for zh in (0, 1)]

        def to_sibling(j, layer):
            for zh, (src, dst) in enumerate(zip(pairs(layer, 1 - c, finals), pairs(layer, 1 - c, other_finals))):
                push(src, dst, sib_send.at[p, j, zh], sib_recv.at[p, j, zh], sib)

        to_sibling(0, yl)
        yield
        landed(finals.at[p, 1 - yl], out_send.at[p, 0], out_recv.at[p, 0])
        to_sibling(1, 1 - yl)
        yield
        for j, layer in ((0, yl), (1, 1 - yl)):
            for zh, ref in enumerate(pairs(layer, c, other_finals)):
                landed(ref, sib_send.at[p, j, zh], sib_recv.at[p, j, zh])

    def small_flow():
        def spread(source, held_in, at, n, dev, first):
            for i in range(1, n):
                push(
                    source((at + i) % n), held_in.at[at],
                    small_send.at[first + i], small_recv.at[first + i], dev(at + i),
                )

        def collect(held_in, at, n, first):
            for i in range(1, n):
                landed(held_in.at[(at + n - i) % n], small_send.at[first + i], small_recv.at[first + i])

        def total_of(held_in, n):
            total = held_in[0]
            for i in range(1, n):
                total = total + held_in[i]
            return total

        for half in (0, 1):
            for k in range(NZ):
                small_split[half, k] = small[pl.ds((k * 2 + half) * SMALL, SMALL), :]
        push(small_split.at[1 - c], small_sib, small_send.at[8], small_recv.at[8], sib)
        yield
        landed(small_sib, small_send.at[8], small_recv.at[8])
        small_sum[...] = small_split[c] + small_sib[...]
        small_z[z] = small_sum[z]
        spread(lambda i: small_sum.at[i], small_z, z, NZ, at_z, 0)
        yield
        collect(small_z, z, NZ, 0)
        small_x[x] = total_of(small_z, NZ)
        spread(lambda i: small_x.at[x], small_x, x, NX, at_x, 8)
        yield
        collect(small_x, x, NX, 8)
        small_y[y] = total_of(small_x, NX)
        spread(lambda i: small_y.at[y], small_y, y, NY, at_y, 12)
        yield
        collect(small_y, y, NY, 12)
        small_out[c, z] = total_of(small_y, NY)
        spread(lambda i: small_out.at[c, z], small_out.at[c], z, NZ, at_z, 16)
        yield
        collect(small_out.at[c], z, NZ, 16)
        push(small_out.at[c], small_out.at[c], small_send.at[0], small_recv.at[0], sib)
        yield
        landed(small_out.at[1 - c], small_send.at[0], small_recv.at[0])

    def gain_in_flow():
        push(gin, gin_sib, gin_send.at[0, 0], gin_recv.at[0, 0], sib)
        yield
        landed(gin_sib, gin_send.at[0, 0], gin_recv.at[0, 0])
        total = gin[...] + gin_sib[...]
        for stage, (axis, store) in enumerate((("z", gin_z), ("x", gin_x), ("y", gin_y)), 1):
            at, n, dev = place_of[axis]
            store[at] = total
            for i in range(1, n):
                push(store.at[at], store.at[at], gin_send.at[stage, i], gin_recv.at[stage, i], dev(at + i))
            yield
            for i in range(1, n):
                landed(store.at[(at + n - i) % n], gin_send.at[stage, i], gin_recv.at[stage, i])
            total = store[0]
            for i in range(1, n):
                total = total + store[i]
        for k in range(slabs):
            gain_in_out[pl.ds(k * LANES, LANES)] = total[k]

    flows = [part_flow(p) for p in range(PARTS)] + [small_flow(), gain_in_flow()]
    over = [False] * len(flows)

    def resume(*which):
        for i in which:
            if not over[i]:
                try:
                    next(flows[i])
                except StopIteration:
                    over[i] = True

    part_slabs = slabs // PARTS

    def backward_some(p):
        lax.fori_loop(p * part_slabs, (p + 1) * part_slabs, backward, 0)

    def start_part(p):
        swap = swap_part(p)
        if p == 0:
            slots_copy.wait()
        swap.wait_recv()
        make_terms(p)
        resume(p)

    def slot_grads(i, carry):
        rows = weight[pl.ds(i * 2, 2)].reshape(2 * cap, width)
        g = contract_last(rows, grad[...])
        slots_t[pl.ds(pl.multiple_of(i * 2 * cap, 32), 2 * cap), :] = g.astype(slots_t.dtype)
        return carry

    def slot_some(lo, hi):
        lax.fori_loop(lo, hi, slot_grads, 0)

    def feature_grads(i, carry):
        owned = owner_ref[...].reshape(1, slots)
        picked = jnp.concatenate([low[...] * slab_mask(owned, 2 * i + h) for h in (0, 1)], axis=0)
        g = jnp.transpose(jnp.dot(picked, slots_t[...], preferred_element_type=f32))
        for h in range(WIDE // LANES):
            deriv[i * (WIDE // LANES) + h] = g[:, h * LANES : (h + 1) * LANES].reshape(STEP, SEG, LANES)
        return carry

    def feature_some(lo, hi):
        lax.fori_loop(lo, hi, feature_grads, 0)

    def first_norm(j, totals):
        hats = [(row(natural, k, j) - means[j]) * inverses[j] for k in range(slabs)]
        gs = [deriv[k, j] for k in range(slabs)]
        totals = tuple(s + g * h for s, g, h in zip(totals, gs, hats))
        gs = [g * gain(gain_in_ref, k) for k, g in enumerate(gs)]
        total, cross = gs[0], gs[0] * hats[0]
        for g, h in zip(gs[1:], hats[1:]):
            total, cross = total + g, cross + g * h
        total, cross = over_lanes(total, features), over_lanes(cross, features)
        for k in range(slabs):
            v = row(cots, k, j) + inverses[j] * (gs[k] - total - hats[k] * cross)
            cots[k, pl.ds(j, SEG, stride=STEP), :] = v
        return totals

    gin[...] = jnp.zeros_like(gin)
    backward_some(0)
    start_part(0)
    backward_some(1)
    start_part(1)
    resume(0)
    backward_some(2)
    start_part(2)
    resume(0, 3)
    slot_some(0, 3)
    resume(1, 3)
    slot_some(3, 6)
    resume(0, 2, 3)
    slot_some(6, 8)
    feature_some(0, 1)
    resume(0, 3)
    feature_some(1, 3)
    resume(1)
    feature_some(3, 5)
    resume(2, 0, 3)
    feature_some(5, 6)
    totals = tuple(jnp.zeros((SEG, LANES), f32) for _ in range(slabs))
    totals = lax.fori_loop(0, STEP // 2, first_norm, totals)
    resume(1, 3)
    totals = lax.fori_loop(STEP // 2, STEP, first_norm, totals)
    for k in range(slabs):
        gin[pl.ds(k, 1), :] = jnp.sum(totals[k], axis=0, keepdims=True)
    resume(4, 2, 0, 4, 1, 2, 4)
    for k in range(slabs):
        out_ref[:, pl.ds(k * LANES, LANES)] = cots[k].astype(out_ref.dtype)
    resume(0, 4, 3)
    while not all(over):
        resume(1, 2, 4, 0, 3)

    for layer in (0, 1):
        for zh in (0, 1):
            for p in range(PARTS):
                column = p * part_cols + (layer * 2 + zh) * LANES
                for source, which in ((finals, c), (other_finals, 1 - c)):
                    block = jnp.concatenate(
                        [wide(source[p, layer, zh * 4 + 2 * c + r]) for r in (0, 1)], axis=0
                    )
                    start = pl.multiple_of(which * features + column, LANES)
                    rows_ref[:, pl.ds(start, LANES)] = block.astype(rows_ref.dtype)
    for k in range(slabs):
        lanes = pl.ds(k * LANES, LANES)
        for m in range(small_rows // SEG):
            group = (k * small_rows) // SEG + m
            which, line = group // (SMALL // SEG), (group % (SMALL // SEG)) * SEG
            value = small_out[which % 2, which // 2, pl.ds(line, SEG), :]
            if m < taps // SEG:
                taps_out[pl.ds(m * SEG, SEG), lanes] = value
            else:
                gain_mid_out[lanes] = value[1]
    for copy in pending:
        copy.wait_send()


def run_module(frames, cotangent, lengths, weight_slots, owner_rows, gain_in, gain_mid, taps):
    tokens, features = frames.shape
    cap, width = weight_slots.shape
    slots = owner_rows.shape[0]
    slabs = features // LANES
    count = taps.shape[0]
    bf, f32 = jnp.bfloat16, jnp.float32
    vmem = pl.BlockSpec(memory_space=pltpu.VMEM)
    slab = (slabs, STEP, SEG, LANES)
    plane = (STEP, SEG, LANES)
    block = (BLOCK, LANES)
    small = (SMALL, LANES)
    gin = (pl.cdiv(slabs, SEG) * SEG, LANES)
    dma = pltpu.SemaphoreType.DMA
    return pl.pallas_call(
        module_kernel,
        out_shape=(
            jax.ShapeDtypeStruct((tokens, features), bf),
            jax.ShapeDtypeStruct((cap, width), bf),
            jax.ShapeDtypeStruct((count, features), f32),
            jax.ShapeDtypeStruct((features,), f32),
            jax.ShapeDtypeStruct((features,), f32),
        ),
        in_specs=[pl.BlockSpec(memory_space=pltpu.SMEM)] + [pl.BlockSpec(memory_space=pl.ANY)] * 3 + [vmem] * 4,
        out_specs=(vmem,) * 5,
        scratch_shapes=[
            pltpu.VMEM((2, NZ) + small, f32),
            pltpu.VMEM((tokens, features), bf),
            pltpu.VMEM((tokens, features), bf),
            pltpu.VMEM(gin, f32),
            pltpu.VMEM(gin, f32),
            pltpu.VMEM((NZ,) + gin, f32),
            pltpu.VMEM((NX,) + gin, f32),
            pltpu.VMEM((NY,) + gin, f32),
            dma((2,)),
            dma((4, NZ)),
            dma((4, NZ)),
            pltpu.VMEM((slots // cap, cap, width), bf),
            pltpu.VMEM((slabs, tokens, LANES), f32),
            pltpu.VMEM((slabs, tokens, LANES), f32),
            pltpu.VMEM((tokens, features), bf),
            pltpu.VMEM((tokens, slots), bf),
            pltpu.VMEM((slots, tokens), bf),
            pltpu.VMEM((tokens, width), bf),
            pltpu.VMEM(plane, f32),
            pltpu.VMEM(plane, f32),
            pltpu.VMEM(slab, f32),
            pltpu.VMEM(slab, f32),
            pltpu.VMEM((slabs, STEP + count, SEG, LANES), f32),
            pltpu.VMEM(slab, f32),
            pltpu.VMEM(slab, f32),
            pltpu.VMEM((STEP + count, SEG, LANES), f32),
            pltpu.VMEM((slabs, count, SEG, LANES), f32),
            pltpu.VMEM(plane, f32),
            pltpu.VMEM(plane, f32),
            pltpu.VMEM(plane, f32),
            pltpu.VMEM((2,) + plane, f32),
            pltpu.VMEM((2 * NZ * SMALL, LANES), f32),
            pltpu.VMEM((2, NZ) + small, f32),
            pltpu.VMEM((slots, tokens), bf),
            pltpu.VMEM((PARTS, tokens, features // PARTS), bf),
            pltpu.VMEM((PARTS, NX, NY, NZ) + block, bf),
            pltpu.VMEM((LANES, slots), bf),
            pltpu.VMEM((2, 2, NY, NZ) + block, bf),
            pltpu.VMEM((2, 2, NX, NZ) + block, bf),
            pltpu.VMEM((4, 2, NX, NY) + block, bf),
            pltpu.VMEM((NX, NY) + block, bf),
            pltpu.VMEM((NY, NZ) + block, bf),
            pltpu.VMEM((NX, NZ) + block, bf),
            pltpu.VMEM((NY,) + block, bf),
            pltpu.VMEM((NZ,) + block, bf),
            pltpu.VMEM((NZ,) + block, bf),
            pltpu.VMEM((NZ,) + small, f32),
            pltpu.VMEM((NZ,) + small, f32),
            pltpu.VMEM((NZ,) + small, f32),
            pltpu.VMEM((NX,) + small, f32),
            pltpu.VMEM((NY,) + small, f32),
            pltpu.VMEM((PARTS, 2, NZ) + block, bf),
            pltpu.VMEM((PARTS, 2, NZ) + block, bf),
            dma,
            dma((53, PIECES)),
            dma((53, PIECES)),
            dma((1 + PARTS,)),
            dma((1 + PARTS,)),
            dma((PARTS, 4, 2)),
            dma((PARTS, 4, 2)),
            dma((PARTS, 2, NZ)),
            dma((PARTS, 2, NZ)),
            dma((24,)),
            dma((24,)),
            dma((PARTS, NZ)),
            dma((PARTS, NZ)),
            dma((PARTS, 2, 2)),
            dma((PARTS, 2, 2)),
        ],
        compiler_params=pltpu.CompilerParams(
            collective_id=0, has_side_effects=True, vmem_limit_bytes=63 << 20
        ),
        name="conv_module",
    )(lengths, frames, cotangent, weight_slots, owner_rows, gain_in, gain_mid, taps)


def per_device(frames, cotangent, lengths, weight_slots, owner_rows, gain_in, gain_mid, kernel):
    utterances, length, features = frames.shape
    frame_grads, weight_grads, taps_total, gain_mid_total, gain_in_total = run_module(
        frames.reshape(length, features), cotangent.reshape(length, features), lengths, weight_slots,
        owner_rows, gain_in, gain_mid, kernel,
    )
    return (frame_grads[None], weight_grads, gain_in_total, gain_mid_total, taps_total)


def solution(mesh):
    in_specs = (
        P(("dp", "fsdp"), None, None),
        P(("dp", "fsdp"), None, None),
        P(("dp", "fsdp")),
        P("fsdp", None),
        P(),
        P(),
        P(),
        P(),
    )
    out_specs = (P(("dp", "fsdp"), None, None), P("fsdp", None), P(), P(), P())
    return jax.shard_map(
        per_device, mesh=mesh, in_specs=in_specs, out_specs=out_specs, check_vma=False
    )
```
